128 devices in a mesh: fsdp: 16 (over y, x), sp: 8 (over z, core).
Axes of the slice: x: 4, y: 4, z: 4, core: 2. Of those that a mesh axis runs over, the one named last changes fastest.
Arguments:
- tokens: bfloat16 [16384, 1024], P(('fsdp', 'sp')), may hold values from -6 to 6
- segments: int32 [16, 1024], P('fsdp'), may hold values from 0 to 3, never falling along the last dimension, each value on 1 to 512 neighbouring positions
- top_idx: int32 [16384, 8], P(('fsdp', 'sp')), may hold values from 0 to 15, all different within a row; in each aligned block of 128 rows (0 to 127, 128 to 255, ...) at most 128 rows name the same one
- cotangent: bfloat16 [16384, 1024], P(('fsdp', 'sp')), may hold values from -6 to 6
- norm1_gain: bfloat16 [1024], P(('fsdp', 'sp')), may hold values from 0.099609375 to 1.8984375
- qkv_weight: bfloat16 [1024, 2048], P(('fsdp', 'sp')), may hold values from -0.1875 to 0.1875
- out_weight: bfloat16 [1024, 1024], P(('fsdp', 'sp')), may hold values from -4 to 4
- norm2_gain: bfloat16 [1024], P(('fsdp', 'sp')), may hold values from 0.099609375 to 1.8984375
- router_weight: bfloat16 [1024, 16], P(('fsdp', 'sp')), may hold values from -0.375 to 0.375
- expert_in: bfloat16 [16, 1024, 1024], P('sp', 'fsdp'), may hold values from -0.1875 to 0.1875
- expert_out: bfloat16 [16, 1024, 512], P('sp', 'fsdp'), may hold values from -2 to 2
Outputs:
- block_out: float32 [16384, 1024], P(('fsdp', 'sp'))
- input_grad: float32 [16384, 1024], P(('fsdp', 'sp'))
- norm1_gain_grad: float32 [1024], P(('fsdp', 'sp'))
- qkv_weight_grad: float32 [1024, 2048], P(('fsdp', 'sp'))
- out_weight_grad: float32 [1024, 1024], P(('fsdp', 'sp'))
- norm2_gain_grad: float32 [1024], P(('fsdp', 'sp'))
- router_weight_grad: float32 [1024, 16], P(('fsdp', 'sp'))
- expert_in_grad: float32 [16, 1024, 1024], P('sp', 'fsdp')
- expert_out_grad: float32 [16, 1024, 512], P('sp', 'fsdp')
The draws below stay inside these ranges and needn't reach their ends.
Inputs may be any that keep to these rules, and one draw needn't show every extreme that they name: `top_idx`: the rows of one device name each expert at most 128 times; the 8 numbers of a row differ. `segments`: each sequence is cut into 4 documents of consecutive positions numbered upward from 0; the longest has 512 positions.
All inputs are finite; a program needn't handle non-finite values.
Results may differ from the reference program's by a relative error of at most 0.02.
Values may be sent and summed in bfloat16 or wider, within the bound.
A program may use at most 128 MiB of HBM per device.

```python
import math
import jax
import jax.numpy as jnp
import numpy as np
from jax import lax

D = 1024
HQ = 16
KEY_VALUE_HEADS = 8
HEAD_SIZE = 64
FF = 512
E = 16
TOP = 8
SEQUENCE_TOKENS = 1024
ROWS = 128
CAP = 128
TOKENS = 16384
N_FSDP = 16
N_SP = 8


def level_of(stream_key, shape, shards, low, largest):
    loudness, own = 1.0, jax.random.fold_in(stream_key, 6)
    for axis_at, shards_of in shards:
        draws = jnp.exp(jax.random.uniform(jax.random.fold_in(own, axis_at), (shards_of,), jnp.float32, low / len(shards), largest / len(shards)))
        loudness = loudness * jnp.repeat(draws, shape[axis_at] // shards_of).reshape([-1 if axis == axis_at else 1 for axis in range(len(shape))])
    return loudness


def split_up(count, total, bound, slope):
    weights = [(1 << 20) // math.isqrt(standing ** slope) + 1 for standing in range(2, count + 1)]
    rest, holding = total - bound - (count - 1), [1] * (count - 1)
    while rest > 0:
        candidates = [i for i in range(count - 1) if holding[i] < bound]
        whole, left = sum([weights[i] for i in candidates]), rest
        for i in candidates:
            addition = min(bound - holding[i], max(1, left * weights[i] // whole), rest)
            holding[i] = holding[i] + addition
            rest = rest - addition
    return np.array([bound] + holding)


def ragged_sizes(own_key, count, total, most, skew):
    if count == 2:
        one = jax.random.randint(own_key, (), max(1, total - most), min(most, total - 1) + 1)
        return jnp.stack([one, total - one])
    sizes = jnp.asarray(split_up(count, total, most, skew), jnp.int32)
    twos = (count - 1) // 2
    source_of, receiver = sizes[1:1 + 2 * twos:2], sizes[2:2 + 2 * twos:2]
    margin = jnp.minimum(source_of - 1, most - receiver)
    moved = jax.random.randint(jax.random.fold_in(own_key, 1), (twos,), 0, 1 << 20) % (margin + 1)
    sizes = sizes.at[1:1 + 2 * twos:2].set(source_of - moved).at[2:2 + 2 * twos:2].set(receiver + moved)
    return sizes[jax.random.permutation(jax.random.fold_in(own_key, 2), count)]


def deal_out(rng, own, number, rows, count, top, bound, skew):
    ranking = jax.random.permutation(rng, count)
    heavy_load, common = shares(count, rows * top, bound, skew, True), shares(count, rows * top, bound, skew, False)
    places = jnp.arange(count)

    def named(tallies, turn):
        used = int((tallies > 0).sum())
        fixed = max(1, used // 4)
        passed = fixed + (places - fixed + turn * (used - fixed)) % max(1, count - fixed)
        return jnp.zeros((count,), jnp.int32).at[ranking[jnp.where(places < fixed, places, passed)]].set(jnp.asarray(tallies, jnp.int32))

    tallies = jnp.where(number % 4 == 0, named(heavy_load, number // 4), named(common, number - number // 4 - 1))
    mixed = jax.random.permutation(jax.random.fold_in(own, 3), count)
    giver, sink = mixed[0:count // 2 * 2:2], mixed[1:count // 2 * 2:2]
    room = jnp.minimum(tallies[giver] - 1, bound - tallies[sink]) // 2
    room = jnp.where((giver == ranking[0]) | (sink == ranking[0]) | (tallies[sink] == 0), 0, jnp.maximum(room, 0))
    passed = jax.random.randint(jax.random.fold_in(own, 4), (count // 2,), 0, 1 << 20) % (room + 1)
    tallies = tallies.at[giver].add(-passed).at[sink].add(passed)
    labels = jnp.searchsorted(jnp.cumsum(tallies), jnp.arange(rows * top), side="right").astype(jnp.int32)
    listing = labels.reshape(top, rows).T
    listing = listing[jax.random.permutation(jax.random.fold_in(own, 1), rows)]
    turn = jax.random.randint(jax.random.fold_in(own, 2), (rows, 1), 0, top)
    return jnp.take_along_axis(listing, (jnp.arange(top)[None, :] + turn) % top, axis=1)


def shares(number_of, total, limit, lean, full):
    portions = [(1 << 20) // math.isqrt(standing ** lean) + 1 for standing in range(1, number_of + 1)]
    largest = limit if full else min(limit, max(-(-total // number_of), total * portions[0] // sum(portions)))
    least = 1 if total - largest >= number_of - 1 else 0
    counts, rest = [largest] + [least] * (number_of - 1), total - largest - least * (number_of - 1)
    while rest > 0:
        candidates = [i for i in range(1, number_of) if counts[i] < largest] or [i for i in range(1, number_of) if counts[i] < limit]
        pool, remaining = sum([portions[i] for i in candidates]), rest
        for i in candidates:
            addition = min(limit - counts[i], max(1, remaining * portions[i] // pool), rest)
            counts[i] = counts[i] + addition
            rest = rest - addition
    return np.array(counts)


def normal_values(rng, extent, deviation, most, pieces=(), held_as=jnp.bfloat16):
    entries = deviation * jax.random.normal(rng, extent, jnp.float32)
    if pieces:
        entries = entries * level_of(rng, extent, pieces, -0.22, 0.18)
    return jnp.clip(entries, -most, most).astype(held_as)


def setup_inputs(seed: int = 0) -> dict:
    splits = jax.random.split(jax.random.key(seed), 12)
    tokens = normal_values(splits[0], (TOKENS, D), 1.0, 6.0, ((0, 128),))
    segments = jax.vmap(lambda own: jnp.searchsorted(jnp.cumsum(ragged_sizes(own, 4, SEQUENCE_TOKENS, SEQUENCE_TOKENS // 2, 1)), jnp.arange(SEQUENCE_TOKENS), side="right"))(jax.random.split(splits[1], N_FSDP)).reshape((N_FSDP, SEQUENCE_TOKENS)).astype(jnp.int32)
    top_idx_keys = jax.random.split(jax.random.fold_in(splits[2], 1), TOKENS // ROWS)
    top_idx_turns = jax.random.permutation(jax.random.fold_in(splits[2], 3), TOKENS // ROWS)
    top_idx = jax.vmap(lambda own, number: deal_out(jax.random.fold_in(splits[2], 2), own, number, ROWS, E, TOP, CAP, 1))(top_idx_keys, top_idx_turns).reshape((TOKENS, TOP))
    cotangent = normal_values(splits[3], (TOKENS, D), 1.0, 6.0, ((0, 128),))
    norm1_gain = jnp.clip(1.0 + 0.18 * jax.random.normal(splits[4], (D,), jnp.float32), 0.099609375, 1.8984375).astype(jnp.bfloat16)
    qkv_weight = normal_values(splits[5], (D, 2 * HQ * HEAD_SIZE), D ** -0.5, 0.1875, ((0, 128),))
    out_weight = normal_values(splits[6], (HQ * HEAD_SIZE, D), 2 ** -0.5, 4.0, ((0, 128),))
    norm2_gain = jnp.clip(1.0 + 0.18 * jax.random.normal(splits[7], (D,), jnp.float32), 0.099609375, 1.8984375).astype(jnp.bfloat16)
    router_weight = normal_values(splits[8], (D, E), (D // 4) ** -0.5, 0.375, ((0, 128),))
    expert_in = normal_values(splits[9], (E, D, 2 * FF), D ** -0.5, 0.1875, ((0, 8), (1, 16)))
    expert_out = normal_values(splits[10], (E, D, FF), (max(1, FF // 64)) ** -0.5, 2.0, ((0, 8), (1, 16)))
    return {"tokens": tokens, "segments": segments, "top_idx": top_idx, "cotangent": cotangent, "norm1_gain": norm1_gain, "qkv_weight": qkv_weight, "out_weight": out_weight, "norm2_gain": norm2_gain, "router_weight": router_weight, "expert_in": expert_in, "expert_out": expert_out}


HIGHEST = lax.Precision.HIGHEST

@jax.custom_vjp
def lower_bound(v):
    return lax.optimization_barrier(v.astype(jnp.bfloat16)).astype(jnp.float32)

@jax.custom_vjp
def lower_bound_backward(v):
    return v

def low_keep(v):
    return (lower_bound(v), None)

def low_pass(kept, grad):
    return (grad,)

def back_keep(v):
    return (v, None)

def back_low(kept, grad):
    return (lower_bound(grad),)
lower_bound.defvjp(low_keep, low_pass)
lower_bound_backward.defvjp(back_keep, back_low)

def rope_tables(positions):
    frequency = 10000.0 ** (-2.0 * jnp.arange(HEAD_SIZE // 2, dtype=jnp.float32) / HEAD_SIZE)
    angles = positions[:, None] * frequency[None, :]
    return (jnp.cos(angles), jnp.sin(angles))

def rotary_apply(value_rows, cosine_table, sine_table):
    half_width = value_rows.shape[-1] // 2
    first_half = value_rows[..., :half_width]
    second_half = value_rows[..., half_width:]
    cos_rows = cosine_table[:, None, :]
    sin_rows = sine_table[:, None, :]
    return jnp.concatenate([first_half * cos_rows - second_half * sin_rows, second_half * cos_rows + first_half * sin_rows], -1)

def rms_norm(value_rows, gain):
    return value_rows * lax.rsqrt(lax.optimization_barrier(jnp.mean(value_rows * value_rows, -1, keepdims=True)) + 1e-06) * gain

def slot_table(chosen_experts):
    expert_of = chosen_experts.reshape(-1)
    one_hot = (expert_of[:, None] == jnp.arange(E, dtype=jnp.int32)[None, :]).astype(jnp.int32)
    earlier = jnp.cumsum(one_hot, 0) - one_hot
    slot_rank = lax.optimization_barrier(jnp.sum(earlier * one_hot, 1))
    return (expert_of, slot_rank)

def routing(chosen_experts):
    per_device = chosen_experts.reshape(N_SP, ROWS, TOP)
    expert_of, slot_rank = jax.vmap(slot_table)(per_device)
    device_rows = jnp.arange(N_SP, dtype=jnp.int32)[:, None]
    slot_index = (expert_of * (N_SP * CAP) + device_rows * CAP + slot_rank).reshape(-1)
    inverse = jnp.full((E * N_SP * CAP,), -1, jnp.int32).at[slot_index].set(jnp.arange(SEQUENCE_TOKENS * TOP, dtype=jnp.int32))
    return (slot_index, inverse >= 0, jnp.maximum(inverse, 0) // TOP)

def layer(hidden_in, gain_one, qkv_w, out_w, gain_two, router_w, experts_in, experts_out, segment_ids, chosen_experts, slot_index, is_filled, source_row):
    query_span_width = HQ * HEAD_SIZE
    key_span_width = KEY_VALUE_HEADS * HEAD_SIZE
    normed = lower_bound(rms_norm(hidden_in, gain_one))
    projected_rows = lower_bound_backward(jnp.dot(normed, qkv_w, precision=HIGHEST))
    query_matrix = projected_rows[:, :query_span_width].reshape(SEQUENCE_TOKENS, HQ, HEAD_SIZE)
    key_rows = projected_rows[:, query_span_width:query_span_width + key_span_width].reshape(SEQUENCE_TOKENS, KEY_VALUE_HEADS, HEAD_SIZE)
    value_rows = projected_rows[:, query_span_width + key_span_width:].reshape(SEQUENCE_TOKENS, KEY_VALUE_HEADS, HEAD_SIZE)
    cosine_table, sine_table = rope_tables(jnp.arange(SEQUENCE_TOKENS, dtype=jnp.float32))
    query_matrix = lower_bound(lower_bound_backward(rotary_apply(query_matrix, cosine_table, sine_table))).reshape(SEQUENCE_TOKENS, KEY_VALUE_HEADS, 2, HEAD_SIZE)
    key_rows = lower_bound(lower_bound_backward(rotary_apply(key_rows, cosine_table, sine_table)))
    value_rows = lower_bound(lower_bound_backward(value_rows))
    scores = lower_bound_backward(jnp.einsum('igjd,kgd->gjik', query_matrix, key_rows, precision=HIGHEST))
    position = jnp.arange(SEQUENCE_TOKENS, dtype=jnp.int32)
    allowed = (position[None, :] <= position[:, None]) & (segment_ids[:, None] == segment_ids[None, :])
    weights = jax.nn.softmax(jnp.where(allowed, scores * HEAD_SIZE ** (-0.5), -jnp.inf), axis=-1)
    weights = lower_bound(weights)
    context = jnp.einsum('gjik,kgd->igjd', weights, value_rows, precision=HIGHEST).reshape(SEQUENCE_TOKENS, query_span_width)
    context = lower_bound(lower_bound_backward(context))
    attended = lower_bound_backward(jnp.dot(context, out_w, precision=HIGHEST))
    middle = hidden_in + 0.22 * attended
    normed_two = lower_bound(rms_norm(middle, gain_two))
    logits = jnp.dot(normed_two, router_w, precision=HIGHEST)
    gate_prob = jax.nn.softmax(jnp.take_along_axis(logits, chosen_experts, 1), axis=-1)
    routed = jnp.where(is_filled[:, None], normed_two[source_row], 0.0).reshape(E, N_SP * CAP, D)
    routed = lower_bound_backward(routed)
    pre_act = lower_bound_backward(jnp.einsum('erd,edf->erf', routed, experts_in, precision=HIGHEST))
    activated = lower_bound(jax.nn.silu(pre_act[..., :FF]) * pre_act[..., FF:])
    expert_result = lower_bound(lower_bound_backward(jnp.einsum('erf,edf->erd', activated, experts_out, precision=HIGHEST)))
    picked = expert_result.reshape(E * N_SP * CAP, D)[slot_index].reshape(SEQUENCE_TOKENS, TOP, D)
    mixed = lax.optimization_barrier(jnp.sum(gate_prob[..., None] * picked, 1))
    return middle + 0.22 * mixed

def reference(tokens, segments, top_idx, cotangent, norm1_gain, qkv_weight, out_weight, norm2_gain, router_weight, expert_in, expert_out):
    params = tuple((weight_arr.astype(jnp.float32) for weight_arr in (norm1_gain, qkv_weight, out_weight, norm2_gain, router_weight, expert_in, expert_out)))
    hidden_all = tokens.astype(jnp.float32).reshape(N_FSDP, SEQUENCE_TOKENS, D)
    cot_all = cotangent.astype(jnp.float32).reshape(N_FSDP, SEQUENCE_TOKENS, D)
    chosen_all = top_idx.reshape(N_FSDP, SEQUENCE_TOKENS, TOP)

    def one_sequence(running, item_set):
        hidden_in, cot_in, segment_ids, chosen_experts = item_set
        slot_index, is_filled, source_row = routing(chosen_experts)

        def forward(hidden_rows, *weight_set):
            return layer(hidden_rows, *weight_set, segment_ids, chosen_experts, slot_index, is_filled, source_row)
        result, pullback = jax.vjp(forward, hidden_in, *params)
        gradients = pullback(cot_in)
        running = tuple((summed + gradient for summed, gradient in zip(running, gradients[1:])))
        return (running, (result, gradients[0]))
    initial = tuple((jnp.zeros_like(weight_arr) for weight_arr in params))
    totals, (results, input_grads) = lax.scan(one_sequence, initial, (hidden_all, cot_all, segments, chosen_all))
    return (results.reshape(TOKENS, D), input_grads.reshape(TOKENS, D), totals[0], totals[1], totals[2], totals[3], totals[4], totals[5], totals[6])
```

```python
import jax
import jax.numpy as jnp
import numpy as np
from jax import lax
from jax.sharding import PartitionSpec as P

HQ = 16
KEY_VALUE_HEADS = 8
HEAD_SIZE = 64
E = 16
EPSILON = 1e-06
RESIDUAL = 0.22
BLOCK = 256
LONGEST = 512
BF16 = jnp.bfloat16
F32 = jnp.float32


def rope_tables(count):
    frequency = np.float32(10000.0) ** (
        np.float32(-2.0) * np.arange(HEAD_SIZE // 2, dtype=np.float32) / np.float32(HEAD_SIZE)
    )
    angles = np.arange(count, dtype=np.float32)[:, None] * frequency.astype(np.float32)[None, :]
    cosine = np.cos(angles).astype(np.float32)
    sine = np.sin(angles).astype(np.float32)
    return np.concatenate([cosine, cosine], 1), np.concatenate([-sine, sine], 1)


def swap_halves(value):
    half = HEAD_SIZE // 2
    return jnp.concatenate([value[..., half:], value[..., :half]], -1)


def dot(left, right, contract):
    return lax.dot_general(left, right, (contract, ((), ())), preferred_element_type=F32)


def inverse_rms(value):
    return lax.rsqrt(jnp.mean(value * value, -1, keepdims=True) + EPSILON)


def rms_backward(grad, value, inverse, gain):
    scaled = grad * gain
    return inverse * scaled - value * (inverse**3) * jnp.mean(scaled * value, -1, keepdims=True)


def block_keys(block, seq_len):
    return max(0, block * BLOCK - LONGEST), (block + 1) * BLOCK


def allowed_pairs(segment_ids, row_lo, row_hi, key_lo, key_hi):
    rows = row_lo + jnp.arange(row_hi - row_lo, dtype=jnp.int32)
    keys = key_lo + jnp.arange(key_hi - key_lo, dtype=jnp.int32)
    return (keys[None, :] <= rows[:, None]) & (
        segment_ids[row_lo:row_hi, None] == segment_ids[None, key_lo:key_hi]
    )


def attention_forward(query, key, value, segment_ids):
    seq_len = key.shape[0]
    scale = HEAD_SIZE**-0.5
    contexts, sums = [], []
    for block in range(seq_len // BLOCK):
        lo, hi = block * BLOCK, (block + 1) * BLOCK
        k_lo, k_hi = block_keys(block, seq_len)
        allowed = allowed_pairs(segment_ids, lo, hi, k_lo, k_hi)
        scores = (
            jnp.einsum("jid,kd->jik", query[:, lo:hi], key[k_lo:k_hi], preferred_element_type=F32)
            * scale
        )
        scores = jnp.where(allowed, scores, -jnp.inf)
        top = jnp.max(scores, -1, keepdims=True)
        expo = jnp.exp(scores - top)
        total = jnp.sum(expo, -1, keepdims=True)
        probs = (expo / total).astype(BF16)
        contexts.append(
            jnp.einsum("jik,kd->ijd", probs, value[k_lo:k_hi], preferred_element_type=F32)
            .astype(BF16)
            .reshape(BLOCK, 2 * HEAD_SIZE)
        )
        sums.append(top + jnp.log(total))
    return jnp.concatenate(contexts, 0), sums


def attention_backward(query, key, value, segment_ids, sums, grad_context):
    seq_len = key.shape[0]
    scale = HEAD_SIZE**-0.5
    grad_heads = grad_context.reshape(seq_len, 2, HEAD_SIZE).transpose(1, 0, 2)
    grad_query = []
    grad_key = [0.0] * (seq_len // BLOCK)
    grad_value = [0.0] * (seq_len // BLOCK)
    for block in range(seq_len // BLOCK):
        lo, hi = block * BLOCK, (block + 1) * BLOCK
        k_lo, k_hi = block_keys(block, seq_len)
        allowed = allowed_pairs(segment_ids, lo, hi, k_lo, k_hi)
        keys, values = key[k_lo:k_hi], value[k_lo:k_hi]
        scores = (
            jnp.einsum("jid,kd->jik", query[:, lo:hi], keys, preferred_element_type=F32) * scale
        )
        probs = jnp.exp(jnp.where(allowed, scores, -jnp.inf) - sums[block])
        grad_rows = grad_heads[:, lo:hi]
        grad_probs = jnp.einsum("jid,kd->jik", grad_rows, values, preferred_element_type=F32)
        row_dot = jnp.sum(grad_probs * probs, -1, keepdims=True)
        grad_scores = (probs * (grad_probs - row_dot) * scale).astype(BF16)
        grad_query.append(
            jnp.einsum("jik,kd->jid", grad_scores, keys, preferred_element_type=F32)
        )
        new_key = jnp.einsum(
            "jik,jid->kd", grad_scores, query[:, lo:hi], preferred_element_type=F32
        )
        new_value = jnp.einsum(
            "jik,jid->kd", probs.astype(BF16), grad_rows, preferred_element_type=F32
        )
        for piece in range(k_lo // BLOCK, k_hi // BLOCK):
            at = piece * BLOCK - k_lo
            grad_key[piece] = grad_key[piece] + new_key[at : at + BLOCK]
            grad_value[piece] = grad_value[piece] + new_value[at : at + BLOCK]
    return (
        jnp.concatenate(grad_query, 1).astype(BF16),
        jnp.concatenate(grad_key, 0).astype(BF16),
        jnp.concatenate(grad_value, 0).astype(BF16),
    )


def shards(
    tokens,
    segments,
    top_idx,
    cotangent,
    norm1_gain,
    qkv_weight,
    out_weight,
    norm2_gain,
    router_weight,
    expert_in,
    expert_out,
):
    n_sp = lax.axis_size("sp")
    n_fsdp = lax.axis_size("fsdp")
    sp_index = lax.axis_index("sp")
    rows, width = tokens.shape
    seq_len = rows * n_sp
    weight_rows = qkv_weight.shape[0]
    hidden = expert_out.shape[2]
    q_span, k_span = HQ * HEAD_SIZE, KEY_VALUE_HEADS * HEAD_SIZE
    group = q_span // n_sp
    head = k_span // n_sp
    segment_ids = segments[0]

    def own(array):
        return lax.dynamic_slice_in_dim(array, sp_index * rows, rows, 0)

    def sum_over(array, axis, count):
        parts = lax.all_to_all(array, axis, split_axis=0, concat_axis=0, tiled=True)
        return jnp.sum(parts.astype(F32), 0)

    small = jnp.concatenate([norm1_gain[:, None], norm2_gain[:, None], router_weight], 1)
    small = jnp.pad(small, ((0, 0), (0, 128 - small.shape[1])))
    packed = jnp.concatenate(
        [
            qkv_weight[:, :q_span].reshape(weight_rows, n_sp, group),
            qkv_weight[:, q_span : q_span + k_span].reshape(weight_rows, n_sp, head),
            qkv_weight[:, q_span + k_span :].reshape(weight_rows, n_sp, head),
            jnp.broadcast_to(small[:, None], (weight_rows, n_sp, 128)),
        ],
        2,
    ).transpose(1, 0, 2)
    packed = lax.all_to_all(packed, "sp", split_axis=0, concat_axis=0, tiled=True)
    packed = lax.all_gather(
        packed.reshape(n_sp * weight_rows, packed.shape[2]), "fsdp", axis=0, tiled=True
    )
    tokens_all = lax.all_gather(tokens, "sp", axis=0, tiled=True)
    chosen = jnp.sum(
        (top_idx[:, :, None] == jnp.arange(128, dtype=jnp.int32)).astype(F32), 1
    ).astype(BF16)
    late = lax.all_gather(jnp.concatenate([cotangent, chosen], 1), "sp", axis=0, tiled=True)
    out_full = lax.all_gather(out_weight, ("fsdp", "sp"), axis=0, tiled=True)
    experts_in = lax.all_gather(expert_in, "fsdp", axis=1, tiled=True)
    experts_out = lax.all_gather(expert_out, "fsdp", axis=1, tiled=True)

    qkv_own = packed[:, : 2 * group]
    small_all = packed[:, 2 * group :].astype(F32).T
    gain_one, gain_two = small_all[0:1], small_all[1:2]
    router = packed[:, 2 * group + 2 : 2 * group + 2 + E]

    hidden_in = tokens_all.astype(F32)
    inverse_one = inverse_rms(hidden_in)
    normed_one = (hidden_in * inverse_one * gain_one).astype(BF16)
    projected = dot(normed_one, qkv_own, ((1,), (0,)))
    cosine, sine = rope_tables(seq_len)

    def rotate(value):
        return value * cosine + swap_halves(value) * sine

    def rotate_back(value):
        return value * cosine - swap_halves(value) * sine

    query = jnp.stack(
        [rotate(projected[:, :head]), rotate(projected[:, head:group])], 0
    ).astype(BF16)
    key = rotate(projected[:, group : group + head]).astype(BF16)
    value = projected[:, group + head :].astype(BF16)
    context, sums = attention_forward(query, key, value, segment_ids)
    contexts = lax.all_gather(context, "sp", axis=0, tiled=False)
    context_all = contexts.transpose(1, 0, 2).reshape(seq_len, width)
    attended = dot(context_all, out_full, ((1,), (0,)))
    middle = hidden_in + RESIDUAL * attended
    inverse_two = inverse_rms(middle)
    normed_two = (middle * inverse_two * gain_two).astype(BF16)
    logits = dot(normed_two, router, ((1,), (0,)))
    mask = late[:, width : width + E] > 0
    shown = jnp.where(mask, logits, -jnp.inf)
    expo = jnp.exp(shown - jnp.max(shown, -1, keepdims=True))
    gates = expo / jnp.sum(expo, -1, keepdims=True)
    grad_mixed = RESIDUAL * late[:, :width].astype(F32)

    mixed = 0.0
    grad_sum = 0.0
    extra = 0.0
    weight_sums = []
    lane = jnp.arange(128, dtype=jnp.int32)
    for local in range(expert_in.shape[0]):
        expert = sp_index * expert_in.shape[0] + local
        gate = jnp.sum(
            jnp.where(jnp.arange(E, dtype=jnp.int32) == expert, gates, 0.0), -1, keepdims=True
        )
        w_in, w_out = experts_in[local], experts_out[local]
        pre_act = dot(normed_two, w_in, ((1,), (0,)))
        gate_part, up_part = pre_act[:, :hidden], pre_act[:, hidden:]
        sigmoid = jax.nn.sigmoid(gate_part)
        activated = (gate_part * sigmoid * up_part).astype(BF16)
        produced = dot(activated, w_out, ((1,), (1,))).astype(BF16).astype(F32)
        mixed = mixed + gate * produced
        grad_gate = jnp.sum(grad_mixed * produced, -1, keepdims=True)
        extra = extra + jnp.where(lane == expert, gate * grad_gate, 0.0)
        grad_result = (gate * grad_mixed).astype(BF16)
        grad_act = dot(grad_result, w_out, ((1,), (0,)))
        grad_pre = jnp.concatenate(
            [
                grad_act * up_part * sigmoid * (1.0 + gate_part * (1.0 - sigmoid)),
                grad_act * gate_part * sigmoid,
            ],
            1,
        ).astype(BF16)
        grad_sum = grad_sum + dot(grad_pre, w_in, ((1,), (1,)))
        grad_in = dot(normed_two, grad_pre, ((0,), (0,))).astype(BF16)
        grad_out = dot(grad_result, activated, ((0,), (0,))).astype(BF16)
        weight_sums.append((grad_in, grad_out))

    mixed_own = lax.psum_scatter(mixed.astype(BF16), "sp", scatter_dimension=0, tiled=True)
    block_out = own(middle) + RESIDUAL * mixed_own.astype(F32)

    back = jnp.concatenate([grad_sum, extra], 1).astype(BF16)
    back = sum_over(back.reshape(n_sp, rows, width + 128), "sp", n_sp)
    weighted = back[:, width : width + E]
    gates_own, normed_own = own(gates), own(normed_two)
    grad_logits = weighted - gates_own * jnp.sum(weighted, -1, keepdims=True)
    grad_normed_two = back[:, :width] + lax.dot_general(
        grad_logits, router.astype(F32), (((1,), (1,)), ((), ())), precision=lax.Precision.HIGHEST
    )
    router_part = lax.dot_general(
        normed_own.astype(F32), grad_logits, (((0,), (0,)), ((), ())), precision=lax.Precision.HIGHEST
    )
    middle_own, inverse_own = own(middle), own(inverse_two)
    gain_two_part = jnp.sum(grad_normed_two * middle_own * inverse_own, 0)
    grad_middle = cotangent.astype(F32) + rms_backward(
        grad_normed_two, middle_own, inverse_own, gain_two
    )
    grad_attended = (RESIDUAL * grad_middle).astype(BF16)

    grad_attended_all = lax.all_gather(grad_attended, "sp", axis=0, tiled=True)
    grad_inner, grad_outer = [], []
    for grad_in, grad_out in weight_sums:
        grad_inner.append(sum_over(grad_in.reshape(n_fsdp, -1, width), "fsdp", n_fsdp))
        grad_outer.append(sum_over(grad_out.reshape(n_fsdp, -1, hidden), "fsdp", n_fsdp))

    out_own = lax.dynamic_slice_in_dim(out_full, sp_index * group, group, 0)
    grad_context = dot(grad_attended_all, out_own, ((1,), (1,))).astype(BF16)
    out_part = dot(context, grad_attended_all, ((0,), (0,)))
    out_sum = sum_over(
        out_part.astype(BF16).reshape(n_fsdp, group // n_fsdp, width), "fsdp", n_fsdp
    )
    shares = out_part.shape[0] // n_fsdp
    moves = []
    for f in range(n_fsdp):
        for s in range(n_sp):
            moves.append((f * n_sp + s, (s * group + f * shares) // weight_rows))
    if shares == weight_rows:
        out_grad = lax.ppermute(out_sum, ("fsdp", "sp"), moves)
    else:
        whole = lax.all_gather(out_sum, ("fsdp", "sp"), axis=0, tiled=False)
        whole = whole.reshape(n_fsdp, n_sp, shares, width).transpose(1, 0, 2, 3)
        device = lax.axis_index("fsdp") * n_sp + sp_index
        out_grad = lax.dynamic_slice_in_dim(
            whole.reshape(width, width), device * weight_rows, weight_rows, 0
        )

    grad_query, grad_key, grad_value = attention_backward(
        query, key, value, segment_ids, sums, grad_context
    )
    grad_proj = jnp.concatenate(
        [
            rotate_back(grad_query[0].astype(F32)),
            rotate_back(grad_query[1].astype(F32)),
            rotate_back(grad_key.astype(F32)),
            grad_value.astype(F32),
        ],
        1,
    ).astype(BF16)
    grad_first = dot(grad_proj, qkv_own, ((1,), (1,))).astype(BF16)
    grad_normed_one = sum_over(grad_first.reshape(n_sp, rows, width), "sp", n_sp)
    qkv_part = dot(normed_one, grad_proj, ((0,), (0,)))
    small_part = jnp.concatenate([gain_two_part[:, None], router_part], 1)
    small_part = jnp.pad(small_part, ((0, 0), (0, 128 - small_part.shape[1])))
    bundle = jnp.concatenate([qkv_part, small_part], 1).astype(BF16)
    bundle = sum_over(bundle.reshape(n_fsdp, -1, bundle.shape[1]), "fsdp", n_fsdp)
    bundle = lax.all_to_all(
        bundle.reshape(n_sp, weight_rows, bundle.shape[1]),
        "sp",
        split_axis=0,
        concat_axis=0,
        tiled=True,
    )
    qkv_grad = jnp.concatenate(
        [
            bundle[:, :, :group].transpose(1, 0, 2).reshape(weight_rows, q_span),
            bundle[:, :, group : group + head].transpose(1, 0, 2).reshape(weight_rows, k_span),
            bundle[:, :, group + head : 2 * group].transpose(1, 0, 2).reshape(weight_rows, k_span),
        ],
        1,
    )
    smalls = jnp.sum(bundle[:, :, 2 * group :], 0)
    gain_two_grad = smalls[:, 0]
    router_grad = smalls[:, 1 : 1 + E]
    gain_one_grad = jnp.sum(qkv_grad * qkv_weight.astype(F32), 1) / norm1_gain.astype(F32)
    hidden_own = tokens.astype(F32)
    input_grad = grad_middle + rms_backward(
        grad_normed_one, hidden_own, inverse_rms(hidden_own), gain_one
    )
    return (
        block_out,
        input_grad,
        gain_one_grad,
        qkv_grad,
        out_grad,
        gain_two_grad,
        router_grad,
        jnp.stack(grad_inner, 0),
        jnp.stack(grad_outer, 0),
    )


def solution(mesh):
    both = P(("fsdp", "sp"), None)
    flat = P(("fsdp", "sp"))
    expert = P("sp", "fsdp", None)
    return jax.shard_map(
        shards,
        mesh=mesh,
        in_specs=(both, P("fsdp", None), both, both, flat, both, both, flat, both, expert, expert),
        out_specs=(both, both, flat, both, both, flat, both, expert, expert),
        check_vma=False,
    )
```

```python
import jax
import jax.numpy as jnp
import numpy as np
from jax import lax
from jax.experimental import pallas as pl
from jax.experimental.pallas import tpu as pltpu
from jax.sharding import PartitionSpec as P

HQ = 16
KEY_VALUE_HEADS = 8
HEAD_SIZE = 64
E = 16
EPSILON = 1e-06
RESIDUAL = 0.22
BLOCK = 256
LONGEST = 512
BF16 = jnp.bfloat16
F32 = jnp.float32


def rope_tables(count):
    frequency = np.float32(10000.0) ** (
        np.float32(-2.0) * np.arange(HEAD_SIZE // 2, dtype=np.float32) / np.float32(HEAD_SIZE)
    )
    angles = np.arange(count, dtype=np.float32)[:, None] * frequency.astype(np.float32)[None, :]
    cosine = np.cos(angles).astype(np.float32)
    sine = np.sin(angles).astype(np.float32)
    return np.concatenate([cosine] * 4, 1), np.concatenate([-sine, sine] * 2, 1)


def dot(left, right, contract):
    return lax.dot_general(left, right, (contract, ((), ())), preferred_element_type=F32)


def inverse_rms(value):
    return lax.rsqrt(jnp.mean(value * value, -1, keepdims=True) + EPSILON)


def rms_backward(grad, value, inverse, gain):
    scaled = grad * gain
    return inverse * scaled - value * (inverse**3) * jnp.mean(scaled * value, -1, keepdims=True)


MESH = pl.DeviceIdType.MESH
VMEM = pl.BlockSpec(memory_space=pltpu.VMEM)
HBM = pl.BlockSpec(memory_space=pl.ANY)
DMA = pltpu.SemaphoreType.DMA
SP, FSDP = 8, 16


def remote(src, dst, send, recv, **device):
    return pltpu.make_async_remote_copy(
        src_ref=src,
        dst_ref=dst,
        send_sem=send,
        recv_sem=recv,
        device_id=device,
        device_id_type=MESH,
    )


def meet(with_fsdp):
    barrier = pltpu.get_barrier_semaphore()
    me = lax.axis_index("sp")
    for step in range(1, SP):
        pl.semaphore_signal(
            barrier, inc=1, device_id={"sp": lax.rem(me + step, SP)}, device_id_type=MESH
        )
    count = SP - 1
    if with_fsdp:
        size = lax.axis_size("fsdp")
        mine = lax.axis_index("fsdp")
        for step in range(1, size):
            pl.semaphore_signal(
                barrier, inc=1, device_id={"fsdp": lax.rem(mine + step, size)}, device_id_type=MESH
            )
        count += size - 1
    pl.semaphore_wait(barrier, count)


def places():
    me = lax.axis_index("sp")
    level, core = me // 2, lax.rem(me, 2)
    up = lax.rem(level + 1, 4)
    down = lax.rem(level + 3, 4)
    far = lax.rem(level + 2, 4)
    return me, core, level, up, down, far


class Ring:
    def __init__(self, source, slot, part, send, recv, local):
        me, core, level, up, down, far = places()
        self.me = me
        up_id, down_id, far_id = up * 2 + core, down * 2 + core, far * 2 + core
        other = level * 2 + (1 - core)

        def go(src, dst, number, peer):
            return remote(src, dst, send.at[number], recv.at[number], sp=peer)

        self.first = [
            go(source, slot(me), 0, up_id),
            go(source, slot(me), 1, down_id),
            go(source, slot(me), 2, other),
        ]
        self.local = pltpu.make_async_copy(source, slot(me), local)
        self.next_up = [
            go(part(down_id, 0), part(down_id, 0), 3, up_id),
            go(slot(down_id), slot(down_id), 4, other),
        ]
        self.next_down = [
            go(part(up_id, 1), part(up_id, 1), 5, down_id),
            go(slot(up_id), slot(up_id), 6, other),
        ]
        self.last = go(slot(far_id), slot(far_id), 7, other)

    def start(self):
        for copy in self.first:
            copy.start()
        self.local.start()

    def finish(self):
        self.first[0].wait_recv()
        for copy in self.next_up:
            copy.start()
        self.first[1].wait_recv()
        for copy in self.next_down:
            copy.start()
        self.next_up[0].wait_recv()
        self.next_down[0].wait_recv()
        self.last.start()
        self.local.wait()
        for copy in (self.first[0], self.first[1], self.next_up[0], self.next_down[0]):
            copy.wait_send()
        for copy in (self.first[2], self.next_up[1], self.next_down[1], self.last):
            copy.wait()


def ring_rows(source, target, send, recv, local):
    half = source.shape[0] // 2
    return Ring(
        source,
        lambda index: target.at[index],
        lambda index, side: target.at[index, pl.ds(side * half, half)],
        send,
        recv,
        local,
    )


def ring_columns(source, target, send, recv, local):
    rows, wide = source.shape
    half = rows // 2

    def columns(index):
        return pl.ds(pl.multiple_of(index * wide, wide), wide)

    return Ring(
        source,
        lambda index: target.at[:, columns(index)],
        lambda index, side: target.at[pl.ds(side * half, half), columns(index)],
        send,
        recv,
        local,
    )


def spread(axis, size, source, target, send, recv, local, blocks):
    me = lax.axis_index(axis)
    copies = []
    for step in range(1, size):
        peer = lax.rem(me + step, size)
        copies.append(
            remote(
                source.at[peer] if blocks else source,
                target.at[me],
                send.at[step],
                recv.at[step],
                **{axis: peer},
            )
        )
    copies.append(pltpu.make_async_copy(source.at[me] if blocks else source, target.at[me], local))
    return copies


def run(copies):
    for copy in copies:
        copy.start()


def settle(copies):
    for copy in copies:
        copy.wait()


def first_kernel(
    tokens, packed, outw, tokens_all, mid, packed_all, out_mid, s0, r0, s1, r1, s2, r2, s3, r3, loc
):
    meet(True)
    size = lax.axis_size("fsdp")
    small = spread("sp", SP, packed, mid, s1, r1, loc.at[0], True)
    run(small)
    ring = ring_rows(tokens, tokens_all, s0, r0, loc.at[1])
    ring.start()
    out_copies = spread("sp", SP, outw, out_mid, s2, r2, loc.at[2], False)
    run(out_copies)
    settle(small)
    big = spread("fsdp", size, mid, packed_all, s3, r3, loc.at[3], False)
    run(big)
    ring.finish()
    settle(out_copies)
    settle(big)


def context_kernel(context, out_mid, context_all, out_all, s0, r0, s1, r1, loc):
    meet(True)
    ring = ring_columns(context, context_all, s0, r0, loc.at[0])
    ring.start()
    big = spread("fsdp", lax.axis_size("fsdp"), out_mid, out_all, s1, r1, loc.at[1], False)
    run(big)
    ring.finish()
    settle(big)


def gather_kernel(source, target, send, recv, local):
    meet(False)
    ring = ring_rows(source, target, send, recv, local)
    ring.start()
    ring.finish()


class Scatter:
    def __init__(self, blocks, other_sums, sums, near, far_parts, send, recv):
        me, core, level, up, down, far = places()
        other = level * 2 + (1 - core)
        self.blocks, self.other_sums, self.sums = blocks, other_sums, sums
        self.near, self.far_parts = near, far_parts
        self.core, self.level, self.up, self.down, self.far = core, level, up, down, far
        half = blocks.shape[1] // 2
        self.half = half
        up_id, down_id = up * 2 + core, down * 2 + core

        def go(src, dst, number, peer):
            return remote(src, dst, send.at[number], recv.at[number], sp=peer)

        order = (far, up, down, level)
        self.pair = [
            go(blocks.at[at * 2 + (1 - core)], other_sums.at[number], number, other)
            for number, at in enumerate(order)
        ]
        self.to_up = go(sums.at[0, pl.ds(0, half)], far_parts.at[0], 4, up_id)
        self.to_down = go(sums.at[0, pl.ds(half, half)], far_parts.at[1], 5, down_id)
        self.full_up = go(sums.at[1], near.at[0], 6, up_id)
        self.full_down = go(sums.at[2], near.at[1], 7, down_id)

    def start(self):
        run(self.pair)

    def both(self, number, at):
        mine = self.blocks[at * 2 + self.core].astype(F32)
        return mine + self.other_sums[number].astype(F32)

    def finish(self, out):
        half = self.half
        self.pair[0].wait_recv()
        self.sums[0] = self.both(0, self.far).astype(BF16)
        self.to_up.start()
        self.to_down.start()
        self.pair[1].wait_recv()
        self.to_up.wait_recv()
        total = self.both(1, self.up)
        self.sums[1, :half] = (total[:half] + self.far_parts[0].astype(F32)).astype(BF16)
        self.sums[1, half:] = total[half:].astype(BF16)
        self.full_up.start()
        self.pair[2].wait_recv()
        self.to_down.wait_recv()
        total = self.both(2, self.down)
        self.sums[2, :half] = total[:half].astype(BF16)
        self.sums[2, half:] = (total[half:] + self.far_parts[1].astype(F32)).astype(BF16)
        self.full_down.start()
        self.pair[3].wait_recv()
        total = self.both(3, self.level)
        self.full_up.wait_recv()
        total = total + self.near[0].astype(F32)
        self.full_down.wait_recv()
        out[...] = total + self.near[1].astype(F32)
        for copy in self.pair + [self.to_up, self.to_down, self.full_up, self.full_down]:
            copy.wait_send()


def scatter_scratch(rows, width):
    return [
        pltpu.VMEM((4, rows, width), BF16),
        pltpu.VMEM((3, rows, width), BF16),
        pltpu.VMEM((2, rows, width), BF16),
        pltpu.VMEM((2, rows // 2, width), BF16),
        DMA((8,)),
        DMA((8,)),
    ]


def scatter_kernel(blocks, out, other_sums, sums, near, far_parts, send, recv):
    meet(False)
    scatter = Scatter(blocks, other_sums, sums, near, far_parts, send, recv)
    scatter.start()
    scatter.finish(out)


def last_kernel(
    blocks, bundle, outp, out, bundle_all, out_sum,
    other_sums, sums, near, far_parts, send, recv,
    bundle_in, out_in, bundle_sum, s1, r1, s2, r2, s3, r3, loc,
):
    meet(True)
    size = lax.axis_size("fsdp")
    scatter = Scatter(blocks, other_sums, sums, near, far_parts, send, recv)
    scatter.start()
    bundles = spread("fsdp", size, bundle, bundle_in, s1, r1, loc.at[0], True)
    run(bundles)
    outs = spread("fsdp", size, outp, out_in, s2, r2, loc.at[1], True)
    run(outs)
    scatter.finish(out)
    settle(bundles)
    total = bundle_in[0].astype(F32)
    for index in range(1, size):
        total = total + bundle_in[index].astype(F32)
    bundle_sum[...] = total.reshape(bundle_sum.shape)
    share = spread("sp", SP, bundle_sum, bundle_all, s3, r3, loc.at[2], True)
    run(share)
    settle(outs)
    total = out_in[0].astype(F32)
    for index in range(1, size):
        total = total + out_in[index].astype(F32)
    out_sum[...] = total
    settle(share)


def wide_call(kernel, name, number, inputs, in_specs, outs, out_specs, scratch):
    return pl.pallas_call(
        kernel,
        name=name,
        out_shape=outs,
        in_specs=in_specs,
        out_specs=out_specs,
        scratch_shapes=scratch,
        compiler_params=pltpu.CompilerParams(
            collective_id=number, has_side_effects=True, vmem_limit_bytes=48 * 2**20
        ),
    )(*inputs)


def local_call(kernel, name, inputs, outs, scratch=(), flops=0):
    moved = sum(array.size * array.dtype.itemsize for array in inputs)
    return pl.pallas_call(
        kernel,
        name=name,
        out_shape=outs,
        in_specs=[VMEM] * len(inputs),
        out_specs=jax.tree.map(lambda _: VMEM, outs),
        scratch_shapes=scratch,
        cost_estimate=pl.CostEstimate(flops=flops, bytes_accessed=moved, transcendentals=0),
        compiler_params=pltpu.CompilerParams(vmem_limit_bytes=48 * 2**20),
    )(*inputs)


def swap_halves(value):
    wide = value.shape[-1]
    lane = lax.broadcasted_iota(jnp.int32, value.shape, 1)
    return jnp.where(
        lane % HEAD_SIZE < HEAD_SIZE // 2,
        pltpu.roll(value, wide - HEAD_SIZE // 2, 1),
        pltpu.roll(value, HEAD_SIZE // 2, 1),
    )


def first_head(shape):
    return lax.broadcasted_iota(jnp.int32, shape, 1) < HEAD_SIZE


def stack_heads(slab):
    is_first = first_head(slab.shape)
    zero = jnp.zeros_like(slab)
    return jnp.concatenate([jnp.where(is_first, slab, zero), jnp.where(is_first, zero, slab)], 0)


def merge_heads(stacked):
    half = stacked.shape[0] // 2
    return jnp.where(first_head((half, stacked.shape[1])), stacked[:half], stacked[half:])


def block_scores(block, query2, key2, seg_column, seg_row):
    lo, hi = block * BLOCK, (block + 1) * BLOCK
    k_lo = max(0, lo - LONGEST)
    rows = lo + lax.broadcasted_iota(jnp.int32, (BLOCK, hi - k_lo), 0)
    keys = k_lo + lax.broadcasted_iota(jnp.int32, (BLOCK, hi - k_lo), 1)
    allowed = (keys <= rows) & (seg_column[lo:hi, :] == seg_row[:, k_lo:hi])
    scores = dot(query2, key2[k_lo:hi, :], ((1,), (1,))) * HEAD_SIZE**-0.5
    return jnp.where(jnp.concatenate([allowed, allowed], 0), scores, -jnp.inf)


def attention_kernel(
    proj, cosine, sine, seg_column, seg_row, context, query, key2, value2, sums
):
    cos_rows, sin_rows = cosine[...], sine[...]
    slab = proj[:, :128]
    query[...] = (slab * cos_rows + swap_halves(slab) * sin_rows).astype(BF16)
    slab = proj[:, 128:]
    is_first = first_head(slab.shape)
    turned = slab * cos_rows + swap_halves(slab) * sin_rows
    key2[...] = jnp.where(is_first, turned, pltpu.roll(turned, HEAD_SIZE, 1)).astype(BF16)
    value2[...] = jnp.where(is_first, pltpu.roll(slab, HEAD_SIZE, 1), slab).astype(BF16)
    for block in range(proj.shape[0] // BLOCK):
        lo, hi = block * BLOCK, (block + 1) * BLOCK
        k_lo = max(0, lo - LONGEST)
        scores = block_scores(block, stack_heads(query[lo:hi, :]), key2, seg_column, seg_row)
        top = jnp.max(scores, -1, keepdims=True)
        expo = jnp.exp(scores - top)
        total = jnp.sum(expo, -1, keepdims=True)
        probs = (expo / total).astype(BF16)
        context[lo:hi, :] = merge_heads(dot(probs, value2[k_lo:hi, :], ((1,), (0,)))).astype(BF16)
        sums[block] = jnp.broadcast_to(top + jnp.log(total), (2 * BLOCK, 128))


def attention_back_kernel(
    query, key2, value2, sums, grad_context, cosine, sine, seg_column, seg_row,
    grad_proj, grad_key, grad_value,
):
    grad_key[...] = jnp.zeros_like(grad_key)
    grad_value[...] = jnp.zeros_like(grad_value)
    for block in range(query.shape[0] // BLOCK):
        lo, hi = block * BLOCK, (block + 1) * BLOCK
        k_lo = max(0, lo - LONGEST)
        query2 = stack_heads(query[lo:hi, :])
        scores = block_scores(block, query2, key2, seg_column, seg_row)
        probs = jnp.exp(scores - sums[block][:, :1])
        grad_rows = stack_heads(grad_context[lo:hi, :])
        grad_probs = dot(grad_rows, value2[k_lo:hi, :], ((1,), (1,)))
        row_dot = jnp.sum(grad_probs * probs, -1, keepdims=True)
        grad_scores = (probs * (grad_probs - row_dot) * HEAD_SIZE**-0.5).astype(BF16)
        moved = merge_heads(dot(grad_scores, key2[k_lo:hi, :], ((1,), (0,))))
        moved = moved.astype(BF16).astype(F32)
        grad_proj[lo:hi, :128] = (
            moved * cosine[lo:hi, :] - swap_halves(moved) * sine[lo:hi, :]
        ).astype(BF16)
        grad_key[k_lo:hi, :] += dot(grad_scores, query2, ((0,), (0,)))
        grad_value[k_lo:hi, :] += dot(probs.astype(BF16), grad_rows, ((0,), (0,)))
    is_first = first_head(grad_key.shape)
    moved = grad_key[...]
    moved = (moved + pltpu.roll(moved, HEAD_SIZE, 1)).astype(BF16).astype(F32)
    moved = moved * cosine[...] - swap_halves(moved) * sine[...]
    other = grad_value[...]
    other = other + pltpu.roll(other, HEAD_SIZE, 1)
    grad_proj[:, 128:] = jnp.where(is_first, moved, other).astype(BF16)


def shards(
    tokens,
    segments,
    top_idx,
    cotangent,
    norm1_gain,
    qkv_weight,
    out_weight,
    norm2_gain,
    router_weight,
    expert_in,
    expert_out,
):
    n_sp = lax.axis_size("sp")
    n_fsdp = lax.axis_size("fsdp")
    sp_index = lax.axis_index("sp")
    rows, width = tokens.shape
    seq_len = rows * n_sp
    weight_rows = qkv_weight.shape[0]
    hidden = expert_out.shape[2]
    q_span, k_span = HQ * HEAD_SIZE, KEY_VALUE_HEADS * HEAD_SIZE
    group = q_span // n_sp
    head = k_span // n_sp
    segment_ids = segments[0]

    def own(array):
        return lax.dynamic_slice_in_dim(array, sp_index * rows, rows, 0)

    def sum_over(array, axis, count):
        parts = lax.all_to_all(array, axis, split_axis=0, concat_axis=0, tiled=True)
        return jnp.sum(parts.astype(F32), 0)

    small = jnp.concatenate([norm1_gain[:, None], norm2_gain[:, None], router_weight], 1)
    small = jnp.pad(small, ((0, 0), (0, 128 - small.shape[1])))
    packed = jnp.concatenate(
        [
            qkv_weight[:, :q_span].reshape(weight_rows, n_sp, group),
            qkv_weight[:, q_span : q_span + k_span].reshape(weight_rows, n_sp, head),
            qkv_weight[:, q_span + k_span :].reshape(weight_rows, n_sp, head),
            jnp.broadcast_to(small[:, None], (weight_rows, n_sp, 128)),
        ],
        2,
    ).transpose(1, 0, 2)
    pack_width = packed.shape[2]
    any_shape = jax.ShapeDtypeStruct
    tokens_all, _, packed, out_mid = wide_call(
        first_kernel,
        "first_gather",
        1,
        (tokens, packed, out_weight),
        [HBM] * 3,
        (
            any_shape((SP, rows, width), BF16),
            any_shape((SP, weight_rows, pack_width), BF16),
            any_shape((n_fsdp, SP, weight_rows, pack_width), BF16),
            any_shape((SP, weight_rows, width), BF16),
        ),
        [HBM] * 4,
        [DMA((8,))] * 6 + [DMA((n_fsdp,))] * 2 + [DMA((4,))],
    )
    packed = packed.reshape(width, pack_width)
    tokens_all = tokens_all.reshape(seq_len, width)
    chosen = jnp.sum(
        (top_idx[:, :, None] == jnp.arange(128, dtype=jnp.int32)).astype(F32), 1
    ).astype(BF16)
    experts = lax.all_gather(
        jnp.concatenate([expert_in, expert_out], 2), "fsdp", axis=1, tiled=True
    )
    late = lax.all_gather(jnp.concatenate([cotangent, chosen], 1), "sp", axis=0, tiled=True)

    qkv_own = packed[:, : 2 * group]
    small_all = packed[:, 2 * group :].astype(F32).T
    gain_one, gain_two = small_all[0:1], small_all[1:2]
    router = packed[:, 2 * group + 2 : 2 * group + 2 + E]

    hidden_in = tokens_all.astype(F32)
    inverse_one = inverse_rms(hidden_in)
    normed_one = (hidden_in * inverse_one * gain_one).astype(BF16)
    projected = dot(normed_one, qkv_own, ((1,), (0,)))
    cosine, sine = rope_tables(seq_len)
    seg_row, seg_column = segment_ids[None, :], segment_ids[:, None]
    context, query, key2, value2, sums = local_call(
        attention_kernel,
        "attention",
        (projected, cosine, sine, seg_column, seg_row),
        (
            any_shape((seq_len, 128), BF16),
            any_shape((seq_len, 128), BF16),
            any_shape((seq_len, 128), BF16),
            any_shape((seq_len, 128), BF16),
            any_shape((seq_len // BLOCK, 2 * BLOCK, 128), F32),
        ),
        flops=2 * 10**9,
    )
    context_all, out_full = wide_call(
        context_kernel,
        "context_gather",
        2,
        (context, out_mid),
        [HBM] * 2,
        (any_shape((seq_len, width), BF16), any_shape((n_fsdp, SP, weight_rows, width), BF16)),
        [HBM] * 2,
        [DMA((8,))] * 2 + [DMA((n_fsdp,))] * 2 + [DMA((2,))],
    )
    out_full = out_full.reshape(width, width)
    attended = dot(context_all, out_full, ((1,), (0,)))
    middle = hidden_in + RESIDUAL * attended
    inverse_two = inverse_rms(middle)
    normed_two = (middle * inverse_two * gain_two).astype(BF16)
    logits = dot(normed_two, router, ((1,), (0,)))
    mask = late[:, width : width + E] > 0
    shown = jnp.where(mask, logits, -jnp.inf)
    expo = jnp.exp(shown - jnp.max(shown, -1, keepdims=True))
    gates = expo / jnp.sum(expo, -1, keepdims=True)
    grad_mixed = RESIDUAL * late[:, :width].astype(F32)

    mixed = 0.0
    grad_sum = 0.0
    extra = 0.0
    weight_sums = []
    lane = jnp.arange(128, dtype=jnp.int32)
    hidden_in_span = expert_in.shape[2]
    for local in range(expert_in.shape[0]):
        expert = sp_index * expert_in.shape[0] + local
        gate = jnp.sum(
            jnp.where(jnp.arange(E, dtype=jnp.int32) == expert, gates, 0.0), -1, keepdims=True
        )
        w_in, w_out = experts[local, :, :hidden_in_span], experts[local, :, hidden_in_span:]
        pre_act = dot(normed_two, w_in, ((1,), (0,)))
        gate_part, up_part = pre_act[:, :hidden], pre_act[:, hidden:]
        sigmoid = jax.nn.sigmoid(gate_part)
        activated = (gate_part * sigmoid * up_part).astype(BF16)
        produced = dot(activated, w_out, ((1,), (1,))).astype(BF16).astype(F32)
        mixed = mixed + gate * produced
        grad_gate = jnp.sum(grad_mixed * produced, -1, keepdims=True)
        extra = extra + jnp.where(lane == expert, gate * grad_gate, 0.0)
        grad_result = (gate * grad_mixed).astype(BF16)
        grad_act = dot(grad_result, w_out, ((1,), (0,)))
        grad_pre = jnp.concatenate(
            [
                grad_act * up_part * sigmoid * (1.0 + gate_part * (1.0 - sigmoid)),
                grad_act * gate_part * sigmoid,
            ],
            1,
        ).astype(BF16)
        grad_sum = grad_sum + dot(grad_pre, w_in, ((1,), (1,)))
        grad_in = dot(normed_two, grad_pre, ((0,), (0,))).astype(BF16)
        grad_out = dot(grad_result, activated, ((0,), (0,))).astype(BF16)
        weight_sums.append((grad_in, grad_out))

    mixed_own = lax.psum_scatter(mixed.astype(BF16), "sp", scatter_dimension=0, tiled=True)
    block_out = own(middle) + RESIDUAL * mixed_own.astype(F32)

    back = jnp.concatenate([grad_sum, extra], 1).astype(BF16)
    back = wide_call(
        scatter_kernel,
        "scatter_back",
        3,
        (back.reshape(SP, rows, width + 128),),
        [VMEM],
        any_shape((rows, width + 128), F32),
        VMEM,
        scatter_scratch(rows, width + 128),
    )
    weighted = back[:, width : width + E]
    gates_own, normed_own = own(gates), own(normed_two)
    grad_logits = weighted - gates_own * jnp.sum(weighted, -1, keepdims=True)
    grad_normed_two = back[:, :width] + lax.dot_general(
        grad_logits, router.astype(F32), (((1,), (1,)), ((), ())), precision=lax.Precision.HIGHEST
    )
    router_part = lax.dot_general(
        normed_own.astype(F32), grad_logits, (((0,), (0,)), ((), ())), precision=lax.Precision.HIGHEST
    )
    middle_own, inverse_own = own(middle), own(inverse_two)
    gain_two_part = jnp.sum(grad_normed_two * middle_own * inverse_own, 0)
    grad_middle = cotangent.astype(F32) + rms_backward(
        grad_normed_two, middle_own, inverse_own, gain_two
    )
    grad_attended = (RESIDUAL * grad_middle).astype(BF16)

    grad_attended_all = wide_call(
        gather_kernel,
        "gather_back",
        4,
        (grad_attended,),
        [HBM],
        any_shape((SP, rows, width), BF16),
        HBM,
        [DMA((8,)), DMA((8,)), DMA],
    ).reshape(seq_len, width)
    grad_inner, grad_outer = [], []
    for grad_in, grad_out in weight_sums:
        grad_inner.append(sum_over(grad_in.reshape(n_fsdp, -1, width), "fsdp", n_fsdp))
        grad_outer.append(sum_over(grad_out.reshape(n_fsdp, -1, hidden), "fsdp", n_fsdp))

    out_own = lax.dynamic_slice_in_dim(out_full, sp_index * group, group, 0)
    grad_context = dot(grad_attended_all, out_own, ((1,), (1,))).astype(BF16)
    out_part = dot(context, grad_attended_all, ((0,), (0,)))
    shares = out_part.shape[0] // n_fsdp
    moves = []
    for f in range(n_fsdp):
        for s in range(n_sp):
            moves.append((f * n_sp + s, (s * group + f * shares) // weight_rows))
    grad_proj = local_call(
        attention_back_kernel,
        "attention_back",
        (query, key2, value2, sums, grad_context, cosine, sine, seg_column, seg_row),
        any_shape((seq_len, 256), BF16),
        [pltpu.VMEM((seq_len, 128), F32)] * 2,
        flops=5 * 10**9,
    )
    grad_first = dot(grad_proj, qkv_own, ((1,), (1,))).astype(BF16)
    qkv_part = dot(normed_one, grad_proj, ((0,), (0,)))
    small_part = jnp.concatenate([gain_two_part[:, None], router_part], 1)
    small_part = jnp.pad(small_part, ((0, 0), (0, 128 - small_part.shape[1])))
    bundle = jnp.concatenate([qkv_part, small_part], 1).astype(BF16)
    grad_normed_one, bundle, out_sum = wide_call(
        last_kernel,
        "last_exchange",
        5,
        (
            grad_first.reshape(SP, rows, width),
            bundle.reshape(n_fsdp, -1, pack_width),
            out_part.astype(BF16).reshape(n_fsdp, shares, width),
        ),
        [VMEM] * 3,
        (
            any_shape((rows, width), F32),
            any_shape((SP, weight_rows, pack_width), F32),
            any_shape((shares, width), F32),
        ),
        (VMEM, VMEM, VMEM),
        scatter_scratch(rows, width)
        + [
            pltpu.VMEM((n_fsdp, width // n_fsdp, pack_width), BF16),
            pltpu.VMEM((n_fsdp, shares, width), BF16),
            pltpu.VMEM((SP, weight_rows, pack_width), F32),
        ]
        + [DMA((n_fsdp,))] * 4
        + [DMA((8,))] * 2
        + [DMA((3,))],
    )
    if shares == weight_rows:
        out_grad = lax.ppermute(out_sum, ("fsdp", "sp"), moves)
    else:
        whole = lax.all_gather(out_sum, ("fsdp", "sp"), axis=0, tiled=False)
        whole = whole.reshape(n_fsdp, n_sp, shares, width).transpose(1, 0, 2, 3)
        device = lax.axis_index("fsdp") * n_sp + sp_index
        out_grad = lax.dynamic_slice_in_dim(
            whole.reshape(width, width), device * weight_rows, weight_rows, 0
        )

    qkv_grad = jnp.concatenate(
        [
            bundle[:, :, :group].transpose(1, 0, 2).reshape(weight_rows, q_span),
            bundle[:, :, group : group + head].transpose(1, 0, 2).reshape(weight_rows, k_span),
            bundle[:, :, group + head : 2 * group].transpose(1, 0, 2).reshape(weight_rows, k_span),
        ],
        1,
    )
    smalls = jnp.sum(bundle[:, :, 2 * group :], 0)
    gain_two_grad = smalls[:, 0]
    router_grad = smalls[:, 1 : 1 + E]
    gain_one_grad = jnp.sum(qkv_grad * qkv_weight.astype(F32), 1) / norm1_gain.astype(F32)
    hidden_own = tokens.astype(F32)
    input_grad = grad_middle + rms_backward(
        grad_normed_one, hidden_own, inverse_rms(hidden_own), gain_one
    )
    return (
        block_out,
        input_grad,
        gain_one_grad,
        qkv_grad,
        out_grad,
        gain_two_grad,
        router_grad,
        jnp.stack(grad_inner, 0),
        jnp.stack(grad_outer, 0),
    )


def solution(mesh):
    both = P(("fsdp", "sp"), None)
    flat = P(("fsdp", "sp"))
    expert = P("sp", "fsdp", None)
    return jax.shard_map(
        shards,
        mesh=mesh,
        in_specs=(both, P("fsdp", None), both, both, flat, both, both, flat, both, expert, expert),
        out_specs=(both, both, flat, both, both, flat, both, expert, expert),
        check_vma=False,
    )
```

```python
import jax
import jax.numpy as jnp
import numpy as np
from jax import lax
from jax.experimental import pallas as pl
from jax.experimental.pallas import tpu as pltpu
from jax.sharding import PartitionSpec as P

HQ = 16
KEY_VALUE_HEADS = 8
HEAD_SIZE = 64
E = 16
EPSILON = 1e-06
RESIDUAL = 0.22
BLOCK = 256
LONGEST = 512
BF16 = jnp.bfloat16
F32 = jnp.float32


def rope_tables(count):
    frequency = np.float32(10000.0) ** (
        np.float32(-2.0) * np.arange(HEAD_SIZE // 2, dtype=np.float32) / np.float32(HEAD_SIZE)
    )
    angles = np.arange(count, dtype=np.float32)[:, None] * frequency.astype(np.float32)[None, :]
    cosine = np.cos(angles).astype(np.float32)
    sine = np.sin(angles).astype(np.float32)
    return np.concatenate([cosine] * 4, 1), np.concatenate([-sine, sine] * 2, 1)


def dot(left, right, contract):
    return lax.dot_general(left, right, (contract, ((), ())), preferred_element_type=F32)


def inverse_rms(value):
    return lax.rsqrt(jnp.mean(value * value, -1, keepdims=True) + EPSILON)


def rms_backward(grad, value, inverse, gain):
    scaled = grad * gain
    return inverse * scaled - value * (inverse**3) * jnp.mean(scaled * value, -1, keepdims=True)


MESH = pl.DeviceIdType.MESH
VMEM = pl.BlockSpec(memory_space=pltpu.VMEM)
HBM = pl.BlockSpec(memory_space=pl.ANY)
DMA = pltpu.SemaphoreType.DMA
SP, FSDP = 8, 16


def remote(src, dst, send, recv, **device):
    return pltpu.make_async_remote_copy(
        src_ref=src,
        dst_ref=dst,
        send_sem=send,
        recv_sem=recv,
        device_id=device,
        device_id_type=MESH,
    )


def meet(with_fsdp):
    barrier = pltpu.get_barrier_semaphore()
    me = lax.axis_index("sp")
    for step in range(1, SP):
        pl.semaphore_signal(
            barrier, inc=1, device_id={"sp": lax.rem(me + step, SP)}, device_id_type=MESH
        )
    count = SP - 1
    if with_fsdp:
        size = lax.axis_size("fsdp")
        mine = lax.axis_index("fsdp")
        for step in range(1, size):
            pl.semaphore_signal(
                barrier, inc=1, device_id={"fsdp": lax.rem(mine + step, size)}, device_id_type=MESH
            )
        count += size - 1
    pl.semaphore_wait(barrier, count)


def places():
    me = lax.axis_index("sp")
    level, core = me // 2, lax.rem(me, 2)
    up = lax.rem(level + 1, 4)
    down = lax.rem(level + 3, 4)
    far = lax.rem(level + 2, 4)
    return me, core, level, up, down, far


class Ring:
    def __init__(self, source, slot, part, send, recv, local):
        me, core, level, up, down, far = places()
        self.me = me
        up_id, down_id, far_id = up * 2 + core, down * 2 + core, far * 2 + core
        other = level * 2 + (1 - core)

        def go(src, dst, number, peer):
            return remote(src, dst, send.at[number], recv.at[number], sp=peer)

        self.first = [
            go(source, slot(me), 0, up_id),
            go(source, slot(me), 1, down_id),
            go(source, slot(me), 2, other),
        ]
        self.local = pltpu.make_async_copy(source, slot(me), local)
        self.next_up = [
            go(part(down_id, 0), part(down_id, 0), 3, up_id),
            go(slot(down_id), slot(down_id), 4, other),
        ]
        self.next_down = [
            go(part(up_id, 1), part(up_id, 1), 5, down_id),
            go(slot(up_id), slot(up_id), 6, other),
        ]
        self.last = go(slot(far_id), slot(far_id), 7, other)

    def start(self):
        for copy in self.first:
            copy.start()
        self.local.start()

    def finish(self):
        self.first[0].wait_recv()
        for copy in self.next_up:
            copy.start()
        self.first[1].wait_recv()
        for copy in self.next_down:
            copy.start()
        self.next_up[0].wait_recv()
        self.next_down[0].wait_recv()
        self.last.start()
        self.local.wait()
        for copy in (self.first[0], self.first[1], self.next_up[0], self.next_down[0]):
            copy.wait_send()
        for copy in (self.first[2], self.next_up[1], self.next_down[1], self.last):
            copy.wait()


def ring_rows(source, target, send, recv, local):
    half = source.shape[0] // 2
    return Ring(
        source,
        lambda index: target.at[index],
        lambda index, side: target.at[index, pl.ds(side * half, half)],
        send,
        recv,
        local,
    )


def ring_columns(source, target, send, recv, local):
    rows, wide = source.shape
    half = rows // 2

    def columns(index):
        return pl.ds(pl.multiple_of(index * wide, wide), wide)

    return Ring(
        source,
        lambda index: target.at[:, columns(index)],
        lambda index, side: target.at[pl.ds(side * half, half), columns(index)],
        send,
        recv,
        local,
    )


def spread(axis, size, source, target, send, recv, local, blocks):
    me = lax.axis_index(axis)
    copies = []
    for step in range(1, size):
        peer = lax.rem(me + step, size)
        copies.append(
            remote(
                source.at[peer] if blocks else source,
                target.at[me],
                send.at[step],
                recv.at[step],
                **{axis: peer},
            )
        )
    copies.append(pltpu.make_async_copy(source.at[me] if blocks else source, target.at[me], local))
    return copies


def run(copies):
    for copy in copies:
        copy.start()


def settle(copies):
    for copy in copies:
        copy.wait()


def first_kernel(
    tokens, cotangent, top_idx, qkv, small, outw,
    tokens_all, late_all, mid, packed_all, out_mid,
    packed, late, s0, r0, s1, r1, s2, r2, s3, r3, s4, r4, loc,
):
    group, q_span = 2 * HEAD_SIZE, HQ * HEAD_SIZE
    k_span = KEY_VALUE_HEADS * HEAD_SIZE
    for index in range(SP):
        k_at = q_span + index * HEAD_SIZE
        packed[index, :, :group] = qkv[:, index * group : (index + 1) * group]
        packed[index, :, group : 2 * group] = jnp.concatenate(
            [
                qkv[:, k_at : k_at + HEAD_SIZE],
                qkv[:, k_at + k_span : k_at + k_span + HEAD_SIZE],
            ],
            1,
        )
        packed[index, :, 2 * group :] = small[...]
    meet(True)
    size = lax.axis_size("fsdp")
    small_copies = spread("sp", SP, packed, mid, s1, r1, loc.at[0], True)
    run(small_copies)
    ring = ring_rows(tokens, tokens_all, s0, r0, loc.at[1])
    ring.start()
    width = cotangent.shape[1]
    late[:, :width] = cotangent[...]
    lane = lax.broadcasted_iota(jnp.int32, (cotangent.shape[0], 128), 1)
    chosen = jnp.zeros(lane.shape, F32)
    for choice in range(top_idx.shape[1]):
        chosen = jnp.where(lane == top_idx[:, choice : choice + 1] + 2, 1.0, chosen)
    late[:, width:] = chosen.astype(BF16)
    late_ring = ring_rows(late, late_all, s4, r4, loc.at[4])
    settle(small_copies)
    big = spread("fsdp", size, mid, packed_all, s3, r3, loc.at[3], False)
    run(big)
    out_copies = spread("sp", SP, outw, out_mid, s2, r2, loc.at[2], False)
    run(out_copies)
    late_ring.start()
    ring.finish()
    late_ring.finish()
    settle(out_copies)
    settle(big)


def context_kernel(context, out_mid, context_all, out_all, s0, r0, s1, r1, s2, r2, loc):
    meet(True)
    me, core, level, up, down, far = places()
    size = lax.axis_size("fsdp")
    mine = lax.axis_index("fsdp")
    other = level * 2 + (1 - core)
    keep = pltpu.make_async_copy(out_mid, out_all.at[mine], loc.at[1])
    keep.start()
    sent, passed = [], []
    for step in range(1, size):
        peer = lax.rem(mine + step, size)
        sent.append(
            remote(
                out_mid.at[core], out_all.at[mine, core], s1.at[step], r1.at[step], fsdp=peer
            )
        )
        source = lax.rem(mine + size - step, size)
        passed.append(
            remote(
                out_all.at[source, core],
                out_all.at[source, core],
                s2.at[step],
                r2.at[step],
                sp=other,
            )
        )
    ring = ring_columns(context, context_all, s0, r0, loc.at[0])
    ring.start()
    run(sent)
    ring.finish()
    for copy, onward in zip(sent, passed):
        copy.wait_recv()
        onward.start()
    for copy in sent:
        copy.wait_send()
    settle(passed)
    keep.wait()


def gather_kernel(source, target, send, recv, local):
    meet(False)
    ring = ring_rows(source, target, send, recv, local)
    ring.start()
    ring.finish()


class Scatter:
    def __init__(self, blocks, other_sums, sums, near, far_parts, send, recv):
        me, core, level, up, down, far = places()
        other = level * 2 + (1 - core)
        self.blocks, self.other_sums, self.sums = blocks, other_sums, sums
        self.near, self.far_parts = near, far_parts
        self.core, self.level, self.up, self.down, self.far = core, level, up, down, far
        half = blocks.shape[1] // 2
        self.half = half
        up_id, down_id = up * 2 + core, down * 2 + core

        def go(src, dst, number, peer):
            return remote(src, dst, send.at[number], recv.at[number], sp=peer)

        order = (far, up, down, level)
        self.pair = [
            go(blocks.at[at * 2 + (1 - core)], other_sums.at[number], number, other)
            for number, at in enumerate(order)
        ]
        self.to_up = go(sums.at[0, pl.ds(0, half)], far_parts.at[0], 4, up_id)
        self.to_down = go(sums.at[0, pl.ds(half, half)], far_parts.at[1], 5, down_id)
        self.full_up = go(sums.at[1], near.at[0], 6, up_id)
        self.full_down = go(sums.at[2], near.at[1], 7, down_id)

    def start(self):
        run(self.pair)

    def both(self, number, at):
        mine = self.blocks[at * 2 + self.core].astype(F32)
        return mine + self.other_sums[number].astype(F32)

    def middle(self):
        self.pair[0].wait_recv()
        self.sums[0] = self.both(0, self.far).astype(BF16)
        self.to_up.start()
        self.to_down.start()

    def near_blocks(self):
        half = self.half
        self.pair[1].wait_recv()
        self.to_up.wait_recv()
        total = self.both(1, self.up)
        self.sums[1, :half] = (total[:half] + self.far_parts[0].astype(F32)).astype(BF16)
        self.sums[1, half:] = total[half:].astype(BF16)
        self.full_up.start()
        self.pair[2].wait_recv()
        self.to_down.wait_recv()
        total = self.both(2, self.down)
        self.sums[2, :half] = total[:half].astype(BF16)
        self.sums[2, half:] = (total[half:] + self.far_parts[1].astype(F32)).astype(BF16)
        self.full_down.start()

    def end(self, out):
        self.pair[3].wait_recv()
        total = self.both(3, self.level)
        self.full_up.wait_recv()
        total = total + self.near[0].astype(F32)
        self.full_down.wait_recv()
        out[...] = total + self.near[1].astype(F32)
        for copy in self.pair + [self.to_up, self.to_down, self.full_up, self.full_down]:
            copy.wait_send()

    def finish(self, out):
        self.middle()
        self.near_blocks()
        self.end(out)


def scatter_scratch(rows, width):
    return [
        pltpu.VMEM((4, rows, width), BF16),
        pltpu.VMEM((3, rows, width), BF16),
        pltpu.VMEM((2, rows, width), BF16),
        pltpu.VMEM((2, rows // 2, width), BF16),
        DMA((8,)),
        DMA((8,)),
    ]


def experts_kernel(
    normed, late, small, weights,
    mixed, gates, out, grads,
    w_buf, acts, grad_acts, grad_results, blocks,
    other_sums, sums, near, far_parts, send, recv, loads,
):
    experts, width, both_span = weights.shape
    in_span = 2 * both_span // 3
    hidden = both_span - in_span
    copies = [
        pltpu.make_async_copy(weights.at[local], w_buf.at[local], loads.at[local])
        for local in range(experts)
    ]
    run(copies)
    meet(False)
    sp_index = lax.axis_index("sp")
    settle(copies)
    chunk = 256

    def tokens_block(index, carry):
        at = pl.ds(pl.multiple_of(index * chunk, chunk), chunk)
        rows = normed[at, :]
        logits = dot(rows, small[...], ((1,), (0,)))
        lane = lax.broadcasted_iota(jnp.int32, logits.shape, 1)
        shown = jnp.where(late[at, width:].astype(F32) > 0, logits, -jnp.inf)
        expo = jnp.exp(shown - jnp.max(shown, -1, keepdims=True))
        gate_rows = expo / jnp.sum(expo, -1, keepdims=True)
        gates[at, :] = gate_rows
        grad_mixed = RESIDUAL * late[at, :width].astype(F32)
        mix = jnp.zeros((chunk, width), F32)
        back = jnp.zeros((chunk, width), F32)
        extra = jnp.zeros((chunk, 128), F32)
        for local in range(experts):
            expert = lane == sp_index * experts + local + 2
            gate = jnp.sum(jnp.where(expert, gate_rows, 0.0), -1, keepdims=True)
            pre_act = dot(rows, w_buf[local, :, :in_span], ((1,), (0,)))
            gate_part, up_part = pre_act[:, :hidden], pre_act[:, hidden:]
            sigmoid = 1.0 / (1.0 + jnp.exp(-gate_part))
            silu = gate_part * sigmoid
            act = (silu * up_part).astype(BF16)
            acts[local, at, :] = act
            produced = dot(act, w_buf[local, :, in_span:], ((1,), (1,))).astype(BF16).astype(F32)
            mix = mix + gate * produced
            grad_gate = jnp.sum(grad_mixed * produced, -1, keepdims=True)
            extra = extra + jnp.where(expert, gate * grad_gate, 0.0)
            grad_result = (gate * grad_mixed).astype(BF16)
            grad_results[local, at, :] = grad_result
            grad_act = dot(grad_result, w_buf[local, :, in_span:], ((1,), (0,)))
            grad_gate_part = grad_act * up_part * sigmoid * (1.0 + gate_part * (1.0 - sigmoid))
            grad_pre = jnp.concatenate([grad_gate_part, grad_act * silu], 1).astype(BF16)
            grad_acts[local, at, :] = grad_pre
            back = back + dot(grad_pre, w_buf[local, :, :in_span], ((1,), (1,)))
        mixed[at, :] = mix.astype(BF16)
        per_block = blocks.shape[1]
        count = chunk // per_block
        for piece in range(count):
            place = slice(piece * per_block, (piece + 1) * per_block)
            blocks[index * count + piece, :, :width] = back[place].astype(BF16)
            blocks[index * count + piece, :, width:] = extra[place].astype(BF16)
        return carry

    lax.fori_loop(0, normed.shape[0] // chunk, tokens_block, 0)
    scatter = Scatter(blocks, other_sums, sums, near, far_parts, send, recv)
    scatter.start()
    owners = grads.shape[0]
    share = width // owners
    tile = 256
    count = tile // share

    def weight_tile(index, carry):
        columns = pl.ds(pl.multiple_of(index * tile, tile), tile)
        turned = normed[:, columns]
        for local in range(experts):
            value = dot(turned, grad_acts[local], ((0,), (0,))).astype(BF16)
            grads[pl.ds(index * count, count), local, :, :in_span] = value.reshape(
                count, share, in_span
            )
            value = dot(grad_results[local, :, columns], acts[local], ((0,), (0,))).astype(BF16)
            grads[pl.ds(index * count, count), local, :, in_span:] = value.reshape(
                count, share, hidden
            )
        return carry

    tiles = width // tile
    lax.fori_loop(0, tiles // 4, weight_tile, 0)
    scatter.middle()
    lax.fori_loop(tiles // 4, tiles // 2, weight_tile, 0)
    scatter.near_blocks()
    lax.fori_loop(tiles // 2, tiles, weight_tile, 0)
    scatter.end(out)


class Quad:
    def __init__(self, axis, source, far_parts, near, sums, send, recv):
        mine = lax.axis_index("fsdp")
        y, x = mine // 4, lax.rem(mine, 4)
        here = x if axis == "x" else y
        self.source, self.far_parts, self.near, self.sums = source, far_parts, near, sums
        self.here = here
        self.up, self.down, self.far = (lax.rem(here + step, 4) for step in (1, 3, 2))

        def device(place):
            return y * 4 + place if axis == "x" else place * 4 + x

        def go(src, dst, number, place):
            return remote(src, dst, send.at[number], recv.at[number], fsdp=device(place))

        self.far_up = go(source(self.far, 0), far_parts.at[0], 0, self.up)
        self.far_down = go(source(self.far, 1), far_parts.at[1], 1, self.down)
        self.plain_up = go(source(self.up, 1), near.at[0, 1], 2, self.up)
        self.plain_down = go(source(self.down, 0), near.at[1, 0], 3, self.down)
        self.sum_up = go(sums.at[0], near.at[0, 0], 4, self.up)
        self.sum_down = go(sums.at[1], near.at[1, 1], 5, self.down)

    def start(self):
        run((self.far_up, self.far_down, self.plain_up, self.plain_down))

    def near_blocks(self):
        self.far_up.wait_recv()
        total = self.source(self.up, 0)[...].astype(F32) + self.far_parts[0].astype(F32)
        self.sums[0] = total.astype(BF16)
        self.sum_up.start()
        self.far_down.wait_recv()
        total = self.source(self.down, 1)[...].astype(F32) + self.far_parts[1].astype(F32)
        self.sums[1] = total.astype(BF16)
        self.sum_down.start()

    def end(self, store):
        for copy in (self.plain_up, self.plain_down, self.sum_up, self.sum_down):
            copy.wait_recv()
        for side in range(2):
            total = self.source(self.here, side)[...].astype(F32)
            total = total + self.near[0, side].astype(F32) + self.near[1, side].astype(F32)
            store(side, total)
        for copy in (
            self.far_up, self.far_down, self.plain_up, self.plain_down, self.sum_up, self.sum_down
        ):
            copy.wait_send()


def quad_scratch(shape):
    return [
        pltpu.VMEM((2,) + shape, BF16),
        pltpu.VMEM((2, 2) + shape, BF16),
        pltpu.VMEM((2,) + shape, BF16),
        DMA((6,)),
        DMA((6,)),
    ]


def exact_dot(left, right, contract):
    return lax.dot_general(
        left, right, (contract, ((), ())), precision=lax.Precision.HIGHEST,
        preferred_element_type=F32,
    )


def back_kernel(
    back, gates, normed, middle, cotangent, gain, small, out_own, context,
    query, key2, value2, sums, cosine, sine, seg_column, seg_row, qkv_own, normed_one,
    grads, mixed,
    grad_middle, grad_normed_one, bundle_all, out_sum, expert_grads, mixed_own,
    attended, attended_all, grad_context, grad_proj, grad_key, grad_value, blocks, small_part,
    bundle, outp, bundle_in, out_in, bundle_sum, halves_a, halves_b,
    *scratch,
):
    scratch = list(scratch)

    def take(count):
        taken = scratch[:count]
        del scratch[:count]
        return taken

    mix_scatter = Scatter(mixed, *take(6))
    scatter = Scatter(blocks, *take(6))

    def half_a(index, side):
        return grads.at[:, index, 0, pl.ds(side * half, half)]

    def half_b(index, side):
        return grads.at[index, :, 1, pl.ds(side * half, half)]

    half = grads.shape[3] // 2
    first_a = Quad("x", half_a, *take(5))
    first_b = Quad("y", half_b, *take(5))
    second_a = Quad("y", lambda index, side: halves_a.at[side, index], *take(5))
    second_b = Quad("x", lambda index, side: halves_b.at[side, index], *take(5))
    ring_send, ring_recv, s1, r1, s2, r2, s3, r3, loc = take(9)

    def keep_a(side, total):
        halves_a[side] = total.astype(BF16)

    def keep_b(side, total):
        halves_b[side] = total.astype(BF16)

    meet(True)
    size = lax.axis_size("fsdp")
    first_a.start()
    first_b.start()
    width = cotangent.shape[1]
    value = middle[...]
    inverse = inverse_rms(value)
    weighted = back[:, width:]
    grad_logits = weighted - gates[...] * jnp.sum(weighted, -1, keepdims=True)
    grad_normed = back[:, :width] + exact_dot(grad_logits, small[...].astype(F32), ((1,), (1,)))
    grad_rows = cotangent[...].astype(F32) + rms_backward(grad_normed, value, inverse, gain[...])
    grad_middle[...] = grad_rows
    attended[...] = (RESIDUAL * grad_rows).astype(BF16)
    ring = ring_rows(attended, attended_all, ring_send, ring_recv, loc.at[0])
    ring.start()
    gain_lane = lax.broadcasted_iota(jnp.int32, grad_logits.shape, 1) == 1
    small_part[...] = exact_dot(normed[...].astype(F32), grad_logits, ((0,), (0,))) + exact_dot(
        grad_normed * value * inverse, gain_lane.astype(F32), ((0,), (0,))
    )
    ring.finish()
    mix_scatter.start()
    first_a.near_blocks()
    first_b.near_blocks()
    rows = attended.shape[0]
    for index in range(SP):
        at = slice(index * rows, (index + 1) * rows)
        grad_context[at, :] = dot(attended_all[index], out_own[...], ((1,), (1,))).astype(BF16)
    out_part = jnp.zeros((context.shape[1], width), F32)
    for index in range(SP):
        at = slice(index * rows, (index + 1) * rows)
        out_part = out_part + dot(context[at, :], attended_all[index], ((0,), (0,)))
    outp[...] = out_part.astype(BF16).reshape(outp.shape)
    outs = spread("fsdp", size, outp, out_in, s2, r2, loc.at[1], True)
    run(outs)
    mix_scatter.middle()
    attention_back_kernel(
        query, key2, value2, sums, grad_context, cosine, sine, seg_column, seg_row,
        grad_proj, grad_key, grad_value,
    )
    mix_scatter.near_blocks()
    span = grad_proj.shape[1]
    share = bundle.shape[1]
    tile = 256
    for index in range(width // tile):
        at = slice(index * tile, (index + 1) * tile)
        part = dot(normed_one[:, at], grad_proj[...], ((0,), (0,))).astype(BF16)
        place = slice(index * tile // share, (index + 1) * tile // share)
        bundle[place, :, :span] = part.reshape(tile // share, share, span)
        bundle[place, :, span:] = small_part[at, :].astype(BF16).reshape(tile // share, share, 128)
    bundles = spread("fsdp", size, bundle, bundle_in, s1, r1, loc.at[2], True)
    run(bundles)
    for index in range(SP):
        at = slice(index * rows, (index + 1) * rows)
        blocks[index] = dot(grad_proj[at, :], qkv_own[...], ((1,), (1,))).astype(BF16)
    scatter.start()
    first_a.end(keep_a)
    first_b.end(keep_b)
    second_a.start()
    second_b.start()
    scatter.middle()
    mix_scatter.end(mixed_own)
    scatter.near_blocks()
    settle(bundles)
    total = bundle_in[0].astype(F32)
    for index in range(1, size):
        total = total + bundle_in[index].astype(F32)
    bundle_sum[...] = total.reshape(bundle_sum.shape)
    shares = spread("sp", SP, bundle_sum, bundle_all, s3, r3, loc.at[3], True)
    run(shares)
    second_a.near_blocks()
    second_b.near_blocks()
    settle(outs)
    total = out_in[0].astype(F32)
    for index in range(1, size):
        total = total + out_in[index].astype(F32)
    out_sum[...] = total

    def store_a(side, total):
        expert_grads[0, side * half : (side + 1) * half, :] = total

    def store_b(side, total):
        expert_grads[1, side * half : (side + 1) * half, :] = total

    second_a.end(store_a)
    second_b.end(store_b)
    scatter.end(grad_normed_one)
    settle(shares)


def wide_call(kernel, name, number, inputs, in_specs, outs, out_specs, scratch):
    return pl.pallas_call(
        kernel,
        name=name,
        out_shape=outs,
        in_specs=in_specs,
        out_specs=out_specs,
        scratch_shapes=scratch,
        cost_estimate=pl.CostEstimate(
            flops=2 * 10**10, bytes_accessed=2 * 10**7, transcendentals=0
        ),
        compiler_params=pltpu.CompilerParams(
            collective_id=number, has_side_effects=True, vmem_limit_bytes=56 * 2**20
        ),
    )(*inputs)


def local_call(kernel, name, inputs, outs, scratch=(), flops=0):
    moved = sum(array.size * array.dtype.itemsize for array in inputs)
    return pl.pallas_call(
        kernel,
        name=name,
        out_shape=outs,
        in_specs=[VMEM] * len(inputs),
        out_specs=jax.tree.map(lambda _: VMEM, outs),
        scratch_shapes=scratch,
        cost_estimate=pl.CostEstimate(flops=flops, bytes_accessed=moved, transcendentals=0),
        compiler_params=pltpu.CompilerParams(vmem_limit_bytes=48 * 2**20),
    )(*inputs)


def swap_halves(value):
    wide = value.shape[-1]
    lane = lax.broadcasted_iota(jnp.int32, value.shape, 1)
    return jnp.where(
        lane % HEAD_SIZE < HEAD_SIZE // 2,
        pltpu.roll(value, wide - HEAD_SIZE // 2, 1),
        pltpu.roll(value, HEAD_SIZE // 2, 1),
    )


def first_head(shape):
    return lax.broadcasted_iota(jnp.int32, shape, 1) < HEAD_SIZE


def stack_heads(slab):
    is_first = first_head(slab.shape)
    zero = jnp.zeros_like(slab)
    return jnp.concatenate([jnp.where(is_first, slab, zero), jnp.where(is_first, zero, slab)], 0)


def merge_heads(stacked):
    half = stacked.shape[0] // 2
    return jnp.where(first_head((half, stacked.shape[1])), stacked[:half], stacked[half:])


def block_scores(block, query2, key2, seg_column, seg_row):
    lo, hi = block * BLOCK, (block + 1) * BLOCK
    k_lo = max(0, lo - LONGEST)
    rows = lo + lax.broadcasted_iota(jnp.int32, (BLOCK, hi - k_lo), 0)
    keys = k_lo + lax.broadcasted_iota(jnp.int32, (BLOCK, hi - k_lo), 1)
    allowed = (keys <= rows) & (seg_column[lo:hi, :] == seg_row[:, k_lo:hi])
    scores = dot(query2, key2[k_lo:hi, :], ((1,), (1,))) * HEAD_SIZE**-0.5
    return jnp.where(jnp.concatenate([allowed, allowed], 0), scores, -jnp.inf)


def attention_kernel(
    proj, cosine, sine, seg_column, seg_row, context, query, key2, value2, sums
):
    cos_rows, sin_rows = cosine[...], sine[...]
    slab = proj[:, :128]
    query[...] = (slab * cos_rows + swap_halves(slab) * sin_rows).astype(BF16)
    slab = proj[:, 128:]
    is_first = first_head(slab.shape)
    turned = slab * cos_rows + swap_halves(slab) * sin_rows
    key2[...] = jnp.where(is_first, turned, pltpu.roll(turned, HEAD_SIZE, 1)).astype(BF16)
    value2[...] = jnp.where(is_first, pltpu.roll(slab, HEAD_SIZE, 1), slab).astype(BF16)
    for block in range(proj.shape[0] // BLOCK):
        lo, hi = block * BLOCK, (block + 1) * BLOCK
        k_lo = max(0, lo - LONGEST)
        scores = block_scores(block, stack_heads(query[lo:hi, :]), key2, seg_column, seg_row)
        top = jnp.max(scores, -1, keepdims=True)
        expo = jnp.exp(scores - top)
        total = jnp.sum(expo, -1, keepdims=True)
        probs = (expo / total).astype(BF16)
        context[lo:hi, :] = merge_heads(dot(probs, value2[k_lo:hi, :], ((1,), (0,)))).astype(BF16)
        sums[block] = jnp.broadcast_to(top + jnp.log(total), (2 * BLOCK, 128))


def attention_back_kernel(
    query, key2, value2, sums, grad_context, cosine, sine, seg_column, seg_row,
    grad_proj, grad_key, grad_value,
):
    grad_key[...] = jnp.zeros_like(grad_key)
    grad_value[...] = jnp.zeros_like(grad_value)
    for block in range(query.shape[0] // BLOCK):
        lo, hi = block * BLOCK, (block + 1) * BLOCK
        k_lo = max(0, lo - LONGEST)
        query2 = stack_heads(query[lo:hi, :])
        scores = block_scores(block, query2, key2, seg_column, seg_row)
        probs = jnp.exp(scores - sums[block][:, :1])
        grad_rows = stack_heads(grad_context[lo:hi, :])
        grad_probs = dot(grad_rows, value2[k_lo:hi, :], ((1,), (1,)))
        row_dot = jnp.sum(grad_probs * probs, -1, keepdims=True)
        grad_scores = (probs * (grad_probs - row_dot) * HEAD_SIZE**-0.5).astype(BF16)
        moved = merge_heads(dot(grad_scores, key2[k_lo:hi, :], ((1,), (0,))))
        moved = moved.astype(BF16).astype(F32)
        grad_proj[lo:hi, :128] = (
            moved * cosine[lo:hi, :] - swap_halves(moved) * sine[lo:hi, :]
        ).astype(BF16)
        grad_key[k_lo:hi, :] += dot(grad_scores, query2, ((0,), (0,)))
        grad_value[k_lo:hi, :] += dot(probs.astype(BF16), grad_rows, ((0,), (0,)))
    is_first = first_head(grad_key.shape)
    moved = grad_key[...]
    moved = (moved + pltpu.roll(moved, HEAD_SIZE, 1)).astype(BF16).astype(F32)
    moved = moved * cosine[...] - swap_halves(moved) * sine[...]
    other = grad_value[...]
    other = other + pltpu.roll(other, HEAD_SIZE, 1)
    grad_proj[:, 128:] = jnp.where(is_first, moved, other).astype(BF16)


def shards(
    tokens,
    segments,
    top_idx,
    cotangent,
    norm1_gain,
    qkv_weight,
    out_weight,
    norm2_gain,
    router_weight,
    expert_in,
    expert_out,
):
    n_sp = lax.axis_size("sp")
    n_fsdp = lax.axis_size("fsdp")
    sp_index = lax.axis_index("sp")
    rows, width = tokens.shape
    seq_len = rows * n_sp
    weight_rows = qkv_weight.shape[0]
    hidden = expert_out.shape[2]
    q_span, k_span = HQ * HEAD_SIZE, KEY_VALUE_HEADS * HEAD_SIZE
    group = q_span // n_sp
    head = k_span // n_sp
    segment_ids = segments[0]

    def own(array):
        return lax.dynamic_slice_in_dim(array, sp_index * rows, rows, 0)

    def sum_over(array, axis, count):
        parts = lax.all_to_all(array, axis, split_axis=0, concat_axis=0, tiled=True)
        return jnp.sum(parts.astype(F32), 0)

    small = jnp.concatenate([norm1_gain[:, None], norm2_gain[:, None], router_weight], 1)
    small = jnp.pad(small, ((0, 0), (0, 128 - small.shape[1])))
    pack_width = 2 * group + 128
    any_shape = jax.ShapeDtypeStruct
    tokens_all, late, _, packed, out_mid = wide_call(
        first_kernel,
        "first_gather",
        1,
        (tokens, cotangent, top_idx, qkv_weight, small, out_weight),
        [HBM, VMEM, VMEM, VMEM, VMEM, HBM],
        (
            any_shape((SP, rows, width), BF16),
            any_shape((SP, rows, width + 128), BF16),
            any_shape((SP, weight_rows, pack_width), BF16),
            any_shape((n_fsdp, SP, weight_rows, pack_width), BF16),
            any_shape((SP, weight_rows, width), BF16),
        ),
        [HBM] * 5,
        [pltpu.VMEM((SP, weight_rows, pack_width), BF16), pltpu.VMEM((rows, width + 128), BF16)]
        + [DMA((8,))] * 6
        + [DMA((n_fsdp,))] * 2
        + [DMA((8,))] * 2
        + [DMA((5,))],
    )
    packed = packed.reshape(width, pack_width)
    tokens_all = tokens_all.reshape(seq_len, width)
    late = late.reshape(seq_len, width + 128)
    experts = lax.all_gather(
        jnp.concatenate([expert_in, expert_out], 2), "fsdp", axis=1, tiled=True
    )

    qkv_own = packed[:, : 2 * group]
    small_own = packed[:, 2 * group :]
    small_all = small_own.astype(F32)
    gain_one, gain_two = small_all[:, 0][None, :], small_all[:, 1][None, :]

    hidden_in = tokens_all.astype(F32)
    inverse_one = inverse_rms(hidden_in)
    normed_one = (hidden_in * inverse_one * gain_one).astype(BF16)
    projected = dot(normed_one, qkv_own, ((1,), (0,)))
    cosine, sine = rope_tables(seq_len)
    seg_row, seg_column = segment_ids[None, :], segment_ids[:, None]
    context, query, key2, value2, sums = local_call(
        attention_kernel,
        "attention",
        (projected, cosine, sine, seg_column, seg_row),
        (
            any_shape((seq_len, 128), BF16),
            any_shape((seq_len, 128), BF16),
            any_shape((seq_len, 128), BF16),
            any_shape((seq_len, 128), BF16),
            any_shape((seq_len // BLOCK, 2 * BLOCK, 128), F32),
        ),
        flops=2 * 10**9,
    )
    context_all, out_full = wide_call(
        context_kernel,
        "context_gather",
        2,
        (context, out_mid.reshape(2, SP * weight_rows // 2, width)),
        [HBM] * 2,
        (
            any_shape((seq_len, width), BF16),
            any_shape((n_fsdp, 2, SP * weight_rows // 2, width), BF16),
        ),
        [HBM] * 2,
        [DMA((8,))] * 2 + [DMA((n_fsdp,))] * 4 + [DMA((2,))],
    )
    out_full = out_full.reshape(width, width)
    attended = dot(context_all, out_full, ((1,), (0,)))
    middle = hidden_in + RESIDUAL * attended
    inverse_two = inverse_rms(middle)
    normed_two = (middle * inverse_two * gain_two).astype(BF16)
    n_experts = expert_in.shape[0]
    in_span = expert_in.shape[2]
    mixed, gates, back, grads = wide_call(
        experts_kernel,
        "experts",
        3,
        (normed_two, late, small_own, experts),
        [VMEM, VMEM, VMEM, HBM],
        (
            any_shape((seq_len, width), BF16),
            any_shape((seq_len, 128), F32),
            any_shape((rows, width + 128), F32),
            any_shape((n_fsdp, n_experts, width // n_fsdp, in_span + hidden), BF16),
        ),
        (VMEM, VMEM, VMEM, VMEM),
        [
            pltpu.VMEM((n_experts, width, in_span + hidden), BF16),
            pltpu.VMEM((n_experts, seq_len, hidden), BF16),
            pltpu.VMEM((n_experts, seq_len, in_span), BF16),
            pltpu.VMEM((n_experts, seq_len, width), BF16),
            pltpu.VMEM((SP, rows, width + 128), BF16),
        ]
        + scatter_scratch(rows, width + 128)
        + [DMA((n_experts,))],
    )
    out_own = lax.dynamic_slice_in_dim(out_full, sp_index * group, group, 0)
    share = width // n_fsdp
    shares = group // n_fsdp
    half_grads = (4, share // 2, in_span + hidden)
    half_share = (share // 2, in_span + hidden)
    grad_middle, grad_normed_one, bundle, out_sum, expert_grads, mixed_own = wide_call(
        back_kernel,
        "backward",
        4,
        (
            back, own(gates), own(normed_two), own(middle), cotangent, gain_two, small_own, out_own,
            context, query, key2, value2, sums, cosine, sine, seg_column, seg_row, qkv_own,
            normed_one, grads.reshape(4, 4, n_experts, share, in_span + hidden),
            mixed.reshape(SP, rows, width),
        ),
        [VMEM] * 21,
        (
            any_shape((rows, width), F32),
            any_shape((rows, width), F32),
            any_shape((SP, weight_rows, pack_width), F32),
            any_shape((shares, width), F32),
            any_shape((n_experts, share, in_span + hidden), F32),
            any_shape((rows, width), F32),
        ),
        (VMEM,) * 6,
        [
            pltpu.VMEM((rows, width), BF16),
            pltpu.VMEM((SP, rows, width), BF16),
            pltpu.VMEM((seq_len, group), BF16),
            pltpu.VMEM((seq_len, 2 * group), BF16),
            pltpu.VMEM((seq_len, group), F32),
            pltpu.VMEM((seq_len, group), F32),
            pltpu.VMEM((SP, rows, width), BF16),
            pltpu.VMEM((width, 128), F32),
            pltpu.VMEM((n_fsdp, share, pack_width), BF16),
            pltpu.VMEM((n_fsdp, shares, width), BF16),
            pltpu.VMEM((n_fsdp, share, pack_width), BF16),
            pltpu.VMEM((n_fsdp, shares, width), BF16),
            pltpu.VMEM((SP, weight_rows, pack_width), F32),
            pltpu.VMEM((2,) + half_grads, BF16),
            pltpu.VMEM((2,) + half_grads, BF16),
        ]
        + scatter_scratch(rows, width) * 2
        + quad_scratch(half_grads) * 2
        + quad_scratch(half_share) * 2
        + [DMA((8,))] * 2
        + [DMA((n_fsdp,))] * 4
        + [DMA((8,))] * 2
        + [DMA((4,))],
    )
    block_out = own(middle) + RESIDUAL * mixed_own
    moves = []
    for f in range(n_fsdp):
        for s in range(n_sp):
            moves.append((f * n_sp + s, (s * group + f * shares) // weight_rows))
    if shares == weight_rows:
        out_grad = lax.ppermute(out_sum, ("fsdp", "sp"), moves)
    else:
        whole = lax.all_gather(out_sum, ("fsdp", "sp"), axis=0, tiled=False)
        whole = whole.reshape(n_fsdp, n_sp, shares, width).transpose(1, 0, 2, 3)
        device = lax.axis_index("fsdp") * n_sp + sp_index
        out_grad = lax.dynamic_slice_in_dim(
            whole.reshape(width, width), device * weight_rows, weight_rows, 0
        )

    qkv_grad = jnp.concatenate(
        [
            bundle[:, :, :group].transpose(1, 0, 2).reshape(weight_rows, q_span),
            bundle[:, :, group : group + head].transpose(1, 0, 2).reshape(weight_rows, k_span),
            bundle[:, :, group + head : 2 * group].transpose(1, 0, 2).reshape(weight_rows, k_span),
        ],
        1,
    )
    smalls = jnp.sum(bundle[:, :, 2 * group :], 0)
    gain_two_grad = smalls[:, 1]
    router_grad = smalls[:, 2 : 2 + E]
    gain_one_grad = jnp.sum(qkv_grad * qkv_weight.astype(F32), 1) / norm1_gain.astype(F32)
    hidden_own = tokens.astype(F32)
    input_grad = grad_middle + rms_backward(
        grad_normed_one, hidden_own, inverse_rms(hidden_own), gain_one
    )
    return (
        block_out,
        input_grad,
        gain_one_grad,
        qkv_grad,
        out_grad,
        gain_two_grad,
        router_grad,
        expert_grads[:, :, :in_span],
        expert_grads[:, :, in_span:],
    )


def solution(mesh):
    both = P(("fsdp", "sp"), None)
    flat = P(("fsdp", "sp"))
    expert = P("sp", "fsdp", None)
    return jax.shard_map(
        shards,
        mesh=mesh,
        in_specs=(both, P("fsdp", None), both, both, flat, both, both, flat, both, expert, expert),
        out_specs=(both, both, flat, both, both, flat, both, expert, expert),
        check_vma=False,
    )
```

```python
import jax
import jax.numpy as jnp
import numpy as np
from jax import lax
from jax.experimental import pallas as pl
from jax.experimental.pallas import tpu as pltpu
from jax.sharding import PartitionSpec as P

HQ = 16
KEY_VALUE_HEADS = 8
HEAD_SIZE = 64
E = 16
EPSILON = 1e-06
RESIDUAL = 0.22
BLOCK = 256
LONGEST = 512
BF16 = jnp.bfloat16
F32 = jnp.float32


def rope_tables(count):
    frequency = np.float32(10000.0) ** (
        np.float32(-2.0) * np.arange(HEAD_SIZE // 2, dtype=np.float32) / np.float32(HEAD_SIZE)
    )
    angles = np.arange(count, dtype=np.float32)[:, None] * frequency.astype(np.float32)[None, :]
    cosine = np.cos(angles).astype(np.float32)
    sine = np.sin(angles).astype(np.float32)
    return np.concatenate([cosine] * 4, 1), np.concatenate([-sine, sine] * 2, 1)


def dot(left, right, contract):
    return lax.dot_general(left, right, (contract, ((), ())), preferred_element_type=F32)


def inverse_rms(value):
    return lax.rsqrt(jnp.mean(value * value, -1, keepdims=True) + EPSILON)


def rms_backward(grad, value, inverse, gain):
    scaled = grad * gain
    return inverse * scaled - value * (inverse**3) * jnp.mean(scaled * value, -1, keepdims=True)


MESH = pl.DeviceIdType.MESH
VMEM = pl.BlockSpec(memory_space=pltpu.VMEM)
HBM = pl.BlockSpec(memory_space=pl.ANY)
DMA = pltpu.SemaphoreType.DMA
SP, FSDP = 8, 16


def remote(src, dst, send, recv, **device):
    return pltpu.make_async_remote_copy(
        src_ref=src,
        dst_ref=dst,
        send_sem=send,
        recv_sem=recv,
        device_id=device,
        device_id_type=MESH,
    )


def meet(with_fsdp):
    barrier = pltpu.get_barrier_semaphore()
    me = lax.axis_index("sp")
    for step in range(1, SP):
        pl.semaphore_signal(
            barrier, inc=1, device_id={"sp": lax.rem(me + step, SP)}, device_id_type=MESH
        )
    count = SP - 1
    if with_fsdp:
        size = lax.axis_size("fsdp")
        mine = lax.axis_index("fsdp")
        for step in range(1, size):
            pl.semaphore_signal(
                barrier, inc=1, device_id={"fsdp": lax.rem(mine + step, size)}, device_id_type=MESH
            )
        count += size - 1
    pl.semaphore_wait(barrier, count)


def places():
    me = lax.axis_index("sp")
    level, core = me // 2, lax.rem(me, 2)
    up = lax.rem(level + 1, 4)
    down = lax.rem(level + 3, 4)
    far = lax.rem(level + 2, 4)
    return me, core, level, up, down, far


class Ring:
    def __init__(self, source, slot, part, send, recv, local):
        me, core, level, up, down, far = places()
        self.me = me
        up_id, down_id, far_id = up * 2 + core, down * 2 + core, far * 2 + core
        other = level * 2 + (1 - core)

        def go(src, dst, number, peer):
            return remote(src, dst, send.at[number], recv.at[number], sp=peer)

        self.first = [
            go(source, slot(me), 0, up_id),
            go(source, slot(me), 1, down_id),
            go(source, slot(me), 2, other),
        ]
        self.local = pltpu.make_async_copy(source, slot(me), local)
        self.next_up = [
            go(part(down_id, 0), part(down_id, 0), 3, up_id),
            go(slot(down_id), slot(down_id), 4, other),
        ]
        self.next_down = [
            go(part(up_id, 1), part(up_id, 1), 5, down_id),
            go(slot(up_id), slot(up_id), 6, other),
        ]
        self.last = go(slot(far_id), slot(far_id), 7, other)

    def start(self):
        for copy in self.first:
            copy.start()
        self.local.start()

    def forward(self):
        self.first[0].wait_recv()
        for copy in self.next_up:
            copy.start()
        self.first[1].wait_recv()
        for copy in self.next_down:
            copy.start()

    def close(self):
        self.next_up[0].wait_recv()
        self.next_down[0].wait_recv()
        self.last.start()
        self.local.wait()
        for copy in (self.first[0], self.first[1], self.next_up[0], self.next_down[0]):
            copy.wait_send()
        for copy in (self.first[2], self.next_up[1], self.next_down[1], self.last):
            copy.wait()

    def finish(self):
        self.forward()
        self.close()


def ring_rows(source, target, send, recv, local):
    half = source.shape[0] // 2
    return Ring(
        source,
        lambda index: target.at[index],
        lambda index, side: target.at[index, pl.ds(side * half, half)],
        send,
        recv,
        local,
    )


def ring_columns(source, target, send, recv, local):
    rows, wide = source.shape
    half = rows // 2

    def columns(index):
        return pl.ds(pl.multiple_of(index * wide, wide), wide)

    return Ring(
        source,
        lambda index: target.at[:, columns(index)],
        lambda index, side: target.at[pl.ds(side * half, half), columns(index)],
        send,
        recv,
        local,
    )


def spread(axis, size, source, target, send, recv, local, blocks, place=None):
    me = lax.axis_index(axis)
    landing = target.at[me] if place is None else place(me)
    copies = []
    for step in range(1, size):
        peer = lax.rem(me + step, size)
        copies.append(
            remote(
                source.at[peer] if blocks else source,
                landing,
                send.at[step],
                recv.at[step],
                **{axis: peer},
            )
        )
    copies.append(pltpu.make_async_copy(source.at[me] if blocks else source, landing, local))
    return copies


def run(copies):
    for copy in copies:
        copy.start()


def settle(copies):
    for copy in copies:
        copy.wait()


class Scatter:
    def __init__(self, blocks, other_sums, sums, near, far_parts, send, recv):
        me, core, level, up, down, far = places()
        other = level * 2 + (1 - core)
        self.blocks, self.other_sums, self.sums = blocks, other_sums, sums
        self.near, self.far_parts = near, far_parts
        self.core, self.level, self.up, self.down, self.far = core, level, up, down, far
        half = blocks.shape[1] // 2
        self.half = half
        up_id, down_id = up * 2 + core, down * 2 + core

        def go(src, dst, number, peer):
            return remote(src, dst, send.at[number], recv.at[number], sp=peer)

        order = (far, up, down, level)
        self.pair = [
            go(blocks.at[at * 2 + (1 - core)], other_sums.at[number], number, other)
            for number, at in enumerate(order)
        ]
        self.to_up = go(sums.at[0, pl.ds(0, half)], far_parts.at[0], 4, up_id)
        self.to_down = go(sums.at[0, pl.ds(half, half)], far_parts.at[1], 5, down_id)
        self.full_up = go(sums.at[1], near.at[0], 6, up_id)
        self.full_down = go(sums.at[2], near.at[1], 7, down_id)

    def start(self):
        run(self.pair)

    def both(self, number, at):
        mine = self.blocks[at * 2 + self.core].astype(F32)
        return mine + self.other_sums[number].astype(F32)

    def middle(self):
        self.pair[0].wait_recv()
        self.sums[0] = self.both(0, self.far).astype(BF16)
        self.to_up.start()
        self.to_down.start()

    def near_blocks(self):
        half = self.half
        self.pair[1].wait_recv()
        self.to_up.wait_recv()
        total = self.both(1, self.up)
        self.sums[1, :half] = (total[:half] + self.far_parts[0].astype(F32)).astype(BF16)
        self.sums[1, half:] = total[half:].astype(BF16)
        self.full_up.start()
        self.pair[2].wait_recv()
        self.to_down.wait_recv()
        total = self.both(2, self.down)
        self.sums[2, :half] = total[:half].astype(BF16)
        self.sums[2, half:] = (total[half:] + self.far_parts[1].astype(F32)).astype(BF16)
        self.full_down.start()

    def end(self, out):
        self.pair[3].wait_recv()
        total = self.both(3, self.level)
        self.full_up.wait_recv()
        total = total + self.near[0].astype(F32)
        self.full_down.wait_recv()
        out[...] = total + self.near[1].astype(F32)
        for copy in self.pair + [self.to_up, self.to_down, self.full_up, self.full_down]:
            copy.wait_send()

    def finish(self, out):
        self.middle()
        self.near_blocks()
        self.end(out)


def scatter_scratch(rows, width):
    return [
        pltpu.VMEM((4, rows, width), BF16),
        pltpu.VMEM((3, rows, width), BF16),
        pltpu.VMEM((2, rows, width), BF16),
        pltpu.VMEM((2, rows // 2, width), BF16),
        DMA((8,)),
        DMA((8,)),
    ]


class Quad:
    def __init__(self, axis, source, far_parts, near, sums, send, recv):
        mine = lax.axis_index("fsdp")
        y, x = mine // 4, lax.rem(mine, 4)
        here = x if axis == "x" else y
        self.source, self.far_parts, self.near, self.sums = source, far_parts, near, sums
        self.here = here
        self.up, self.down, self.far = (lax.rem(here + step, 4) for step in (1, 3, 2))

        def device(place):
            return y * 4 + place if axis == "x" else place * 4 + x

        def go(src, dst, number, place):
            return remote(src, dst, send.at[number], recv.at[number], fsdp=device(place))

        self.far_up = go(source(self.far, 0), far_parts.at[0], 0, self.up)
        self.far_down = go(source(self.far, 1), far_parts.at[1], 1, self.down)
        self.plain_up = go(source(self.up, 1), near.at[0, 1], 2, self.up)
        self.plain_down = go(source(self.down, 0), near.at[1, 0], 3, self.down)
        self.sum_up = go(sums.at[0], near.at[0, 0], 4, self.up)
        self.sum_down = go(sums.at[1], near.at[1, 1], 5, self.down)

    def start(self):
        run((self.far_up, self.far_down, self.plain_up, self.plain_down))

    def near_blocks(self):
        self.far_up.wait_recv()
        total = self.source(self.up, 0)[...].astype(F32) + self.far_parts[0].astype(F32)
        self.sums[0] = total.astype(BF16)
        self.sum_up.start()
        self.far_down.wait_recv()
        total = self.source(self.down, 1)[...].astype(F32) + self.far_parts[1].astype(F32)
        self.sums[1] = total.astype(BF16)
        self.sum_down.start()

    def end(self, store):
        for copy in (self.plain_up, self.plain_down, self.sum_up, self.sum_down):
            copy.wait_recv()
        for side in range(2):
            total = self.source(self.here, side)[...].astype(F32)
            total = total + self.near[0, side].astype(F32) + self.near[1, side].astype(F32)
            store(side, total)
        for copy in (
            self.far_up, self.far_down, self.plain_up, self.plain_down, self.sum_up, self.sum_down
        ):
            copy.wait_send()


def quad_scratch(shape):
    return [
        pltpu.VMEM((2,) + shape, BF16),
        pltpu.VMEM((2, 2) + shape, BF16),
        pltpu.VMEM((2,) + shape, BF16),
        DMA((6,)),
        DMA((6,)),
    ]


def exact_dot(left, right, contract):
    return lax.dot_general(
        left, right, (contract, ((), ())), precision=lax.Precision.HIGHEST,
        preferred_element_type=F32,
    )


def back_kernel(
    back, gates, normed, middle, cotangent, gain, small, out_own, context,
    query, key2, value2, sums, cosine, sine, seg_column, seg_row, qkv_own, normed_one,
    grads, mixed,
    grad_middle, grad_normed_one, bundle_all, out_sum, expert_grads, mixed_own,
    attended, attended_all, grad_context, grad_proj, grad_key, grad_value, blocks, small_part,
    bundle, outp, bundle_in, out_in, bundle_sum, halves_a, halves_b,
    *scratch,
):
    scratch = list(scratch)

    def take(count):
        taken = scratch[:count]
        del scratch[:count]
        return taken

    mix_scatter = Scatter(mixed, *take(6))
    scatter = Scatter(blocks, *take(6))

    def half_a(index, side):
        return grads.at[:, index, 0, pl.ds(side * half, half)]

    def half_b(index, side):
        return grads.at[index, :, 1, pl.ds(side * half, half)]

    half = grads.shape[3] // 2
    first_a = Quad("x", half_a, *take(5))
    first_b = Quad("y", half_b, *take(5))
    second_a = Quad("y", lambda index, side: halves_a.at[side, index], *take(5))
    second_b = Quad("x", lambda index, side: halves_b.at[side, index], *take(5))
    ring_send, ring_recv, s1, r1, s2, r2, s3, r3, loc = take(9)

    def keep_a(side, total):
        halves_a[side] = total.astype(BF16)

    def keep_b(side, total):
        halves_b[side] = total.astype(BF16)

    meet(True)
    size = lax.axis_size("fsdp")
    first_a.start()
    first_b.start()
    width = cotangent.shape[1]
    value = middle[...]
    inverse = inverse_rms(value)
    weighted = back[:, width:]
    grad_logits = weighted - gates[...] * jnp.sum(weighted, -1, keepdims=True)
    grad_normed = back[:, :width] + exact_dot(grad_logits, small[...].astype(F32), ((1,), (1,)))
    grad_rows = cotangent[...].astype(F32) + rms_backward(grad_normed, value, inverse, gain[...])
    grad_middle[...] = grad_rows
    attended[...] = (RESIDUAL * grad_rows).astype(BF16)
    ring = ring_rows(attended, attended_all, ring_send, ring_recv, loc.at[0])
    ring.start()
    gain_lane = lax.broadcasted_iota(jnp.int32, grad_logits.shape, 1) == 1
    small_part[...] = exact_dot(normed[...].astype(F32), grad_logits, ((0,), (0,))) + exact_dot(
        grad_normed * value * inverse, gain_lane.astype(F32), ((0,), (0,))
    )
    ring.finish()
    mix_scatter.start()
    first_a.near_blocks()
    first_b.near_blocks()
    rows = attended.shape[0]
    for index in range(SP):
        at = slice(index * rows, (index + 1) * rows)
        grad_context[at, :] = dot(attended_all[index], out_own[...], ((1,), (1,))).astype(BF16)
    out_part = jnp.zeros((context.shape[1], width), F32)
    for index in range(SP):
        at = slice(index * rows, (index + 1) * rows)
        out_part = out_part + dot(context[at, :], attended_all[index], ((0,), (0,)))
    outp[...] = out_part.astype(BF16).reshape(outp.shape)
    outs = spread("fsdp", size, outp, out_in, s2, r2, loc.at[1], True)
    run(outs)
    mix_scatter.middle()
    attention_back_kernel(
        query, key2, value2, sums, grad_context, cosine, sine, seg_column, seg_row,
        grad_proj, grad_key, grad_value,
    )
    mix_scatter.near_blocks()
    span = grad_proj.shape[1]
    share = bundle.shape[1]
    tile = 256
    for index in range(width // tile):
        at = slice(index * tile, (index + 1) * tile)
        part = dot(normed_one[:, at], grad_proj[...], ((0,), (0,))).astype(BF16)
        place = slice(index * tile // share, (index + 1) * tile // share)
        bundle[place, :, :span] = part.reshape(tile // share, share, span)
        bundle[place, :, span:] = small_part[at, :].astype(BF16).reshape(tile // share, share, 128)
    bundles = spread("fsdp", size, bundle, bundle_in, s1, r1, loc.at[2], True)
    run(bundles)
    for index in range(SP):
        at = slice(index * rows, (index + 1) * rows)
        blocks[index] = dot(grad_proj[at, :], qkv_own[...], ((1,), (1,))).astype(BF16)
    scatter.start()
    first_a.end(keep_a)
    first_b.end(keep_b)
    second_a.start()
    second_b.start()
    scatter.middle()
    mix_scatter.end(mixed_own)
    scatter.near_blocks()
    settle(bundles)
    total = bundle_in[0].astype(F32)
    for index in range(1, size):
        total = total + bundle_in[index].astype(F32)
    bundle_sum[...] = total.reshape(bundle_sum.shape)
    shares = spread("sp", SP, bundle_sum, bundle_all, s3, r3, loc.at[3], True)
    run(shares)
    second_a.near_blocks()
    second_b.near_blocks()
    settle(outs)
    total = out_in[0].astype(F32)
    for index in range(1, size):
        total = total + out_in[index].astype(F32)
    out_sum[...] = total

    def store_a(side, total):
        expert_grads[0, side * half : (side + 1) * half, :] = total

    def store_b(side, total):
        expert_grads[1, side * half : (side + 1) * half, :] = total

    second_a.end(store_a)
    second_b.end(store_b)
    scatter.end(grad_normed_one)
    settle(shares)


def swap_halves(value):
    wide = value.shape[-1]
    lane = lax.broadcasted_iota(jnp.int32, value.shape, 1)
    return jnp.where(
        lane % HEAD_SIZE < HEAD_SIZE // 2,
        pltpu.roll(value, wide - HEAD_SIZE // 2, 1),
        pltpu.roll(value, HEAD_SIZE // 2, 1),
    )


def first_head(shape):
    return lax.broadcasted_iota(jnp.int32, shape, 1) < HEAD_SIZE


def stack_heads(slab):
    is_first = first_head(slab.shape)
    zero = jnp.zeros_like(slab)
    return jnp.concatenate([jnp.where(is_first, slab, zero), jnp.where(is_first, zero, slab)], 0)


def merge_heads(stacked):
    half = stacked.shape[0] // 2
    return jnp.where(first_head((half, stacked.shape[1])), stacked[:half], stacked[half:])


def block_scores(block, query2, key2, seg_column, seg_row):
    lo, hi = block * BLOCK, (block + 1) * BLOCK
    k_lo = max(0, lo - LONGEST)
    rows = lo + lax.broadcasted_iota(jnp.int32, (BLOCK, hi - k_lo), 0)
    keys = k_lo + lax.broadcasted_iota(jnp.int32, (BLOCK, hi - k_lo), 1)
    allowed = (keys <= rows) & (seg_column[lo:hi, :] == seg_row[:, k_lo:hi])
    scores = dot(query2, key2[k_lo:hi, :], ((1,), (1,))) * HEAD_SIZE**-0.5
    return jnp.where(jnp.concatenate([allowed, allowed], 0), scores, -jnp.inf)


def attention_kernel(
    proj, cosine, sine, seg_column, seg_row, context, query, key2, value2, sums
):
    cos_rows, sin_rows = cosine[...], sine[...]
    slab = proj[:, :128]
    query[...] = (slab * cos_rows + swap_halves(slab) * sin_rows).astype(BF16)
    slab = proj[:, 128:]
    is_first = first_head(slab.shape)
    turned = slab * cos_rows + swap_halves(slab) * sin_rows
    key2[...] = jnp.where(is_first, turned, pltpu.roll(turned, HEAD_SIZE, 1)).astype(BF16)
    value2[...] = jnp.where(is_first, pltpu.roll(slab, HEAD_SIZE, 1), slab).astype(BF16)
    for block in range(proj.shape[0] // BLOCK):
        lo, hi = block * BLOCK, (block + 1) * BLOCK
        k_lo = max(0, lo - LONGEST)
        scores = block_scores(block, stack_heads(query[lo:hi, :]), key2, seg_column, seg_row)
        top = jnp.max(scores, -1, keepdims=True)
        expo = jnp.exp(scores - top)
        total = jnp.sum(expo, -1, keepdims=True)
        probs = (expo / total).astype(BF16)
        context[lo:hi, :] = merge_heads(dot(probs, value2[k_lo:hi, :], ((1,), (0,)))).astype(BF16)
        sums[block] = jnp.broadcast_to(top + jnp.log(total), (2 * BLOCK, 128))


def attention_back_kernel(
    query, key2, value2, sums, grad_context, cosine, sine, seg_column, seg_row,
    grad_proj, grad_key, grad_value,
):
    grad_key[...] = jnp.zeros_like(grad_key)
    grad_value[...] = jnp.zeros_like(grad_value)
    for block in range(query.shape[0] // BLOCK):
        lo, hi = block * BLOCK, (block + 1) * BLOCK
        k_lo = max(0, lo - LONGEST)
        query2 = stack_heads(query[lo:hi, :])
        scores = block_scores(block, query2, key2, seg_column, seg_row)
        probs = jnp.exp(scores - sums[block][:, :1])
        grad_rows = stack_heads(grad_context[lo:hi, :])
        grad_probs = dot(grad_rows, value2[k_lo:hi, :], ((1,), (1,)))
        row_dot = jnp.sum(grad_probs * probs, -1, keepdims=True)
        grad_scores = (probs * (grad_probs - row_dot) * HEAD_SIZE**-0.5).astype(BF16)
        moved = merge_heads(dot(grad_scores, key2[k_lo:hi, :], ((1,), (0,))))
        moved = moved.astype(BF16).astype(F32)
        grad_proj[lo:hi, :128] = (
            moved * cosine[lo:hi, :] - swap_halves(moved) * sine[lo:hi, :]
        ).astype(BF16)
        grad_key[k_lo:hi, :] += dot(grad_scores, query2, ((0,), (0,)))
        grad_value[k_lo:hi, :] += dot(probs.astype(BF16), grad_rows, ((0,), (0,)))
    is_first = first_head(grad_key.shape)
    moved = grad_key[...]
    moved = (moved + pltpu.roll(moved, HEAD_SIZE, 1)).astype(BF16).astype(F32)
    moved = moved * cosine[...] - swap_halves(moved) * sine[...]
    other = grad_value[...]
    other = other + pltpu.roll(other, HEAD_SIZE, 1)
    grad_proj[:, 128:] = jnp.where(is_first, moved, other).astype(BF16)


class QuadGather:
    def __init__(self, axis, block, part, send, recv):
        mine = lax.axis_index("fsdp")
        y, x = mine // 4, lax.rem(mine, 4)
        here = x if axis == "x" else y
        up, down = lax.rem(here + 1, 4), lax.rem(here + 3, 4)

        def go(ref, number, place):
            device = y * 4 + place if axis == "x" else place * 4 + x
            return remote(ref, ref, send.at[number], recv.at[number], fsdp=device)

        self.own = [go(block(here), 0, up), go(block(here), 1, down)]
        self.onward = [go(part(down, 0), 2, up), go(part(up, 1), 3, down)]

    def start(self):
        run(self.own)

    def forward(self):
        for came, onward in zip(self.own, self.onward):
            came.wait_recv()
            onward.start()

    def close(self):
        for copy in self.onward:
            copy.wait_recv()
        for copy in self.own + self.onward:
            copy.wait_send()


def forward_kernel(
    tokens, cotangent, top_idx, qkv, small, outw, expert_in, expert_out,
    cosine, sine, seg_column, seg_row,
    mid, out_mid, qkv_own, small_own, gains, normed_one, context, query, key2, value2, sums,
    out_own, normed_own, middle_own, gates_own, mixed, back, grads,
    packed, late, tokens_all, late_all, packed_all, out_all, w_buf, context_all, proj, normed,
    acts, grad_acts, grad_results, blocks, middle_part, gates,
    *scratch,
):
    scratch = list(scratch)

    def take(count):
        taken = scratch[:count]
        del scratch[:count]
        return taken

    scatter_parts = take(6)
    (s0, r0, s1, r1, s2, r2, s3, r3, s4, r4, s5, r5, s6, r6, s7, r7, loc) = take(17)
    quad_sems = take(8)
    group, q_span = 2 * HEAD_SIZE, HQ * HEAD_SIZE
    k_span = KEY_VALUE_HEADS * HEAD_SIZE
    me, core, level, up, down, far = places()
    size = lax.axis_size("fsdp")
    mine = lax.axis_index("fsdp")
    y, x = mine // 4, lax.rem(mine, 4)
    other = level * 2 + (1 - core)
    experts = expert_in.shape[0]
    in_span, hidden = expert_in.shape[2], expert_out.shape[2]
    rows, width = cotangent.shape
    seq_len = normed.shape[0]
    chunk = 256
    per_chunk = chunk // rows

    shard_copies = []
    for local in range(experts):
        shard_copies += [
            pltpu.make_async_copy(
                expert_in.at[local], w_buf.at[local, y, x, :, pl.ds(0, in_span)], loc.at[6 + local]
            ),
            pltpu.make_async_copy(
                expert_out.at[local],
                w_buf.at[local, y, x, :, pl.ds(in_span, hidden)],
                loc.at[8 + local],
            ),
        ]
    run(shard_copies)
    for index in range(SP):
        k_at = q_span + index * HEAD_SIZE
        packed[index, :, :group] = qkv[:, index * group : (index + 1) * group]
        packed[index, :, group : 2 * group] = jnp.concatenate(
            [
                qkv[:, k_at : k_at + HEAD_SIZE],
                qkv[:, k_at + k_span : k_at + k_span + HEAD_SIZE],
            ],
            1,
        )
        packed[index, :, 2 * group :] = small[...]
    own_rows = packed.shape[1]

    def rows_of(target):
        return lambda index: target.at[pl.ds(pl.multiple_of(index * own_rows, own_rows), own_rows)]

    meet(True)
    small_copies = spread("sp", SP, packed, mid, s1, r1, loc.at[0], True, rows_of(mid))
    run(small_copies)
    ring = ring_rows(tokens, tokens_all, s0, r0, loc.at[1])
    ring.start()
    out_copies = spread("sp", SP, outw, out_mid, s2, r2, loc.at[2], False, rows_of(out_mid))
    run(out_copies)
    late[:, :width] = cotangent[...]
    lane = lax.broadcasted_iota(jnp.int32, (rows, 128), 1)
    chosen = jnp.zeros(lane.shape, F32)
    for choice in range(top_idx.shape[1]):
        chosen = jnp.where(lane == top_idx[:, choice : choice + 1] + 2, 1.0, chosen)
    late[:, width:] = chosen.astype(BF16)
    settle(small_copies)
    big = spread("fsdp", size, mid, packed_all, s3, r3, loc.at[3], False)
    run(big)
    ring.forward()
    late_ring = ring_rows(late, late_all, s4, r4, loc.at[4])
    late_ring.start()
    settle(shard_copies)
    first = [
        QuadGather(
            "x",
            lambda index: w_buf.at[0, y, index],
            lambda index, side: w_buf.at[0, y, index, pl.ds(side * 32, 32)],
            *quad_sems[0:2],
        ),
        QuadGather(
            "y",
            lambda index: w_buf.at[1, index, x],
            lambda index, side: w_buf.at[1, index, x, pl.ds(side * 32, 32)],
            *quad_sems[2:4],
        ),
    ]
    second = [
        QuadGather(
            "y",
            lambda index: w_buf.at[0, index],
            lambda index, side: w_buf.at[0, index, pl.ds(side * 2, 2)],
            *quad_sems[4:6],
        ),
        QuadGather(
            "x",
            lambda index: w_buf.at[1, :, index],
            lambda index, side: w_buf.at[1, pl.ds(side * 2, 2), index],
            *quad_sems[6:8],
        ),
    ]
    ring.close()
    settle(big)
    for quad in first:
        quad.start()
    settle(out_copies)
    half_rows = out_all.shape[2]
    own_half = out_mid.at[pl.ds(pl.multiple_of(core * half_rows, half_rows), half_rows)]
    keep = [
        pltpu.make_async_copy(
            out_mid.at[pl.ds(side * half_rows, half_rows)],
            out_all.at[mine, side],
            loc.at[10 + side],
        )
        for side in range(2)
    ]
    run(keep)
    sent, passed = [], []
    for step in range(1, size):
        peer = lax.rem(mine + step, size)
        sent.append(
            remote(own_half, out_all.at[mine, core], s5.at[step], r5.at[step], fsdp=peer)
        )
        source = lax.rem(mine + size - step, size)
        passed.append(
            remote(
                out_all.at[source, core],
                out_all.at[source, core],
                s6.at[step],
                r6.at[step],
                sp=other,
            )
        )
    run(sent)
    everything = packed_all[...].reshape(width, packed_all.shape[2])
    qkv_own[...] = everything[:, : 2 * group]
    small_own[...] = everything[:, 2 * group :]
    pick = (
        lax.broadcasted_iota(jnp.int32, (8, 128), 0) == lax.broadcasted_iota(jnp.int32, (8, 128), 1)
    ).astype(F32).astype(BF16)
    gains[...] = dot(pick, small_own[...], ((1,), (1,)))

    def first_norm(index, carry):
        at = pl.ds(pl.multiple_of(index * chunk, chunk), chunk)
        value = tokens_all[pl.ds(index * per_chunk, per_chunk)].reshape(chunk, width).astype(F32)
        normal = (value * inverse_rms(value) * gains[0:1, :]).astype(BF16)
        normed_one[at, :] = normal
        proj[at, :] = dot(normal, qkv_own[...], ((1,), (0,)))
        return carry

    lax.fori_loop(0, seq_len // chunk, first_norm, 0)
    for quad in first:
        quad.forward()
    late_ring.forward()
    attention_kernel(
        proj, cosine, sine, seg_column, seg_row, context, query, key2, value2, sums
    )
    context_ring = ring_columns(context, context_all, s7, r7, loc.at[5])
    context_ring.start()
    for quad in first:
        quad.close()
    for quad in second:
        quad.start()
    late_ring.close()
    for copy, onward in zip(sent, passed):
        copy.wait_recv()
        onward.start()
    context_ring.forward()
    context_ring.close()
    for copy in sent:
        copy.wait_send()
    settle(passed)
    settle(keep)
    out_own[...] = out_all[pl.ds(2 * me, 2)].reshape(out_own.shape)

    def second_norm(index, carry):
        at = pl.ds(pl.multiple_of(index * chunk, chunk), chunk)
        value = tokens_all[pl.ds(index * per_chunk, per_chunk)].reshape(chunk, width).astype(F32)
        out_full = out_all[...].reshape(width, width)
        value = value + RESIDUAL * dot(context_all[at, :], out_full, ((1,), (0,)))

        @pl.when(index == me // per_chunk)
        def _():
            middle_part[...] = value.reshape(middle_part.shape)

        normed[at, :] = (value * inverse_rms(value) * gains[1:2, :]).astype(BF16)
        return carry

    lax.fori_loop(0, seq_len // chunk, second_norm, 0)
    for quad in second:
        quad.forward()
    middle_own[...] = middle_part[lax.rem(me, per_chunk)]
    at_own = pl.ds(pl.multiple_of(me * rows, rows), rows)
    normed_own[...] = normed[at_own, :]
    for quad in second:
        quad.close()

    def weights_of(local, low, high):
        return w_buf[local, :, :, :, low:high].reshape(width, high - low)

    def tokens_block(index, carry):
        at = pl.ds(pl.multiple_of(index * chunk, chunk), chunk)
        rows_in = normed[at, :]
        logits = dot(rows_in, small_own[...], ((1,), (0,)))
        late_rows = late_all[pl.ds(index * per_chunk, per_chunk)].reshape(chunk, width + 128)
        lanes = lax.broadcasted_iota(jnp.int32, logits.shape, 1)
        shown = jnp.where(late_rows[:, width:].astype(F32) > 0, logits, -jnp.inf)
        expo = jnp.exp(shown - jnp.max(shown, -1, keepdims=True))
        gate_rows = expo / jnp.sum(expo, -1, keepdims=True)
        gates[at, :] = gate_rows
        grad_mixed = RESIDUAL * late_rows[:, :width].astype(F32)
        mix = jnp.zeros((chunk, width), F32)
        grad_rows = jnp.zeros((chunk, width), F32)
        extra = jnp.zeros((chunk, 128), F32)
        for local in range(experts):
            expert = lanes == me * experts + local + 2
            gate = jnp.sum(jnp.where(expert, gate_rows, 0.0), -1, keepdims=True)
            pre_act = dot(rows_in, weights_of(local, 0, in_span), ((1,), (0,)))
            gate_part, up_part = pre_act[:, :hidden], pre_act[:, hidden:]
            sigmoid = 1.0 / (1.0 + jnp.exp(-gate_part))
            silu = gate_part * sigmoid
            act = (silu * up_part).astype(BF16)
            acts[local, at, :] = act
            w_out = weights_of(local, in_span, in_span + hidden)
            produced = dot(act, w_out, ((1,), (1,))).astype(BF16).astype(F32)
            mix = mix + gate * produced
            grad_gate = jnp.sum(grad_mixed * produced, -1, keepdims=True)
            extra = extra + jnp.where(expert, gate * grad_gate, 0.0)
            grad_result = (gate * grad_mixed).astype(BF16)
            grad_results[local, at, :] = grad_result
            grad_act = dot(grad_result, w_out, ((1,), (0,)))
            grad_gate_part = grad_act * up_part * sigmoid * (1.0 + gate_part * (1.0 - sigmoid))
            grad_pre = jnp.concatenate([grad_gate_part, grad_act * silu], 1).astype(BF16)
            grad_acts[local, at, :] = grad_pre
            grad_rows = grad_rows + dot(grad_pre, weights_of(local, 0, in_span), ((1,), (1,)))
        mixed[at, :] = mix.astype(BF16)
        for piece in range(per_chunk):
            place = slice(piece * rows, (piece + 1) * rows)
            blocks[index * per_chunk + piece, :, :width] = grad_rows[place].astype(BF16)
            blocks[index * per_chunk + piece, :, width:] = extra[place].astype(BF16)
        return carry

    lax.fori_loop(0, seq_len // chunk, tokens_block, 0)
    scatter = Scatter(blocks, *scatter_parts)
    scatter.start()
    gates_own[...] = gates[at_own, :]
    owners = grads.shape[0]
    share = width // owners
    count = chunk // share

    def weight_tile(index, carry):
        columns = pl.ds(pl.multiple_of(index * chunk, chunk), chunk)
        turned = normed[:, columns]
        for local in range(experts):
            value = dot(turned, grad_acts[local], ((0,), (0,))).astype(BF16)
            grads[pl.ds(index * count, count), local, :, :in_span] = value.reshape(
                count, share, in_span
            )
            value = dot(grad_results[local, :, columns], acts[local], ((0,), (0,))).astype(BF16)
            grads[pl.ds(index * count, count), local, :, in_span:] = value.reshape(
                count, share, hidden
            )
        return carry

    tiles = width // chunk
    lax.fori_loop(0, tiles // 4, weight_tile, 0)
    scatter.middle()
    lax.fori_loop(tiles // 4, tiles // 2, weight_tile, 0)
    scatter.near_blocks()
    lax.fori_loop(tiles // 2, tiles, weight_tile, 0)
    scatter.end(back)


def wide_call(kernel, name, number, inputs, in_specs, outs, out_specs, scratch):
    return pl.pallas_call(
        kernel,
        name=name,
        out_shape=outs,
        in_specs=in_specs,
        out_specs=out_specs,
        scratch_shapes=scratch,
        cost_estimate=pl.CostEstimate(
            flops=2 * 10**10, bytes_accessed=2 * 10**7, transcendentals=0
        ),
        compiler_params=pltpu.CompilerParams(
            collective_id=number, has_side_effects=True, vmem_limit_bytes=60 * 2**20
        ),
    )(*inputs)


def shards(
    tokens,
    segments,
    top_idx,
    cotangent,
    norm1_gain,
    qkv_weight,
    out_weight,
    norm2_gain,
    router_weight,
    expert_in,
    expert_out,
):
    n_sp = lax.axis_size("sp")
    n_fsdp = lax.axis_size("fsdp")
    sp_index = lax.axis_index("sp")
    rows, width = tokens.shape
    seq_len = rows * n_sp
    weight_rows = qkv_weight.shape[0]
    hidden = expert_out.shape[2]
    q_span, k_span = HQ * HEAD_SIZE, KEY_VALUE_HEADS * HEAD_SIZE
    group = q_span // n_sp
    head = k_span // n_sp
    small = jnp.concatenate([norm1_gain[:, None], norm2_gain[:, None], router_weight], 1)
    small = jnp.pad(small, ((0, 0), (0, 128 - small.shape[1])))
    pack_width = 2 * group + 128
    any_shape = jax.ShapeDtypeStruct
    cosine, sine = rope_tables(seq_len)
    seg_row, seg_column = segments, segments.reshape(seq_len, 1)
    n_experts = expert_in.shape[0]
    in_span = expert_in.shape[2]
    slab = any_shape((seq_len, group), BF16)
    (
        _, _, qkv_own, small_own, gains, normed_one, context, query, key2, value2, sums,
        out_own, normed_own, middle_own, gates_own, mixed, back, grads,
    ) = wide_call(
        forward_kernel,
        "forward",
        1,
        (
            tokens, cotangent, top_idx, qkv_weight, small, out_weight, expert_in, expert_out,
            cosine, sine, seg_column, seg_row,
        ),
        [HBM] + [VMEM] * 4 + [HBM] * 3 + [VMEM] * 4,
        (
            any_shape((SP * weight_rows, pack_width), BF16),
            any_shape((SP * weight_rows, width), BF16),
            any_shape((width, 2 * group), BF16),
            any_shape((width, 128), BF16),
            any_shape((8, width), F32),
            any_shape((seq_len, width), BF16),
            slab, slab, slab, slab,
            any_shape((seq_len // BLOCK, 2 * BLOCK, 128), F32),
            any_shape((group, width), BF16),
            any_shape((rows, width), BF16),
            any_shape((rows, width), F32),
            any_shape((rows, 128), F32),
            any_shape((seq_len, width), BF16),
            any_shape((rows, width + 128), F32),
            any_shape((n_fsdp, n_experts, width // n_fsdp, in_span + hidden), BF16),
        ),
        (HBM, HBM) + (VMEM,) * 16,
        [
            pltpu.VMEM((SP, weight_rows, pack_width), BF16),
            pltpu.VMEM((rows, width + 128), BF16),
            pltpu.VMEM((SP, rows, width), BF16),
            pltpu.VMEM((SP, rows, width + 128), BF16),
            pltpu.VMEM((n_fsdp, SP * weight_rows, pack_width), BF16),
            pltpu.VMEM((n_fsdp, 2, SP * weight_rows // 2, width), BF16),
            pltpu.VMEM((n_experts, 4, 4, width // n_fsdp, in_span + hidden), BF16),
            pltpu.VMEM((seq_len, width), BF16),
            pltpu.VMEM((seq_len, 2 * group), F32),
            pltpu.VMEM((seq_len, width), BF16),
            pltpu.VMEM((n_experts, seq_len, hidden), BF16),
            pltpu.VMEM((n_experts, seq_len, in_span), BF16),
            pltpu.VMEM((n_experts, seq_len, width), BF16),
            pltpu.VMEM((SP, rows, width + 128), BF16),
            pltpu.VMEM((2, rows, width), F32),
            pltpu.VMEM((seq_len, 128), F32),
        ]
        + scatter_scratch(rows, width + 128)
        + [DMA((8,))] * 6
        + [DMA((n_fsdp,))] * 2
        + [DMA((8,))] * 2
        + [DMA((n_fsdp,))] * 4
        + [DMA((8,))] * 2
        + [DMA((12,))]
        + [DMA((4,))] * 8,
    )
    gain_one, gain_two = gains[0:1], gains[1:2]
    share = width // n_fsdp
    shares = group // n_fsdp
    half_grads = (4, share // 2, in_span + hidden)
    half_share = (share // 2, in_span + hidden)
    grad_middle, grad_normed_one, bundle, out_sum, expert_grads, mixed_own = wide_call(
        back_kernel,
        "backward",
        4,
        (
            back, gates_own, normed_own, middle_own, cotangent, gain_two, small_own, out_own,
            context, query, key2, value2, sums, cosine, sine, seg_column, seg_row, qkv_own,
            normed_one, grads.reshape(4, 4, n_experts, share, in_span + hidden),
            mixed.reshape(SP, rows, width),
        ),
        [VMEM] * 21,
        (
            any_shape((rows, width), F32),
            any_shape((rows, width), F32),
            any_shape((SP, weight_rows, pack_width), F32),
            any_shape((shares, width), F32),
            any_shape((n_experts, share, in_span + hidden), F32),
            any_shape((rows, width), F32),
        ),
        (VMEM,) * 6,
        [
            pltpu.VMEM((rows, width), BF16),
            pltpu.VMEM((SP, rows, width), BF16),
            pltpu.VMEM((seq_len, group), BF16),
            pltpu.VMEM((seq_len, 2 * group), BF16),
            pltpu.VMEM((seq_len, group), F32),
            pltpu.VMEM((seq_len, group), F32),
            pltpu.VMEM((SP, rows, width), BF16),
            pltpu.VMEM((width, 128), F32),
            pltpu.VMEM((n_fsdp, share, pack_width), BF16),
            pltpu.VMEM((n_fsdp, shares, width), BF16),
            pltpu.VMEM((n_fsdp, share, pack_width), BF16),
            pltpu.VMEM((n_fsdp, shares, width), BF16),
            pltpu.VMEM((SP, weight_rows, pack_width), F32),
            pltpu.VMEM((2,) + half_grads, BF16),
            pltpu.VMEM((2,) + half_grads, BF16),
        ]
        + scatter_scratch(rows, width) * 2
        + quad_scratch(half_grads) * 2
        + quad_scratch(half_share) * 2
        + [DMA((8,))] * 2
        + [DMA((n_fsdp,))] * 4
        + [DMA((8,))] * 2
        + [DMA((4,))],
    )
    block_out = middle_own + RESIDUAL * mixed_own
    moves = []
    for f in range(n_fsdp):
        for s in range(n_sp):
            moves.append((f * n_sp + s, (s * group + f * shares) // weight_rows))
    if shares == weight_rows:
        out_grad = lax.ppermute(out_sum, ("fsdp", "sp"), moves)
    else:
        whole = lax.all_gather(out_sum, ("fsdp", "sp"), axis=0, tiled=False)
        whole = whole.reshape(n_fsdp, n_sp, shares, width).transpose(1, 0, 2, 3)
        device = lax.axis_index("fsdp") * n_sp + sp_index
        out_grad = lax.dynamic_slice_in_dim(
            whole.reshape(width, width), device * weight_rows, weight_rows, 0
        )

    qkv_grad = jnp.concatenate(
        [
            bundle[:, :, :group].transpose(1, 0, 2).reshape(weight_rows, q_span),
            bundle[:, :, group : group + head].transpose(1, 0, 2).reshape(weight_rows, k_span),
            bundle[:, :, group + head : 2 * group].transpose(1, 0, 2).reshape(weight_rows, k_span),
        ],
        1,
    )
    smalls = jnp.sum(bundle[:, :, 2 * group :], 0)
    gain_two_grad = smalls[:, 1]
    router_grad = smalls[:, 2 : 2 + E]
    gain_one_grad = jnp.sum(qkv_grad * qkv_weight.astype(F32), 1) / norm1_gain.astype(F32)
    hidden_own = tokens.astype(F32)
    input_grad = grad_middle + rms_backward(
        grad_normed_one, hidden_own, inverse_rms(hidden_own), gain_one
    )
    return (
        block_out,
        input_grad,
        gain_one_grad,
        qkv_grad,
        out_grad,
        gain_two_grad,
        router_grad,
        expert_grads[:, :, :in_span],
        expert_grads[:, :, in_span:],
    )


def solution(mesh):
    both = P(("fsdp", "sp"), None)
    flat = P(("fsdp", "sp"))
    expert = P("sp", "fsdp", None)
    return jax.shard_map(
        shards,
        mesh=mesh,
        in_specs=(both, P("fsdp", None), both, both, flat, both, both, flat, both, expert, expert),
        out_specs=(both, both, flat, both, both, flat, both, expert, expert),
        check_vma=False,
    )
```

```python
import jax
import jax.numpy as jnp
import numpy as np
from jax import lax
from jax.experimental import pallas as pl
from jax.experimental.pallas import tpu as pltpu
from jax.sharding import PartitionSpec as P

HQ = 16
KEY_VALUE_HEADS = 8
HEAD_SIZE = 64
E = 16
EPSILON = 1e-06
RESIDUAL = 0.22
BLOCK = 256
LONGEST = 512
BF16 = jnp.bfloat16
F32 = jnp.float32


def rope_tables(count):
    frequency = np.float32(10000.0) ** (
        np.float32(-2.0) * np.arange(HEAD_SIZE // 2, dtype=np.float32) / np.float32(HEAD_SIZE)
    )
    angles = np.arange(count, dtype=np.float32)[:, None] * frequency.astype(np.float32)[None, :]
    cosine = np.cos(angles).astype(np.float32)
    sine = np.sin(angles).astype(np.float32)
    return np.concatenate([cosine] * 4, 1), np.concatenate([-sine, sine] * 2, 1)


def dot(left, right, contract):
    return lax.dot_general(left, right, (contract, ((), ())), preferred_element_type=F32)


def inverse_rms(value):
    return lax.rsqrt(jnp.mean(value * value, -1, keepdims=True) + EPSILON)


def rms_backward(grad, value, inverse, gain):
    scaled = grad * gain
    return inverse * scaled - value * (inverse**3) * jnp.mean(scaled * value, -1, keepdims=True)


MESH = pl.DeviceIdType.MESH
VMEM = pl.BlockSpec(memory_space=pltpu.VMEM)
HBM = pl.BlockSpec(memory_space=pl.ANY)
DMA = pltpu.SemaphoreType.DMA
SP, FSDP = 8, 16


def remote(src, dst, send, recv, **device):
    return pltpu.make_async_remote_copy(
        src_ref=src,
        dst_ref=dst,
        send_sem=send,
        recv_sem=recv,
        device_id=device,
        device_id_type=MESH,
    )


def meet(with_fsdp):
    barrier = pltpu.get_barrier_semaphore()
    me = lax.axis_index("sp")
    for step in range(1, SP):
        pl.semaphore_signal(
            barrier, inc=1, device_id={"sp": lax.rem(me + step, SP)}, device_id_type=MESH
        )
    count = SP - 1
    if with_fsdp:
        size = lax.axis_size("fsdp")
        mine = lax.axis_index("fsdp")
        for step in range(1, size):
            pl.semaphore_signal(
                barrier, inc=1, device_id={"fsdp": lax.rem(mine + step, size)}, device_id_type=MESH
            )
        count += size - 1
    pl.semaphore_wait(barrier, count)


def places():
    me = lax.axis_index("sp")
    level, core = me // 2, lax.rem(me, 2)
    up = lax.rem(level + 1, 4)
    down = lax.rem(level + 3, 4)
    far = lax.rem(level + 2, 4)
    return me, core, level, up, down, far


class Ring:
    def __init__(self, source, slot, part, send, recv, local):
        me, core, level, up, down, far = places()
        self.me = me
        up_id, down_id, far_id = up * 2 + core, down * 2 + core, far * 2 + core
        other = level * 2 + (1 - core)

        def go(src, dst, number, peer):
            return remote(src, dst, send.at[number], recv.at[number], sp=peer)

        self.first = [
            go(source, slot(me), 0, up_id),
            go(source, slot(me), 1, down_id),
            go(source, slot(me), 2, other),
        ]
        self.local = pltpu.make_async_copy(source, slot(me), local)
        self.next_up = [
            go(part(down_id, 0), part(down_id, 0), 3, up_id),
            go(slot(down_id), slot(down_id), 4, other),
        ]
        self.next_down = [
            go(part(up_id, 1), part(up_id, 1), 5, down_id),
            go(slot(up_id), slot(up_id), 6, other),
        ]
        self.last = go(slot(far_id), slot(far_id), 7, other)

    def start(self):
        for copy in self.first:
            copy.start()
        self.local.start()

    def forward(self):
        self.first[0].wait_recv()
        for copy in self.next_up:
            copy.start()
        self.first[1].wait_recv()
        for copy in self.next_down:
            copy.start()

    def close(self):
        self.next_up[0].wait_recv()
        self.next_down[0].wait_recv()
        self.last.start()
        self.local.wait()
        for copy in (self.first[0], self.first[1], self.next_up[0], self.next_down[0]):
            copy.wait_send()
        for copy in (self.first[2], self.next_up[1], self.next_down[1], self.last):
            copy.wait()

    def finish(self):
        self.forward()
        self.close()


def ring_rows(source, target, send, recv, local):
    half = source.shape[0] // 2
    return Ring(
        source,
        lambda index: target.at[index],
        lambda index, side: target.at[index, pl.ds(side * half, half)],
        send,
        recv,
        local,
    )


def ring_columns(source, target, send, recv, local):
    rows, wide = source.shape
    half = rows // 2

    def columns(index):
        return pl.ds(pl.multiple_of(index * wide, wide), wide)

    return Ring(
        source,
        lambda index: target.at[:, columns(index)],
        lambda index, side: target.at[pl.ds(side * half, half), columns(index)],
        send,
        recv,
        local,
    )


def spread(axis, size, source, target, send, recv, local, blocks, place=None):
    me = lax.axis_index(axis)
    landing = target.at[me] if place is None else place(me)
    copies = []
    for step in range(1, size):
        peer = lax.rem(me + step, size)
        copies.append(
            remote(
                source.at[peer] if blocks else source,
                landing,
                send.at[step],
                recv.at[step],
                **{axis: peer},
            )
        )
    copies.append(pltpu.make_async_copy(source.at[me] if blocks else source, landing, local))
    return copies


def run(copies):
    for copy in copies:
        copy.start()


def settle(copies):
    for copy in copies:
        copy.wait()


class Scatter:
    def __init__(self, blocks, other_sums, sums, near, far_parts, send, recv):
        me, core, level, up, down, far = places()
        other = level * 2 + (1 - core)
        self.blocks, self.other_sums, self.sums = blocks, other_sums, sums
        self.near, self.far_parts = near, far_parts
        self.core, self.level, self.up, self.down, self.far = core, level, up, down, far
        half = blocks.shape[1] // 2
        self.half = half
        up_id, down_id = up * 2 + core, down * 2 + core

        def go(src, dst, number, peer):
            return remote(src, dst, send.at[number], recv.at[number], sp=peer)

        order = (far, up, down, level)
        self.pair = [
            go(blocks.at[at * 2 + (1 - core)], other_sums.at[number], number, other)
            for number, at in enumerate(order)
        ]
        self.to_up = go(sums.at[0, pl.ds(0, half)], far_parts.at[0], 4, up_id)
        self.to_down = go(sums.at[0, pl.ds(half, half)], far_parts.at[1], 5, down_id)
        self.full_up = go(sums.at[1], near.at[0], 6, up_id)
        self.full_down = go(sums.at[2], near.at[1], 7, down_id)

    def start(self):
        run(self.pair)

    def both(self, number, at):
        mine = self.blocks[at * 2 + self.core].astype(F32)
        return mine + self.other_sums[number].astype(F32)

    def middle(self):
        self.pair[0].wait_recv()
        self.sums[0] = self.both(0, self.far).astype(BF16)
        self.to_up.start()
        self.to_down.start()

    def near_blocks(self):
        half = self.half
        self.pair[1].wait_recv()
        self.to_up.wait_recv()
        total = self.both(1, self.up)
        self.sums[1, :half] = (total[:half] + self.far_parts[0].astype(F32)).astype(BF16)
        self.sums[1, half:] = total[half:].astype(BF16)
        self.full_up.start()
        self.pair[2].wait_recv()
        self.to_down.wait_recv()
        total = self.both(2, self.down)
        self.sums[2, :half] = total[:half].astype(BF16)
        self.sums[2, half:] = (total[half:] + self.far_parts[1].astype(F32)).astype(BF16)
        self.full_down.start()

    def end(self, out):
        self.pair[3].wait_recv()
        total = self.both(3, self.level)
        self.full_up.wait_recv()
        total = total + self.near[0].astype(F32)
        self.full_down.wait_recv()
        out[...] = total + self.near[1].astype(F32)
        for copy in self.pair + [self.to_up, self.to_down, self.full_up, self.full_down]:
            copy.wait_send()

    def finish(self, out):
        self.middle()
        self.near_blocks()
        self.end(out)


def scatter_scratch(rows, width):
    return [
        pltpu.VMEM((4, rows, width), BF16),
        pltpu.VMEM((3, rows, width), BF16),
        pltpu.VMEM((2, rows, width), BF16),
        pltpu.VMEM((2, rows // 2, width), BF16),
        DMA((8,)),
        DMA((8,)),
    ]


class Quad:
    def __init__(self, axis, source, far_parts, near, sums, send, recv):
        mine = lax.axis_index("fsdp")
        y, x = mine // 4, lax.rem(mine, 4)
        here = x if axis == "x" else y
        self.source, self.far_parts, self.near, self.sums = source, far_parts, near, sums
        self.here = here
        self.up, self.down, self.far = (lax.rem(here + step, 4) for step in (1, 3, 2))

        def device(place):
            return y * 4 + place if axis == "x" else place * 4 + x

        def go(src, dst, number, place):
            return remote(src, dst, send.at[number], recv.at[number], fsdp=device(place))

        self.far_up = go(source(self.far, 0), far_parts.at[0], 0, self.up)
        self.far_down = go(source(self.far, 1), far_parts.at[1], 1, self.down)
        self.plain_up = go(source(self.up, 1), near.at[0, 1], 2, self.up)
        self.plain_down = go(source(self.down, 0), near.at[1, 0], 3, self.down)
        self.sum_up = go(sums.at[0], near.at[0, 0], 4, self.up)
        self.sum_down = go(sums.at[1], near.at[1, 1], 5, self.down)

    def start(self):
        run((self.far_up, self.far_down, self.plain_up, self.plain_down))

    def near_blocks(self):
        self.far_up.wait_recv()
        total = self.source(self.up, 0)[...].astype(F32) + self.far_parts[0].astype(F32)
        self.sums[0] = total.astype(BF16)
        self.sum_up.start()
        self.far_down.wait_recv()
        total = self.source(self.down, 1)[...].astype(F32) + self.far_parts[1].astype(F32)
        self.sums[1] = total.astype(BF16)
        self.sum_down.start()

    def end(self, store):
        for copy in (self.plain_up, self.plain_down, self.sum_up, self.sum_down):
            copy.wait_recv()
        for side in range(2):
            total = self.source(self.here, side)[...].astype(F32)
            total = total + self.near[0, side].astype(F32) + self.near[1, side].astype(F32)
            store(side, total)
        for copy in (
            self.far_up, self.far_down, self.plain_up, self.plain_down, self.sum_up, self.sum_down
        ):
            copy.wait_send()


def quad_scratch(shape):
    return [
        pltpu.VMEM((2,) + shape, BF16),
        pltpu.VMEM((2, 2) + shape, BF16),
        pltpu.VMEM((2,) + shape, BF16),
        DMA((6,)),
        DMA((6,)),
    ]


def exact_dot(left, right, contract):
    return lax.dot_general(
        left, right, (contract, ((), ())), precision=lax.Precision.HIGHEST,
        preferred_element_type=F32,
    )


def back_kernel(
    back, gates, normed, middle, cotangent, gain, small, out_own, context,
    query, key2, value2, sums, cosine, sine, seg_row, qkv_own, normed_one,
    grads, mixed,
    grad_middle, grad_normed_one, bundle_all, out_sum, expert_grads, mixed_own,
    attended, attended_all, grad_context, grad_proj, grad_key, grad_value, blocks, small_part,
    bundle, outp, out_in, bundle_sum, halves_a, halves_b, hold_a, hold_b,
    seg_column,
    *scratch,
):
    scratch = list(scratch)

    def take(count):
        taken = scratch[:count]
        del scratch[:count]
        return taken

    mix_scatter = Scatter(mixed, *take(6))
    scatter = Scatter(blocks, *take(6))

    def half_a(index, side):
        return grads.at[:, index, 0, pl.ds(side * half, half)]

    def half_b(index, side):
        return grads.at[index, :, 1, pl.ds(side * half, half)]

    half = grads.shape[3] // 2
    first_a = Quad("x", half_a, *take(5))
    first_b = Quad("y", half_b, *take(5))
    second_a = Quad("y", lambda index, side: halves_a.at[side, index], *take(5))
    second_b = Quad("x", lambda index, side: halves_b.at[side, index], *take(5))
    quarter = bundle.shape[2] // 4

    def bundle_a(index, side):
        return bundle.at[:, index, pl.ds(side * quarter, quarter)]

    def bundle_b(index, side):
        return bundle.at[index, :, pl.ds((2 + side) * quarter, quarter)]

    bundle_first = [Quad("x", bundle_a, *take(5)), Quad("y", bundle_b, *take(5))]
    bundle_second = [
        Quad("y", lambda index, side: hold_a.at[side, index], *take(5)),
        Quad("x", lambda index, side: hold_b.at[side, index], *take(5)),
    ]

    def keep_bundle(hold):
        def store(side, total):
            hold[side] = total.astype(BF16)

        return store

    def store_bundle(first_row):
        def store(side, total):
            groups = quarter // bundle_sum.shape[1]
            start = (first_row + side * quarter) // bundle_sum.shape[1]
            bundle_sum[start : start + groups] = total.reshape(
                groups, bundle_sum.shape[1], total.shape[1]
            )

        return store

    ring_send, ring_recv, s2, r2, s3, r3, loc = take(7)

    def keep_a(side, total):
        halves_a[side] = total.astype(BF16)

    def keep_b(side, total):
        halves_b[side] = total.astype(BF16)

    meet(True)
    size = lax.axis_size("fsdp")
    first_a.start()
    first_b.start()
    fill_column(seg_row, seg_column)
    width = cotangent.shape[1]
    value = middle[...]
    inverse = inverse_rms(value)
    weighted = back[:, width:]
    grad_logits = weighted - gates[...] * jnp.sum(weighted, -1, keepdims=True)
    grad_normed = back[:, :width] + exact_dot(grad_logits, small[...].astype(F32), ((1,), (1,)))
    grad_rows = cotangent[...].astype(F32) + rms_backward(grad_normed, value, inverse, gain[...])
    grad_middle[...] = grad_rows
    attended[...] = (RESIDUAL * grad_rows).astype(BF16)
    ring = ring_rows(attended, attended_all, ring_send, ring_recv, loc.at[0])
    ring.start()
    gain_lane = lax.broadcasted_iota(jnp.int32, grad_logits.shape, 1) == 1
    small_part[...] = exact_dot(normed[...].astype(F32), grad_logits, ((0,), (0,))) + exact_dot(
        grad_normed * value * inverse, gain_lane.astype(F32), ((0,), (0,))
    )
    ring.finish()
    mix_scatter.start()
    first_a.near_blocks()
    first_b.near_blocks()
    rows = attended.shape[0]
    for index in range(SP):
        at = slice(index * rows, (index + 1) * rows)
        grad_context[at, :] = dot(attended_all[index], out_own[...], ((1,), (1,))).astype(BF16)
    out_part = jnp.zeros((context.shape[1], width), F32)
    for index in range(SP):
        at = slice(index * rows, (index + 1) * rows)
        out_part = out_part + dot(context[at, :], attended_all[index], ((0,), (0,)))
    outp[...] = out_part.astype(BF16).reshape(outp.shape)
    outs = spread("fsdp", size, outp, out_in, s2, r2, loc.at[1], True)
    run(outs)
    mix_scatter.middle()
    attention_back_kernel(
        query, key2, value2, sums, grad_context, cosine, sine, seg_column, seg_row,
        grad_proj, grad_key, grad_value,
    )
    mix_scatter.near_blocks()
    span = grad_proj.shape[1]
    share = bundle.shape[2]
    tile = 4 * share
    for index in range(width // tile):
        at = slice(index * tile, (index + 1) * tile)
        part = dot(normed_one[:, at], grad_proj[...], ((0,), (0,))).astype(BF16)
        bundle[index, :, :, :span] = part.reshape(tile // share, share, span)
        bundle[index, :, :, span:] = (
            small_part[at, :].astype(BF16).reshape(tile // share, share, 128)
        )
    for quad in bundle_first:
        quad.start()
    for index in range(SP):
        at = slice(index * rows, (index + 1) * rows)
        blocks[index] = dot(grad_proj[at, :], qkv_own[...], ((1,), (1,))).astype(BF16)
    scatter.start()
    for quad in bundle_first:
        quad.near_blocks()
    first_a.end(keep_a)
    first_b.end(keep_b)
    scatter.middle()
    bundle_first[0].end(keep_bundle(hold_a))
    bundle_first[1].end(keep_bundle(hold_b))
    for quad in bundle_second:
        quad.start()
    second_a.start()
    second_b.start()
    mix_scatter.end(mixed_own)
    for quad in bundle_second:
        quad.near_blocks()
    scatter.near_blocks()
    bundle_second[0].end(store_bundle(0))
    bundle_second[1].end(store_bundle(2 * quarter))
    shares = spread("sp", SP, bundle_sum, bundle_all, s3, r3, loc.at[3], True)
    run(shares)
    second_a.near_blocks()
    second_b.near_blocks()
    settle(outs)
    total = out_in[0].astype(F32)
    for index in range(1, size):
        total = total + out_in[index].astype(F32)
    out_sum[...] = total

    def store_a(side, total):
        expert_grads[0, side * half : (side + 1) * half, :] = total

    def store_b(side, total):
        expert_grads[1, side * half : (side + 1) * half, :] = total

    second_a.end(store_a)
    second_b.end(store_b)
    scatter.end(grad_normed_one)
    settle(shares)


def swap_halves(value):
    wide = value.shape[-1]
    lane = lax.broadcasted_iota(jnp.int32, value.shape, 1)
    return jnp.where(
        lane % HEAD_SIZE < HEAD_SIZE // 2,
        pltpu.roll(value, wide - HEAD_SIZE // 2, 1),
        pltpu.roll(value, HEAD_SIZE // 2, 1),
    )


def first_head(shape):
    return lax.broadcasted_iota(jnp.int32, shape, 1) < HEAD_SIZE


def stack_heads(slab):
    is_first = first_head(slab.shape)
    zero = jnp.zeros_like(slab)
    return jnp.concatenate([jnp.where(is_first, slab, zero), jnp.where(is_first, zero, slab)], 0)


def merge_heads(stacked):
    half = stacked.shape[0] // 2
    return jnp.where(first_head((half, stacked.shape[1])), stacked[:half], stacked[half:])


def row_to_column(row):
    count = row.shape[1]
    same = lax.broadcasted_iota(jnp.int32, (count, count), 0) == lax.broadcasted_iota(
        jnp.int32, (count, count), 1
    )
    spread_row = jnp.broadcast_to(row.astype(F32), (count, count))
    return jnp.sum(jnp.where(same, spread_row, 0.0), 1, keepdims=True)


def fill_column(seg_row, seg_column):
    for index in range(seg_row.shape[1] // 128):
        at = slice(index * 128, (index + 1) * 128)
        seg_column[at, :] = row_to_column(seg_row[:, at])


def block_scores(block, query2, key2, seg_column, seg_row):
    lo, hi = block * BLOCK, (block + 1) * BLOCK
    k_lo = max(0, lo - LONGEST)
    rows = lo + lax.broadcasted_iota(jnp.int32, (BLOCK, hi - k_lo), 0)
    keys = k_lo + lax.broadcasted_iota(jnp.int32, (BLOCK, hi - k_lo), 1)
    allowed = (keys <= rows) & (
        seg_column[lo:hi, :] == seg_row[:, k_lo:hi].astype(F32)
    )
    scores = dot(query2, key2[k_lo:hi, :], ((1,), (1,))) * HEAD_SIZE**-0.5
    return jnp.where(jnp.concatenate([allowed, allowed], 0), scores, -jnp.inf)


def attention_kernel(
    proj, cosine, sine, seg_column, seg_row, context, query, key2, value2, sums
):
    cos_rows, sin_rows = cosine[...], sine[...]
    slab = proj[:, :128]
    query[...] = (slab * cos_rows + swap_halves(slab) * sin_rows).astype(BF16)
    slab = proj[:, 128:]
    is_first = first_head(slab.shape)
    turned = slab * cos_rows + swap_halves(slab) * sin_rows
    key2[...] = jnp.where(is_first, turned, pltpu.roll(turned, HEAD_SIZE, 1)).astype(BF16)
    value2[...] = jnp.where(is_first, pltpu.roll(slab, HEAD_SIZE, 1), slab).astype(BF16)
    for block in range(proj.shape[0] // BLOCK):
        lo, hi = block * BLOCK, (block + 1) * BLOCK
        k_lo = max(0, lo - LONGEST)
        scores = block_scores(block, stack_heads(query[lo:hi, :]), key2, seg_column, seg_row)
        top = jnp.max(scores, -1, keepdims=True)
        expo = jnp.exp(scores - top)
        total = jnp.sum(expo, -1, keepdims=True)
        probs = (expo / total).astype(BF16)
        context[lo:hi, :] = merge_heads(dot(probs, value2[k_lo:hi, :], ((1,), (0,)))).astype(BF16)
        sums[block] = jnp.broadcast_to(top + jnp.log(total), (2 * BLOCK, 128))


def attention_back_kernel(
    query, key2, value2, sums, grad_context, cosine, sine, seg_column, seg_row,
    grad_proj, grad_key, grad_value,
):
    grad_key[...] = jnp.zeros_like(grad_key)
    grad_value[...] = jnp.zeros_like(grad_value)
    for block in range(query.shape[0] // BLOCK):
        lo, hi = block * BLOCK, (block + 1) * BLOCK
        k_lo = max(0, lo - LONGEST)
        query2 = stack_heads(query[lo:hi, :])
        scores = block_scores(block, query2, key2, seg_column, seg_row)
        probs = jnp.exp(scores - sums[block][:, :1])
        grad_rows = stack_heads(grad_context[lo:hi, :])
        grad_probs = dot(grad_rows, value2[k_lo:hi, :], ((1,), (1,)))
        row_dot = jnp.sum(grad_probs * probs, -1, keepdims=True)
        grad_scores = (probs * (grad_probs - row_dot) * HEAD_SIZE**-0.5).astype(BF16)
        moved = merge_heads(dot(grad_scores, key2[k_lo:hi, :], ((1,), (0,))))
        moved = moved.astype(BF16).astype(F32)
        grad_proj[lo:hi, :128] = (
            moved * cosine[lo:hi, :] - swap_halves(moved) * sine[lo:hi, :]
        ).astype(BF16)
        grad_key[k_lo:hi, :] += dot(grad_scores, query2, ((0,), (0,)))
        grad_value[k_lo:hi, :] += dot(probs.astype(BF16), grad_rows, ((0,), (0,)))
    is_first = first_head(grad_key.shape)
    moved = grad_key[...]
    moved = (moved + pltpu.roll(moved, HEAD_SIZE, 1)).astype(BF16).astype(F32)
    moved = moved * cosine[...] - swap_halves(moved) * sine[...]
    other = grad_value[...]
    other = other + pltpu.roll(other, HEAD_SIZE, 1)
    grad_proj[:, 128:] = jnp.where(is_first, moved, other).astype(BF16)


class QuadGather:
    def __init__(self, axis, block, part, send, recv):
        mine = lax.axis_index("fsdp")
        y, x = mine // 4, lax.rem(mine, 4)
        here = x if axis == "x" else y
        up, down = lax.rem(here + 1, 4), lax.rem(here + 3, 4)

        def go(ref, number, place):
            device = y * 4 + place if axis == "x" else place * 4 + x
            return remote(ref, ref, send.at[number], recv.at[number], fsdp=device)

        self.own = [go(block(here), 0, up), go(block(here), 1, down)]
        self.onward = [go(part(down, 0), 2, up), go(part(up, 1), 3, down)]

    def start(self):
        run(self.own)

    def forward(self):
        for came, onward in zip(self.own, self.onward):
            came.wait_recv()
            onward.start()

    def close(self):
        for copy in self.onward:
            copy.wait_recv()
        for copy in self.own + self.onward:
            copy.wait_send()


def forward_kernel(
    tokens, cotangent, top_idx, qkv, gain_one, gain_two, router, outw, expert_in, expert_out,
    cosine, sine, seg_row,
    mid, out_mid, qkv_own, small_own, gains, normed_one, context, query, key2, value2, sums,
    out_own, normed_own, middle_own, gates_own, mixed, back, grads,
    packed, late, tokens_all, late_all, packed_all, out_all, w_buf, context_all, proj, normed,
    acts, grad_acts, grad_results, blocks, middle_part, gates, seg_column,
    *scratch,
):
    scratch = list(scratch)

    def take(count):
        taken = scratch[:count]
        del scratch[:count]
        return taken

    scatter_parts = take(6)
    (s0, r0, s1, r1, s2, r2, s3, r3, s4, r4, s5, r5, s6, r6, s7, r7, loc) = take(17)
    quad_sems = take(8)
    group, q_span = 2 * HEAD_SIZE, HQ * HEAD_SIZE
    k_span = KEY_VALUE_HEADS * HEAD_SIZE
    me, core, level, up, down, far = places()
    size = lax.axis_size("fsdp")
    mine = lax.axis_index("fsdp")
    y, x = mine // 4, lax.rem(mine, 4)
    other = level * 2 + (1 - core)
    experts = expert_in.shape[0]
    in_span, hidden = expert_in.shape[2], expert_out.shape[2]
    rows, width = cotangent.shape
    seq_len = normed.shape[0]
    chunk = 256
    per_chunk = chunk // rows

    shard_copies = []
    for local in range(experts):
        shard_copies += [
            pltpu.make_async_copy(
                expert_in.at[local], w_buf.at[local, y, x, :, pl.ds(0, in_span)], loc.at[6 + local]
            ),
            pltpu.make_async_copy(
                expert_out.at[local],
                w_buf.at[local, y, x, :, pl.ds(in_span, hidden)],
                loc.at[8 + local],
            ),
        ]
    run(shard_copies)
    fill_column(seg_row, seg_column)
    lanes = lax.broadcasted_iota(jnp.int32, (qkv.shape[0], 128), 1)
    shift = (
        lax.broadcasted_iota(jnp.int32, (E, 128), 0) + 2
        == lax.broadcasted_iota(jnp.int32, (E, 128), 1)
    ).astype(F32).astype(BF16)
    small = dot(router[...], shift, ((1,), (0,)))
    small = small + jnp.where(lanes == 0, row_to_column(gain_one[...]), 0.0)
    small = small + jnp.where(lanes == 1, row_to_column(gain_two[...]), 0.0)
    small = small.astype(BF16)
    for index in range(SP):
        k_at = q_span + index * HEAD_SIZE
        packed[index, :, :group] = qkv[:, index * group : (index + 1) * group]
        packed[index, :, group : 2 * group] = jnp.concatenate(
            [
                qkv[:, k_at : k_at + HEAD_SIZE],
                qkv[:, k_at + k_span : k_at + k_span + HEAD_SIZE],
            ],
            1,
        )
        packed[index, :, 2 * group :] = small
    own_rows = packed.shape[1]

    def rows_of(target):
        return lambda index: target.at[pl.ds(pl.multiple_of(index * own_rows, own_rows), own_rows)]

    meet(True)
    small_copies = spread("sp", SP, packed, mid, s1, r1, loc.at[0], True, rows_of(mid))
    run(small_copies)
    ring = ring_rows(tokens, tokens_all, s0, r0, loc.at[1])
    ring.start()
    out_copies = spread("sp", SP, outw, out_mid, s2, r2, loc.at[2], False, rows_of(out_mid))
    run(out_copies)
    late[:, :width] = cotangent[...]
    lane = lax.broadcasted_iota(jnp.int32, (rows, 128), 1)
    chosen = jnp.zeros(lane.shape, F32)
    for choice in range(top_idx.shape[1]):
        chosen = jnp.where(lane == top_idx[:, choice : choice + 1] + 2, 1.0, chosen)
    late[:, width:] = chosen.astype(BF16)
    settle(small_copies)
    big = spread("fsdp", size, mid, packed_all, s3, r3, loc.at[3], False)
    run(big)
    ring.forward()
    late_ring = ring_rows(late, late_all, s4, r4, loc.at[4])
    late_ring.start()
    settle(shard_copies)
    first = [
        QuadGather(
            "x",
            lambda index: w_buf.at[0, y, index],
            lambda index, side: w_buf.at[0, y, index, pl.ds(side * 32, 32)],
            *quad_sems[0:2],
        ),
        QuadGather(
            "y",
            lambda index: w_buf.at[1, index, x],
            lambda index, side: w_buf.at[1, index, x, pl.ds(side * 32, 32)],
            *quad_sems[2:4],
        ),
    ]
    second = [
        QuadGather(
            "y",
            lambda index: w_buf.at[0, index],
            lambda index, side: w_buf.at[0, index, pl.ds(side * 2, 2)],
            *quad_sems[4:6],
        ),
        QuadGather(
            "x",
            lambda index: w_buf.at[1, :, index],
            lambda index, side: w_buf.at[1, pl.ds(side * 2, 2), index],
            *quad_sems[6:8],
        ),
    ]
    ring.close()
    settle(big)
    for quad in first:
        quad.start()
    settle(out_copies)
    half_rows = out_all.shape[2]
    own_half = out_mid.at[pl.ds(pl.multiple_of(core * half_rows, half_rows), half_rows)]
    keep = [
        pltpu.make_async_copy(
            out_mid.at[pl.ds(side * half_rows, half_rows)],
            out_all.at[mine, side],
            loc.at[10 + side],
        )
        for side in range(2)
    ]
    run(keep)
    sent, passed = [], []
    for step in range(1, size):
        peer = lax.rem(mine + step, size)
        sent.append(
            remote(own_half, out_all.at[mine, core], s5.at[step], r5.at[step], fsdp=peer)
        )
        source = lax.rem(mine + size - step, size)
        passed.append(
            remote(
                out_all.at[source, core],
                out_all.at[source, core],
                s6.at[step],
                r6.at[step],
                sp=other,
            )
        )
    everything = packed_all[...].reshape(width, packed_all.shape[2])
    qkv_own[...] = everything[:, : 2 * group]
    small_own[...] = everything[:, 2 * group :]
    pick = (
        lax.broadcasted_iota(jnp.int32, (8, 128), 0) == lax.broadcasted_iota(jnp.int32, (8, 128), 1)
    ).astype(F32).astype(BF16)
    gains[...] = dot(pick, small_own[...], ((1,), (1,)))

    def first_norm(index, carry):
        at = pl.ds(pl.multiple_of(index * chunk, chunk), chunk)
        value = tokens_all[pl.ds(index * per_chunk, per_chunk)].reshape(chunk, width).astype(F32)
        normal = (value * inverse_rms(value) * gains[0:1, :]).astype(BF16)
        normed_one[at, :] = normal
        proj[at, :] = dot(normal, qkv_own[...], ((1,), (0,)))
        return carry

    lax.fori_loop(0, seq_len // chunk, first_norm, 0)
    for quad in first:
        quad.forward()
    late_ring.forward()
    run(sent)
    for quad in first:
        quad.close()
    for quad in second:
        quad.start()
    attention_kernel(
        proj, cosine, sine, seg_column, seg_row, context, query, key2, value2, sums
    )
    context_ring = ring_columns(context, context_all, s7, r7, loc.at[5])
    context_ring.start()
    late_ring.close()
    for copy, onward in zip(sent, passed):
        copy.wait_recv()
        onward.start()
    context_ring.forward()
    context_ring.close()
    for copy in sent:
        copy.wait_send()
    settle(passed)
    settle(keep)
    for quad in second:
        quad.forward()
    out_own[...] = out_all[pl.ds(2 * me, 2)].reshape(out_own.shape)

    def second_norm(index, carry):
        at = pl.ds(pl.multiple_of(index * chunk, chunk), chunk)
        value = tokens_all[pl.ds(index * per_chunk, per_chunk)].reshape(chunk, width).astype(F32)
        out_full = out_all[...].reshape(width, width)
        value = value + RESIDUAL * dot(context_all[at, :], out_full, ((1,), (0,)))

        @pl.when(index == me // per_chunk)
        def _():
            middle_part[...] = value.reshape(middle_part.shape)

        normed[at, :] = (value * inverse_rms(value) * gains[1:2, :]).astype(BF16)
        return carry

    lax.fori_loop(0, seq_len // chunk, second_norm, 0)
    middle_own[...] = middle_part[lax.rem(me, per_chunk)]
    at_own = pl.ds(pl.multiple_of(me * rows, rows), rows)
    normed_own[...] = normed[at_own, :]
    for quad in second:
        quad.close()

    def weights_of(local, low, high):
        return w_buf[local, :, :, :, low:high].reshape(width, high - low)

    def tokens_block(index, carry):
        at = pl.ds(pl.multiple_of(index * chunk, chunk), chunk)
        rows_in = normed[at, :]
        logits = dot(rows_in, small_own[...], ((1,), (0,)))
        late_rows = late_all[pl.ds(index * per_chunk, per_chunk)].reshape(chunk, width + 128)
        lanes = lax.broadcasted_iota(jnp.int32, logits.shape, 1)
        shown = jnp.where(late_rows[:, width:].astype(F32) > 0, logits, -jnp.inf)
        expo = jnp.exp(shown - jnp.max(shown, -1, keepdims=True))
        gate_rows = expo / jnp.sum(expo, -1, keepdims=True)
        gates[at, :] = gate_rows
        grad_mixed = RESIDUAL * late_rows[:, :width].astype(F32)
        mix = jnp.zeros((chunk, width), F32)
        grad_rows = jnp.zeros((chunk, width), F32)
        extra = jnp.zeros((chunk, 128), F32)
        for local in range(experts):
            expert = lanes == me * experts + local + 2
            gate = jnp.sum(jnp.where(expert, gate_rows, 0.0), -1, keepdims=True)
            pre_act = dot(rows_in, weights_of(local, 0, in_span), ((1,), (0,)))
            gate_part, up_part = pre_act[:, :hidden], pre_act[:, hidden:]
            sigmoid = 1.0 / (1.0 + jnp.exp(-gate_part))
            silu = gate_part * sigmoid
            act = (silu * up_part).astype(BF16)
            acts[local, at, :] = act
            w_out = weights_of(local, in_span, in_span + hidden)
            produced = dot(act, w_out, ((1,), (1,))).astype(BF16).astype(F32)
            mix = mix + gate * produced
            grad_gate = jnp.sum(grad_mixed * produced, -1, keepdims=True)
            extra = extra + jnp.where(expert, gate * grad_gate, 0.0)
            grad_result = (gate * grad_mixed).astype(BF16)
            grad_results[local, at, :] = grad_result
            grad_act = dot(grad_result, w_out, ((1,), (0,)))
            grad_gate_part = grad_act * up_part * sigmoid * (1.0 + gate_part * (1.0 - sigmoid))
            grad_pre = jnp.concatenate([grad_gate_part, grad_act * silu], 1).astype(BF16)
            grad_acts[local, at, :] = grad_pre
            grad_rows = grad_rows + dot(grad_pre, weights_of(local, 0, in_span), ((1,), (1,)))
        mixed[at, :] = mix.astype(BF16)
        for piece in range(per_chunk):
            place = slice(piece * rows, (piece + 1) * rows)
            blocks[index * per_chunk + piece, :, :width] = grad_rows[place].astype(BF16)
            blocks[index * per_chunk + piece, :, width:] = extra[place].astype(BF16)
        return carry

    lax.fori_loop(0, seq_len // chunk, tokens_block, 0)
    scatter = Scatter(blocks, *scatter_parts)
    scatter.start()
    gates_own[...] = gates[at_own, :]
    owners = grads.shape[0]
    share = width // owners
    count = chunk // share

    def weight_tile(index, carry):
        columns = pl.ds(pl.multiple_of(index * chunk, chunk), chunk)
        turned = normed[:, columns]
        for local in range(experts):
            value = dot(turned, grad_acts[local], ((0,), (0,))).astype(BF16)
            grads[pl.ds(index * count, count), local, :, :in_span] = value.reshape(
                count, share, in_span
            )
            value = dot(grad_results[local, :, columns], acts[local], ((0,), (0,))).astype(BF16)
            grads[pl.ds(index * count, count), local, :, in_span:] = value.reshape(
                count, share, hidden
            )
        return carry

    tiles = width // chunk
    lax.fori_loop(0, tiles // 4, weight_tile, 0)
    scatter.middle()
    lax.fori_loop(tiles // 4, tiles // 2, weight_tile, 0)
    scatter.near_blocks()
    lax.fori_loop(tiles // 2, tiles, weight_tile, 0)
    scatter.end(back)


def wide_call(kernel, name, number, inputs, in_specs, outs, out_specs, scratch):
    return pl.pallas_call(
        kernel,
        name=name,
        out_shape=outs,
        in_specs=in_specs,
        out_specs=out_specs,
        scratch_shapes=scratch,
        cost_estimate=pl.CostEstimate(
            flops=2 * 10**10, bytes_accessed=2 * 10**7, transcendentals=0
        ),
        compiler_params=pltpu.CompilerParams(
            collective_id=number, has_side_effects=True, vmem_limit_bytes=60 * 2**20
        ),
    )(*inputs)


def shards(
    tokens,
    segments,
    top_idx,
    cotangent,
    norm1_gain,
    qkv_weight,
    out_weight,
    norm2_gain,
    router_weight,
    expert_in,
    expert_out,
):
    n_sp = lax.axis_size("sp")
    n_fsdp = lax.axis_size("fsdp")
    sp_index = lax.axis_index("sp")
    rows, width = tokens.shape
    seq_len = rows * n_sp
    weight_rows = qkv_weight.shape[0]
    hidden = expert_out.shape[2]
    q_span, k_span = HQ * HEAD_SIZE, KEY_VALUE_HEADS * HEAD_SIZE
    group = q_span // n_sp
    head = k_span // n_sp
    pack_width = 2 * group + 128
    any_shape = jax.ShapeDtypeStruct
    cosine, sine = rope_tables(seq_len)
    seg_row = segments
    n_experts = expert_in.shape[0]
    in_span = expert_in.shape[2]
    slab = any_shape((seq_len, group), BF16)
    (
        _, _, qkv_own, small_own, gains, normed_one, context, query, key2, value2, sums,
        out_own, normed_own, middle_own, gates_own, mixed, back, grads,
    ) = wide_call(
        forward_kernel,
        "forward",
        1,
        (
            tokens, cotangent, top_idx, qkv_weight, norm1_gain[None, :], norm2_gain[None, :],
            router_weight, out_weight, expert_in, expert_out, cosine, sine, seg_row,
        ),
        [HBM] + [VMEM] * 6 + [HBM] * 3 + [VMEM] * 3,
        (
            any_shape((SP * weight_rows, pack_width), BF16),
            any_shape((SP * weight_rows, width), BF16),
            any_shape((width, 2 * group), BF16),
            any_shape((width, 128), BF16),
            any_shape((8, width), F32),
            any_shape((seq_len, width), BF16),
            slab, slab, slab, slab,
            any_shape((seq_len // BLOCK, 2 * BLOCK, 128), F32),
            any_shape((group, width), BF16),
            any_shape((rows, width), BF16),
            any_shape((rows, width), F32),
            any_shape((rows, 128), F32),
            any_shape((seq_len, width), BF16),
            any_shape((rows, width + 128), F32),
            any_shape((n_fsdp, n_experts, width // n_fsdp, in_span + hidden), BF16),
        ),
        (HBM, HBM) + (VMEM,) * 16,
        [
            pltpu.VMEM((SP, weight_rows, pack_width), BF16),
            pltpu.VMEM((rows, width + 128), BF16),
            pltpu.VMEM((SP, rows, width), BF16),
            pltpu.VMEM((SP, rows, width + 128), BF16),
            pltpu.VMEM((n_fsdp, SP * weight_rows, pack_width), BF16),
            pltpu.VMEM((n_fsdp, 2, SP * weight_rows // 2, width), BF16),
            pltpu.VMEM((n_experts, 4, 4, width // n_fsdp, in_span + hidden), BF16),
            pltpu.VMEM((seq_len, width), BF16),
            pltpu.VMEM((seq_len, 2 * group), F32),
            pltpu.VMEM((seq_len, width), BF16),
            pltpu.VMEM((n_experts, seq_len, hidden), BF16),
            pltpu.VMEM((n_experts, seq_len, in_span), BF16),
            pltpu.VMEM((n_experts, seq_len, width), BF16),
            pltpu.VMEM((SP, rows, width + 128), BF16),
            pltpu.VMEM((2, rows, width), F32),
            pltpu.VMEM((seq_len, 128), F32),
            pltpu.VMEM((seq_len, 1), F32),
        ]
        + scatter_scratch(rows, width + 128)
        + [DMA((8,))] * 6
        + [DMA((n_fsdp,))] * 2
        + [DMA((8,))] * 2
        + [DMA((n_fsdp,))] * 4
        + [DMA((8,))] * 2
        + [DMA((12,))]
        + [DMA((4,))] * 8,
    )
    gain_one, gain_two = gains[0:1], gains[1:2]
    share = width // n_fsdp
    shares = group // n_fsdp
    half_grads = (4, share // 2, in_span + hidden)
    half_share = (share // 2, in_span + hidden)
    grad_middle, grad_normed_one, bundle, out_sum, expert_grads, mixed_own = wide_call(
        back_kernel,
        "backward",
        4,
        (
            back, gates_own, normed_own, middle_own, cotangent, gain_two, small_own, out_own,
            context, query, key2, value2, sums, cosine, sine, seg_row, qkv_own,
            normed_one, grads.reshape(4, 4, n_experts, share, in_span + hidden),
            mixed.reshape(SP, rows, width),
        ),
        [VMEM] * 20,
        (
            any_shape((rows, width), F32),
            any_shape((rows, width), F32),
            any_shape((SP, weight_rows, pack_width), F32),
            any_shape((shares, width), F32),
            any_shape((n_experts, share, in_span + hidden), F32),
            any_shape((rows, width), F32),
        ),
        (VMEM,) * 6,
        [
            pltpu.VMEM((rows, width), BF16),
            pltpu.VMEM((SP, rows, width), BF16),
            pltpu.VMEM((seq_len, group), BF16),
            pltpu.VMEM((seq_len, 2 * group), BF16),
            pltpu.VMEM((seq_len, group), F32),
            pltpu.VMEM((seq_len, group), F32),
            pltpu.VMEM((SP, rows, width), BF16),
            pltpu.VMEM((width, 128), F32),
            pltpu.VMEM((4, 4, share, pack_width), BF16),
            pltpu.VMEM((n_fsdp, shares, width), BF16),
            pltpu.VMEM((n_fsdp, shares, width), BF16),
            pltpu.VMEM((SP, weight_rows, pack_width), F32),
            pltpu.VMEM((2,) + half_grads, BF16),
            pltpu.VMEM((2,) + half_grads, BF16),
            pltpu.VMEM((2, 4, share // 4, pack_width), BF16),
            pltpu.VMEM((2, 4, share // 4, pack_width), BF16),
            pltpu.VMEM((seq_len, 1), F32),
        ]
        + scatter_scratch(rows, width) * 2
        + quad_scratch(half_grads) * 2
        + quad_scratch(half_share) * 2
        + quad_scratch((4, share // 4, pack_width)) * 2
        + quad_scratch((share // 4, pack_width)) * 2
        + [DMA((8,))] * 2
        + [DMA((n_fsdp,))] * 2
        + [DMA((8,))] * 2
        + [DMA((4,))],
    )
    block_out = middle_own + RESIDUAL * mixed_own
    moves = []
    for f in range(n_fsdp):
        for s in range(n_sp):
            moves.append((f * n_sp + s, (s * group + f * shares) // weight_rows))
    if shares == weight_rows:
        out_grad = lax.ppermute(out_sum, ("fsdp", "sp"), moves)
    else:
        whole = lax.all_gather(out_sum, ("fsdp", "sp"), axis=0, tiled=False)
        whole = whole.reshape(n_fsdp, n_sp, shares, width).transpose(1, 0, 2, 3)
        device = lax.axis_index("fsdp") * n_sp + sp_index
        out_grad = lax.dynamic_slice_in_dim(
            whole.reshape(width, width), device * weight_rows, weight_rows, 0
        )

    qkv_grad = jnp.concatenate(
        [
            bundle[:, :, :group].transpose(1, 0, 2).reshape(weight_rows, q_span),
            bundle[:, :, group : group + head].transpose(1, 0, 2).reshape(weight_rows, k_span),
            bundle[:, :, group + head : 2 * group].transpose(1, 0, 2).reshape(weight_rows, k_span),
        ],
        1,
    )
    smalls = jnp.sum(bundle[:, :, 2 * group :], 0)
    gain_two_grad = smalls[:, 1]
    router_grad = smalls[:, 2 : 2 + E]
    gain_one_grad = jnp.sum(qkv_grad * qkv_weight.astype(F32), 1) / norm1_gain.astype(F32)
    hidden_own = tokens.astype(F32)
    input_grad = grad_middle + rms_backward(
        grad_normed_one, hidden_own, inverse_rms(hidden_own), gain_one
    )
    return (
        block_out,
        input_grad,
        gain_one_grad,
        qkv_grad,
        out_grad,
        gain_two_grad,
        router_grad,
        expert_grads[:, :, :in_span],
        expert_grads[:, :, in_span:],
    )


def solution(mesh):
    both = P(("fsdp", "sp"), None)
    flat = P(("fsdp", "sp"))
    expert = P("sp", "fsdp", None)
    return jax.shard_map(
        shards,
        mesh=mesh,
        in_specs=(both, P("fsdp", None), both, both, flat, both, both, flat, both, expert, expert),
        out_specs=(both, both, flat, both, both, flat, both, expert, expert),
        check_vma=False,
    )
```

```python
import jax
import jax.numpy as jnp
import numpy as np
from jax import lax
from jax.experimental import pallas as pl
from jax.experimental.pallas import tpu as pltpu
from jax.sharding import PartitionSpec as P

HQ = 16
KEY_VALUE_HEADS = 8
HEAD_SIZE = 64
E = 16
EPSILON = 1e-06
RESIDUAL = 0.22
BLOCK = 256
LONGEST = 512
BF16 = jnp.bfloat16
F32 = jnp.float32


def rope_tables(count):
    frequency = np.float32(10000.0) ** (
        np.float32(-2.0) * np.arange(HEAD_SIZE // 2, dtype=np.float32) / np.float32(HEAD_SIZE)
    )
    angles = np.arange(count, dtype=np.float32)[:, None] * frequency.astype(np.float32)[None, :]
    cosine = np.cos(angles).astype(np.float32)
    sine = np.sin(angles).astype(np.float32)
    return np.concatenate([cosine] * 4, 1), np.concatenate([-sine, sine] * 2, 1)


def dot(left, right, contract):
    return lax.dot_general(left, right, (contract, ((), ())), preferred_element_type=F32)


def inverse_rms(value):
    return lax.rsqrt(jnp.mean(value * value, -1, keepdims=True) + EPSILON)


def rms_backward(grad, value, inverse, gain):
    scaled = grad * gain
    return inverse * scaled - value * (inverse**3) * jnp.mean(scaled * value, -1, keepdims=True)


MESH = pl.DeviceIdType.MESH
VMEM = pl.BlockSpec(memory_space=pltpu.VMEM)
HBM = pl.BlockSpec(memory_space=pl.ANY)
DMA = pltpu.SemaphoreType.DMA
SP, FSDP = 8, 16


def remote(src, dst, send, recv, **device):
    return pltpu.make_async_remote_copy(
        src_ref=src,
        dst_ref=dst,
        send_sem=send,
        recv_sem=recv,
        device_id=device,
        device_id_type=MESH,
    )


def meet(with_fsdp):
    barrier = pltpu.get_barrier_semaphore()
    me = lax.axis_index("sp")
    for step in range(1, SP):
        pl.semaphore_signal(
            barrier, inc=1, device_id={"sp": lax.rem(me + step, SP)}, device_id_type=MESH
        )
    count = SP - 1
    if with_fsdp:
        size = lax.axis_size("fsdp")
        mine = lax.axis_index("fsdp")
        for step in range(1, size):
            pl.semaphore_signal(
                barrier, inc=1, device_id={"fsdp": lax.rem(mine + step, size)}, device_id_type=MESH
            )
        count += size - 1
    pl.semaphore_wait(barrier, count)


def places():
    me = lax.axis_index("sp")
    level, core = me // 2, lax.rem(me, 2)
    up = lax.rem(level + 1, 4)
    down = lax.rem(level + 3, 4)
    far = lax.rem(level + 2, 4)
    return me, core, level, up, down, far


class Ring:
    def __init__(self, source, slot, part, send, recv, local):
        me, core, level, up, down, far = places()
        self.me = me
        up_id, down_id, far_id = up * 2 + core, down * 2 + core, far * 2 + core
        other = level * 2 + (1 - core)

        def go(src, dst, number, peer):
            return remote(src, dst, send.at[number], recv.at[number], sp=peer)

        self.first = [
            go(source, slot(me), 0, up_id),
            go(source, slot(me), 1, down_id),
            go(source, slot(me), 2, other),
        ]
        self.local = pltpu.make_async_copy(source, slot(me), local)
        self.next_up = [
            go(part(down_id, 0), part(down_id, 0), 3, up_id),
            go(slot(down_id), slot(down_id), 4, other),
        ]
        self.next_down = [
            go(part(up_id, 1), part(up_id, 1), 5, down_id),
            go(slot(up_id), slot(up_id), 6, other),
        ]
        self.last = go(slot(far_id), slot(far_id), 7, other)

    def start(self):
        for copy in self.first:
            copy.start()
        self.local.start()

    def forward(self):
        self.first[0].wait_recv()
        for copy in self.next_up:
            copy.start()
        self.first[1].wait_recv()
        for copy in self.next_down:
            copy.start()

    def close(self):
        self.next_up[0].wait_recv()
        self.next_down[0].wait_recv()
        self.last.start()
        self.local.wait()
        for copy in (self.first[0], self.first[1], self.next_up[0], self.next_down[0]):
            copy.wait_send()
        for copy in (self.first[2], self.next_up[1], self.next_down[1], self.last):
            copy.wait()

    def finish(self):
        self.forward()
        self.close()


def ring_rows(source, target, send, recv, local):
    half = source.shape[0] // 2
    return Ring(
        source,
        lambda index: target.at[index],
        lambda index, side: target.at[index, pl.ds(side * half, half)],
        send,
        recv,
        local,
    )


def ring_columns(source, target, send, recv, local):
    rows, wide = source.shape
    half = rows // 2

    def columns(index):
        return pl.ds(pl.multiple_of(index * wide, wide), wide)

    return Ring(
        source,
        lambda index: target.at[:, columns(index)],
        lambda index, side: target.at[pl.ds(side * half, half), columns(index)],
        send,
        recv,
        local,
    )


def spread(axis, size, source, target, send, recv, local, blocks, place=None):
    me = lax.axis_index(axis)
    landing = target.at[me] if place is None else place(me)
    copies = []
    for step in range(1, size):
        peer = lax.rem(me + step, size)
        copies.append(
            remote(
                source.at[peer] if blocks else source,
                landing,
                send.at[step],
                recv.at[step],
                **{axis: peer},
            )
        )
    copies.append(pltpu.make_async_copy(source.at[me] if blocks else source, landing, local))
    return copies


def run(copies):
    for copy in copies:
        copy.start()


def settle(copies):
    for copy in copies:
        copy.wait()


class Scatter:
    def __init__(self, blocks, other_sums, sums, near, far_parts, send, recv):
        me, core, level, up, down, far = places()
        other = level * 2 + (1 - core)
        self.blocks, self.other_sums, self.sums = blocks, other_sums, sums
        self.near, self.far_parts = near, far_parts
        self.core, self.level, self.up, self.down, self.far = core, level, up, down, far
        half = blocks.shape[1] // 2
        self.half = half
        up_id, down_id = up * 2 + core, down * 2 + core

        def go(src, dst, number, peer):
            return remote(src, dst, send.at[number], recv.at[number], sp=peer)

        order = (far, up, down, level)
        self.pair = [
            go(blocks.at[at * 2 + (1 - core)], other_sums.at[number], number, other)
            for number, at in enumerate(order)
        ]
        self.to_up = go(sums.at[0, pl.ds(0, half)], far_parts.at[0], 4, up_id)
        self.to_down = go(sums.at[0, pl.ds(half, half)], far_parts.at[1], 5, down_id)
        self.full_up = go(sums.at[1], near.at[0], 6, up_id)
        self.full_down = go(sums.at[2], near.at[1], 7, down_id)

    def start(self):
        run(self.pair)

    def both(self, number, at):
        mine = self.blocks[at * 2 + self.core].astype(F32)
        return mine + self.other_sums[number].astype(F32)

    def middle(self):
        self.pair[0].wait_recv()
        self.sums[0] = self.both(0, self.far).astype(BF16)
        self.to_up.start()
        self.to_down.start()

    def near_blocks(self):
        half = self.half
        self.pair[1].wait_recv()
        self.to_up.wait_recv()
        total = self.both(1, self.up)
        self.sums[1, :half] = (total[:half] + self.far_parts[0].astype(F32)).astype(BF16)
        self.sums[1, half:] = total[half:].astype(BF16)
        self.full_up.start()
        self.pair[2].wait_recv()
        self.to_down.wait_recv()
        total = self.both(2, self.down)
        self.sums[2, :half] = total[:half].astype(BF16)
        self.sums[2, half:] = (total[half:] + self.far_parts[1].astype(F32)).astype(BF16)
        self.full_down.start()

    def end(self, out):
        self.pair[3].wait_recv()
        total = self.both(3, self.level)
        self.full_up.wait_recv()
        total = total + self.near[0].astype(F32)
        self.full_down.wait_recv()
        out[...] = total + self.near[1].astype(F32)
        for copy in self.pair + [self.to_up, self.to_down, self.full_up, self.full_down]:
            copy.wait_send()

    def finish(self, out):
        self.middle()
        self.near_blocks()
        self.end(out)


def scatter_scratch(rows, width):
    return [
        pltpu.VMEM((4, rows, width), BF16),
        pltpu.VMEM((3, rows, width), BF16),
        pltpu.VMEM((2, rows, width), BF16),
        pltpu.VMEM((2, rows // 2, width), BF16),
        DMA((8,)),
        DMA((8,)),
    ]


class Quad:
    def __init__(self, axis, source, far_parts, near, sums, send, recv):
        mine = lax.axis_index("fsdp")
        y, x = mine // 4, lax.rem(mine, 4)
        here = x if axis == "x" else y
        self.source, self.far_parts, self.near, self.sums = source, far_parts, near, sums
        self.here = here
        self.up, self.down, self.far = (lax.rem(here + step, 4) for step in (1, 3, 2))

        def device(place):
            return y * 4 + place if axis == "x" else place * 4 + x

        def go(src, dst, number, place):
            return remote(src, dst, send.at[number], recv.at[number], fsdp=device(place))

        self.far_up = go(source(self.far, 0), far_parts.at[0], 0, self.up)
        self.far_down = go(source(self.far, 1), far_parts.at[1], 1, self.down)
        self.plain_up = go(source(self.up, 1), near.at[0, 1], 2, self.up)
        self.plain_down = go(source(self.down, 0), near.at[1, 0], 3, self.down)
        self.sum_up = go(sums.at[0], near.at[0, 0], 4, self.up)
        self.sum_down = go(sums.at[1], near.at[1, 1], 5, self.down)

    def start(self):
        run((self.far_up, self.far_down, self.plain_up, self.plain_down))

    def near_blocks(self):
        self.far_up.wait_recv()
        total = self.source(self.up, 0)[...].astype(F32) + self.far_parts[0].astype(F32)
        self.sums[0] = total.astype(BF16)
        self.sum_up.start()
        self.far_down.wait_recv()
        total = self.source(self.down, 1)[...].astype(F32) + self.far_parts[1].astype(F32)
        self.sums[1] = total.astype(BF16)
        self.sum_down.start()

    def end(self, store):
        for copy in (self.plain_up, self.plain_down, self.sum_up, self.sum_down):
            copy.wait_recv()
        for side in range(2):
            total = self.source(self.here, side)[...].astype(F32)
            total = total + self.near[0, side].astype(F32) + self.near[1, side].astype(F32)
            store(side, total)
        for copy in (
            self.far_up, self.far_down, self.plain_up, self.plain_down, self.sum_up, self.sum_down
        ):
            copy.wait_send()


def quad_scratch(shape):
    return [
        pltpu.VMEM((2,) + shape, BF16),
        pltpu.VMEM((2, 2) + shape, BF16),
        pltpu.VMEM((2,) + shape, BF16),
        DMA((6,)),
        DMA((6,)),
    ]


def exact_dot(left, right, contract):
    return lax.dot_general(
        left, right, (contract, ((), ())), precision=lax.Precision.HIGHEST,
        preferred_element_type=F32,
    )


def back_kernel(
    back, gates, normed, middle, tokens, cotangent, gain, small, out_own, context,
    query, key2, value2, sums, cosine, sine, seg_row, qkv_own, normed_one,
    grads, mixed,
    block_out, input_grad, bundle_all, out_sum, expert_grads,
    grad_middle, grad_normed_one, mixed_own, attended, attended_all, grad_context, grad_proj, grad_key, grad_value, blocks, small_part,
    bundle, outp, out_in, bundle_sum, halves_a, halves_b, hold_a, hold_b,
    seg_column,
    *scratch,
):
    scratch = list(scratch)

    def take(count):
        taken = scratch[:count]
        del scratch[:count]
        return taken

    mix_scatter = Scatter(mixed, *take(6))
    scatter = Scatter(blocks, *take(6))

    def half_a(index, side):
        return grads.at[:, index, 0, pl.ds(side * half, half)]

    def half_b(index, side):
        return grads.at[index, :, 1, pl.ds(side * half, half)]

    half = grads.shape[3] // 2
    first_a = Quad("x", half_a, *take(5))
    first_b = Quad("y", half_b, *take(5))
    second_a = Quad("y", lambda index, side: halves_a.at[side, index], *take(5))
    second_b = Quad("x", lambda index, side: halves_b.at[side, index], *take(5))
    quarter = bundle.shape[2] // 4

    def bundle_a(index, side):
        return bundle.at[:, index, pl.ds(side * quarter, quarter)]

    def bundle_b(index, side):
        return bundle.at[index, :, pl.ds((2 + side) * quarter, quarter)]

    bundle_first = [Quad("x", bundle_a, *take(5)), Quad("y", bundle_b, *take(5))]
    bundle_second = [
        Quad("y", lambda index, side: hold_a.at[side, index], *take(5)),
        Quad("x", lambda index, side: hold_b.at[side, index], *take(5)),
    ]

    def keep_bundle(hold):
        def store(side, total):
            hold[side] = total.astype(BF16)

        return store

    def store_bundle(first_row):
        def store(side, total):
            groups = quarter // bundle_sum.shape[1]
            start = (first_row + side * quarter) // bundle_sum.shape[1]
            bundle_sum[start : start + groups] = total.reshape(
                groups, bundle_sum.shape[1], total.shape[1]
            )

        return store

    ring_send, ring_recv, s2, r2, s3, r3, loc = take(7)

    def keep_a(side, total):
        halves_a[side] = total.astype(BF16)

    def keep_b(side, total):
        halves_b[side] = total.astype(BF16)

    meet(True)
    size = lax.axis_size("fsdp")
    first_a.start()
    first_b.start()
    fill_column(seg_row, seg_column)
    width = cotangent.shape[1]
    value = middle[...]
    inverse = inverse_rms(value)
    weighted = back[:, width:]
    grad_logits = weighted - gates[...] * jnp.sum(weighted, -1, keepdims=True)
    grad_normed = back[:, :width] + exact_dot(grad_logits, small[...].astype(F32), ((1,), (1,)))
    grad_rows = cotangent[...].astype(F32) + rms_backward(
        grad_normed, value, inverse, gain[1:2, :]
    )
    grad_middle[...] = grad_rows
    attended[...] = (RESIDUAL * grad_rows).astype(BF16)
    ring = ring_rows(attended, attended_all, ring_send, ring_recv, loc.at[0])
    ring.start()
    gain_lane = lax.broadcasted_iota(jnp.int32, grad_logits.shape, 1) == 1
    small_part[...] = exact_dot(normed[...].astype(F32), grad_logits, ((0,), (0,))) + exact_dot(
        grad_normed * value * inverse, gain_lane.astype(F32), ((0,), (0,))
    )
    ring.finish()
    mix_scatter.start()
    first_a.near_blocks()
    first_b.near_blocks()
    rows = attended.shape[0]
    for index in range(SP):
        at = slice(index * rows, (index + 1) * rows)
        grad_context[at, :] = dot(attended_all[index], out_own[...], ((1,), (1,))).astype(BF16)
    out_part = jnp.zeros((context.shape[1], width), F32)
    for index in range(SP):
        at = slice(index * rows, (index + 1) * rows)
        out_part = out_part + dot(context[at, :], attended_all[index], ((0,), (0,)))
    outp[...] = out_part.astype(BF16).reshape(outp.shape)
    outs = spread("fsdp", size, outp, out_in, s2, r2, loc.at[1], True)
    run(outs)
    mix_scatter.middle()
    attention_back_kernel(
        query, key2, value2, sums, grad_context, cosine, sine, seg_column, seg_row,
        grad_proj, grad_key, grad_value,
    )
    mix_scatter.near_blocks()
    span = grad_proj.shape[1]
    share = bundle.shape[2]
    tile = 4 * share
    for index in range(width // tile):
        at = slice(index * tile, (index + 1) * tile)
        part = dot(normed_one[:, at], grad_proj[...], ((0,), (0,))).astype(BF16)
        bundle[index, :, :, :span] = part.reshape(tile // share, share, span)
        bundle[index, :, :, span:] = (
            small_part[at, :].astype(BF16).reshape(tile // share, share, 128)
        )
    for quad in bundle_first:
        quad.start()
    for index in range(SP):
        at = slice(index * rows, (index + 1) * rows)
        blocks[index] = dot(grad_proj[at, :], qkv_own[...], ((1,), (1,))).astype(BF16)
    scatter.start()
    for quad in bundle_first:
        quad.near_blocks()
    first_a.end(keep_a)
    first_b.end(keep_b)
    scatter.middle()
    bundle_first[0].end(keep_bundle(hold_a))
    bundle_first[1].end(keep_bundle(hold_b))
    for quad in bundle_second:
        quad.start()
    second_a.start()
    second_b.start()
    mix_scatter.end(mixed_own)
    block_out[...] = middle[...] + RESIDUAL * mixed_own[...]
    for quad in bundle_second:
        quad.near_blocks()
    scatter.near_blocks()
    bundle_second[0].end(store_bundle(0))
    bundle_second[1].end(store_bundle(2 * quarter))
    shares = spread("sp", SP, bundle_sum, bundle_all, s3, r3, loc.at[3], True)
    run(shares)
    second_a.near_blocks()
    second_b.near_blocks()
    settle(outs)
    total = out_in[0].astype(F32)
    for index in range(1, size):
        total = total + out_in[index].astype(F32)
    out_sum[...] = total

    def store_a(side, total):
        expert_grads[0, side * half : (side + 1) * half, :] = total

    def store_b(side, total):
        expert_grads[1, side * half : (side + 1) * half, :] = total

    second_a.end(store_a)
    second_b.end(store_b)
    scatter.end(grad_normed_one)
    value = tokens[...].astype(F32)
    input_grad[...] = grad_middle[...] + rms_backward(
        grad_normed_one[...], value, inverse_rms(value), gain[0:1, :]
    )
    settle(shares)


def swap_halves(value):
    wide = value.shape[-1]
    lane = lax.broadcasted_iota(jnp.int32, value.shape, 1)
    return jnp.where(
        lane % HEAD_SIZE < HEAD_SIZE // 2,
        pltpu.roll(value, wide - HEAD_SIZE // 2, 1),
        pltpu.roll(value, HEAD_SIZE // 2, 1),
    )


def first_head(shape):
    return lax.broadcasted_iota(jnp.int32, shape, 1) < HEAD_SIZE


def stack_heads(slab):
    is_first = first_head(slab.shape)
    zero = jnp.zeros_like(slab)
    return jnp.concatenate([jnp.where(is_first, slab, zero), jnp.where(is_first, zero, slab)], 0)


def merge_heads(stacked):
    half = stacked.shape[0] // 2
    return jnp.where(first_head((half, stacked.shape[1])), stacked[:half], stacked[half:])


def row_to_column(row):
    count = row.shape[1]
    same = lax.broadcasted_iota(jnp.int32, (count, count), 0) == lax.broadcasted_iota(
        jnp.int32, (count, count), 1
    )
    spread_row = jnp.broadcast_to(row.astype(F32), (count, count))
    return jnp.sum(jnp.where(same, spread_row, 0.0), 1, keepdims=True)


def fill_column(seg_row, seg_column):
    for index in range(seg_row.shape[1] // 128):
        at = slice(index * 128, (index + 1) * 128)
        seg_column[at, :] = row_to_column(seg_row[:, at])


def block_scores(block, query2, key2, seg_column, seg_row):
    lo, hi = block * BLOCK, (block + 1) * BLOCK
    k_lo = max(0, lo - LONGEST)
    rows = lo + lax.broadcasted_iota(jnp.int32, (BLOCK, hi - k_lo), 0)
    keys = k_lo + lax.broadcasted_iota(jnp.int32, (BLOCK, hi - k_lo), 1)
    allowed = (keys <= rows) & (
        seg_column[lo:hi, :] == seg_row[:, k_lo:hi].astype(F32)
    )
    scores = dot(query2, key2[k_lo:hi, :], ((1,), (1,))) * HEAD_SIZE**-0.5
    return jnp.where(jnp.concatenate([allowed, allowed], 0), scores, -jnp.inf)


def attention_kernel(
    proj, cosine, sine, seg_column, seg_row, context, query, key2, value2, sums
):
    cos_rows, sin_rows = cosine[...], sine[...]
    slab = proj[:, :128]
    query[...] = (slab * cos_rows + swap_halves(slab) * sin_rows).astype(BF16)
    slab = proj[:, 128:]
    is_first = first_head(slab.shape)
    turned = slab * cos_rows + swap_halves(slab) * sin_rows
    key2[...] = jnp.where(is_first, turned, pltpu.roll(turned, HEAD_SIZE, 1)).astype(BF16)
    value2[...] = jnp.where(is_first, pltpu.roll(slab, HEAD_SIZE, 1), slab).astype(BF16)
    for block in range(proj.shape[0] // BLOCK):
        lo, hi = block * BLOCK, (block + 1) * BLOCK
        k_lo = max(0, lo - LONGEST)
        scores = block_scores(block, stack_heads(query[lo:hi, :]), key2, seg_column, seg_row)
        top = jnp.max(scores, -1, keepdims=True)
        expo = jnp.exp(scores - top)
        total = jnp.sum(expo, -1, keepdims=True)
        probs = (expo / total).astype(BF16)
        context[lo:hi, :] = merge_heads(dot(probs, value2[k_lo:hi, :], ((1,), (0,)))).astype(BF16)
        sums[block] = jnp.broadcast_to(top + jnp.log(total), (2 * BLOCK, 128))


def attention_back_kernel(
    query, key2, value2, sums, grad_context, cosine, sine, seg_column, seg_row,
    grad_proj, grad_key, grad_value,
):
    grad_key[...] = jnp.zeros_like(grad_key)
    grad_value[...] = jnp.zeros_like(grad_value)
    for block in range(query.shape[0] // BLOCK):
        lo, hi = block * BLOCK, (block + 1) * BLOCK
        k_lo = max(0, lo - LONGEST)
        query2 = stack_heads(query[lo:hi, :])
        scores = block_scores(block, query2, key2, seg_column, seg_row)
        probs = jnp.exp(scores - sums[block][:, :1])
        grad_rows = stack_heads(grad_context[lo:hi, :])
        grad_probs = dot(grad_rows, value2[k_lo:hi, :], ((1,), (1,)))
        row_dot = jnp.sum(grad_probs * probs, -1, keepdims=True)
        grad_scores = (probs * (grad_probs - row_dot) * HEAD_SIZE**-0.5).astype(BF16)
        moved = merge_heads(dot(grad_scores, key2[k_lo:hi, :], ((1,), (0,))))
        moved = moved.astype(BF16).astype(F32)
        grad_proj[lo:hi, :128] = (
            moved * cosine[lo:hi, :] - swap_halves(moved) * sine[lo:hi, :]
        ).astype(BF16)
        grad_key[k_lo:hi, :] += dot(grad_scores, query2, ((0,), (0,)))
        grad_value[k_lo:hi, :] += dot(probs.astype(BF16), grad_rows, ((0,), (0,)))
    is_first = first_head(grad_key.shape)
    moved = grad_key[...]
    moved = (moved + pltpu.roll(moved, HEAD_SIZE, 1)).astype(BF16).astype(F32)
    moved = moved * cosine[...] - swap_halves(moved) * sine[...]
    other = grad_value[...]
    other = other + pltpu.roll(other, HEAD_SIZE, 1)
    grad_proj[:, 128:] = jnp.where(is_first, moved, other).astype(BF16)


class QuadGather:
    def __init__(self, axis, block, part, send, recv):
        mine = lax.axis_index("fsdp")
        y, x = mine // 4, lax.rem(mine, 4)
        here = x if axis == "x" else y
        up, down = lax.rem(here + 1, 4), lax.rem(here + 3, 4)

        def go(ref, number, place):
            device = y * 4 + place if axis == "x" else place * 4 + x
            return remote(ref, ref, send.at[number], recv.at[number], fsdp=device)

        self.own = [go(block(here), 0, up), go(block(here), 1, down)]
        self.onward = [go(part(down, 0), 2, up), go(part(up, 1), 3, down)]

    def start(self):
        run(self.own)

    def forward(self):
        for came, onward in zip(self.own, self.onward):
            came.wait_recv()
            onward.start()

    def close(self):
        for copy in self.onward:
            copy.wait_recv()
        for copy in self.own + self.onward:
            copy.wait_send()


def forward_kernel(
    tokens, cotangent, top_idx, qkv, gain_one, gain_two, router, outw, expert_in, expert_out,
    cosine, sine, seg_row,
    mid, out_mid, qkv_own, small_own, gains, normed_one, context, query, key2, value2, sums,
    out_own, normed_own, middle_own, gates_own, mixed, back, grads,
    packed, late, tokens_all, late_all, packed_all, out_all, w_buf, context_all, proj, normed,
    acts, grad_acts, grad_results, blocks, middle_part, gates, seg_column,
    *scratch,
):
    scratch = list(scratch)

    def take(count):
        taken = scratch[:count]
        del scratch[:count]
        return taken

    scatter_parts = take(6)
    (s0, r0, s1, r1, s2, r2, s3, r3, s4, r4, s5, r5, s6, r6, s7, r7, loc) = take(17)
    quad_sems = take(8)
    group, q_span = 2 * HEAD_SIZE, HQ * HEAD_SIZE
    k_span = KEY_VALUE_HEADS * HEAD_SIZE
    me, core, level, up, down, far = places()
    size = lax.axis_size("fsdp")
    mine = lax.axis_index("fsdp")
    y, x = mine // 4, lax.rem(mine, 4)
    other = level * 2 + (1 - core)
    experts = expert_in.shape[0]
    in_span, hidden = expert_in.shape[2], expert_out.shape[2]
    rows, width = cotangent.shape
    seq_len = normed.shape[0]
    chunk = 256
    per_chunk = chunk // rows

    shard_copies = []
    for local in range(experts):
        shard_copies += [
            pltpu.make_async_copy(
                expert_in.at[local], w_buf.at[local, y, x, :, pl.ds(0, in_span)], loc.at[6 + local]
            ),
            pltpu.make_async_copy(
                expert_out.at[local],
                w_buf.at[local, y, x, :, pl.ds(in_span, hidden)],
                loc.at[8 + local],
            ),
        ]
    run(shard_copies)
    fill_column(seg_row, seg_column)
    lanes = lax.broadcasted_iota(jnp.int32, (qkv.shape[0], 128), 1)
    shift = (
        lax.broadcasted_iota(jnp.int32, (E, 128), 0) + 2
        == lax.broadcasted_iota(jnp.int32, (E, 128), 1)
    ).astype(F32).astype(BF16)
    small = dot(router[...], shift, ((1,), (0,)))
    small = small + jnp.where(lanes == 0, row_to_column(gain_one[...]), 0.0)
    small = small + jnp.where(lanes == 1, row_to_column(gain_two[...]), 0.0)
    small = small.astype(BF16)
    for index in range(SP):
        k_at = q_span + index * HEAD_SIZE
        packed[index, :, :group] = qkv[:, index * group : (index + 1) * group]
        packed[index, :, group : 2 * group] = jnp.concatenate(
            [
                qkv[:, k_at : k_at + HEAD_SIZE],
                qkv[:, k_at + k_span : k_at + k_span + HEAD_SIZE],
            ],
            1,
        )
        packed[index, :, 2 * group :] = small
    own_rows = packed.shape[1]

    def rows_of(target):
        return lambda index: target.at[pl.ds(pl.multiple_of(index * own_rows, own_rows), own_rows)]

    meet(True)
    small_copies = spread("sp", SP, packed, mid, s1, r1, loc.at[0], True, rows_of(mid))
    run(small_copies)
    ring = ring_rows(tokens, tokens_all, s0, r0, loc.at[1])
    ring.start()
    out_copies = spread("sp", SP, outw, out_mid, s2, r2, loc.at[2], False, rows_of(out_mid))
    run(out_copies)
    late[:, :width] = cotangent[...]
    lane = lax.broadcasted_iota(jnp.int32, (rows, 128), 1)
    chosen = jnp.zeros(lane.shape, F32)
    for choice in range(top_idx.shape[1]):
        chosen = jnp.where(lane == top_idx[:, choice : choice + 1] + 2, 1.0, chosen)
    late[:, width:] = chosen.astype(BF16)
    settle(small_copies)
    big = spread("fsdp", size, mid, packed_all, s3, r3, loc.at[3], False)
    run(big)
    ring.forward()
    late_ring = ring_rows(late, late_all, s4, r4, loc.at[4])
    late_ring.start()
    settle(shard_copies)
    first = [
        QuadGather(
            "x",
            lambda index: w_buf.at[0, y, index],
            lambda index, side: w_buf.at[0, y, index, pl.ds(side * 32, 32)],
            *quad_sems[0:2],
        ),
        QuadGather(
            "y",
            lambda index: w_buf.at[1, index, x],
            lambda index, side: w_buf.at[1, index, x, pl.ds(side * 32, 32)],
            *quad_sems[2:4],
        ),
    ]
    second = [
        QuadGather(
            "y",
            lambda index: w_buf.at[0, index],
            lambda index, side: w_buf.at[0, index, pl.ds(side * 2, 2)],
            *quad_sems[4:6],
        ),
        QuadGather(
            "x",
            lambda index: w_buf.at[1, :, index],
            lambda index, side: w_buf.at[1, pl.ds(side * 2, 2), index],
            *quad_sems[6:8],
        ),
    ]
    ring.close()
    settle(big)
    for quad in first:
        quad.start()
    settle(out_copies)
    half_rows = out_all.shape[2]
    own_half = out_mid.at[pl.ds(pl.multiple_of(core * half_rows, half_rows), half_rows)]
    keep = [
        pltpu.make_async_copy(
            out_mid.at[pl.ds(side * half_rows, half_rows)],
            out_all.at[mine, side],
            loc.at[10 + side],
        )
        for side in range(2)
    ]
    run(keep)
    sent, passed = [], []
    for step in range(1, size):
        peer = lax.rem(mine + step, size)
        sent.append(
            remote(own_half, out_all.at[mine, core], s5.at[step], r5.at[step], fsdp=peer)
        )
        source = lax.rem(mine + size - step, size)
        passed.append(
            remote(
                out_all.at[source, core],
                out_all.at[source, core],
                s6.at[step],
                r6.at[step],
                sp=other,
            )
        )
    everything = packed_all[...].reshape(width, packed_all.shape[2])
    qkv_own[...] = everything[:, : 2 * group]
    small_own[...] = everything[:, 2 * group :]
    pick = (
        lax.broadcasted_iota(jnp.int32, (8, 128), 0) == lax.broadcasted_iota(jnp.int32, (8, 128), 1)
    ).astype(F32).astype(BF16)
    gains[...] = dot(pick, small_own[...], ((1,), (1,)))

    def first_norm(index, carry):
        at = pl.ds(pl.multiple_of(index * chunk, chunk), chunk)
        value = tokens_all[pl.ds(index * per_chunk, per_chunk)].reshape(chunk, width).astype(F32)
        normal = (value * inverse_rms(value) * gains[0:1, :]).astype(BF16)
        normed_one[at, :] = normal
        proj[at, :] = dot(normal, qkv_own[...], ((1,), (0,)))
        return carry

    lax.fori_loop(0, seq_len // chunk, first_norm, 0)
    for quad in first:
        quad.forward()
    late_ring.forward()
    run(sent)
    for quad in first:
        quad.close()
    for quad in second:
        quad.start()
    attention_kernel(
        proj, cosine, sine, seg_column, seg_row, context, query, key2, value2, sums
    )
    context_ring = ring_columns(context, context_all, s7, r7, loc.at[5])
    context_ring.start()
    late_ring.close()
    for copy, onward in zip(sent, passed):
        copy.wait_recv()
        onward.start()
    context_ring.forward()
    context_ring.close()
    for copy in sent:
        copy.wait_send()
    settle(passed)
    settle(keep)
    for quad in second:
        quad.forward()
    out_own[...] = out_all[pl.ds(2 * me, 2)].reshape(out_own.shape)

    def second_norm(index, carry):
        at = pl.ds(pl.multiple_of(index * chunk, chunk), chunk)
        value = tokens_all[pl.ds(index * per_chunk, per_chunk)].reshape(chunk, width).astype(F32)
        out_full = out_all[...].reshape(width, width)
        value = value + RESIDUAL * dot(context_all[at, :], out_full, ((1,), (0,)))

        @pl.when(index == me // per_chunk)
        def _():
            middle_part[...] = value.reshape(middle_part.shape)

        normed[at, :] = (value * inverse_rms(value) * gains[1:2, :]).astype(BF16)
        return carry

    lax.fori_loop(0, seq_len // chunk, second_norm, 0)
    middle_own[...] = middle_part[lax.rem(me, per_chunk)]
    at_own = pl.ds(pl.multiple_of(me * rows, rows), rows)
    normed_own[...] = normed[at_own, :]
    for quad in second:
        quad.close()

    def weights_of(local, low, high):
        return w_buf[local, :, :, :, low:high].reshape(width, high - low)

    def tokens_block(index, carry):
        at = pl.ds(pl.multiple_of(index * chunk, chunk), chunk)
        rows_in = normed[at, :]
        logits = dot(rows_in, small_own[...], ((1,), (0,)))
        late_rows = late_all[pl.ds(index * per_chunk, per_chunk)].reshape(chunk, width + 128)
        lanes = lax.broadcasted_iota(jnp.int32, logits.shape, 1)
        shown = jnp.where(late_rows[:, width:].astype(F32) > 0, logits, -jnp.inf)
        expo = jnp.exp(shown - jnp.max(shown, -1, keepdims=True))
        gate_rows = expo / jnp.sum(expo, -1, keepdims=True)
        gates[at, :] = gate_rows
        grad_mixed = RESIDUAL * late_rows[:, :width].astype(F32)
        mix = jnp.zeros((chunk, width), F32)
        grad_rows = jnp.zeros((chunk, width), F32)
        extra = jnp.zeros((chunk, 128), F32)
        for local in range(experts):
            expert = lanes == me * experts + local + 2
            gate = jnp.sum(jnp.where(expert, gate_rows, 0.0), -1, keepdims=True)
            pre_act = dot(rows_in, weights_of(local, 0, in_span), ((1,), (0,)))
            gate_part, up_part = pre_act[:, :hidden], pre_act[:, hidden:]
            sigmoid = 1.0 / (1.0 + jnp.exp(-gate_part))
            silu = gate_part * sigmoid
            act = (silu * up_part).astype(BF16)
            acts[local, at, :] = act
            w_out = weights_of(local, in_span, in_span + hidden)
            produced = dot(act, w_out, ((1,), (1,))).astype(BF16).astype(F32)
            mix = mix + gate * produced
            grad_gate = jnp.sum(grad_mixed * produced, -1, keepdims=True)
            extra = extra + jnp.where(expert, gate * grad_gate, 0.0)
            grad_result = (gate * grad_mixed).astype(BF16)
            grad_results[local, at, :] = grad_result
            grad_act = dot(grad_result, w_out, ((1,), (0,)))
            grad_gate_part = grad_act * up_part * sigmoid * (1.0 + gate_part * (1.0 - sigmoid))
            grad_pre = jnp.concatenate([grad_gate_part, grad_act * silu], 1).astype(BF16)
            grad_acts[local, at, :] = grad_pre
            grad_rows = grad_rows + dot(grad_pre, weights_of(local, 0, in_span), ((1,), (1,)))
        mixed[at, :] = mix.astype(BF16)
        for piece in range(per_chunk):
            place = slice(piece * rows, (piece + 1) * rows)
            blocks[index * per_chunk + piece, :, :width] = grad_rows[place].astype(BF16)
            blocks[index * per_chunk + piece, :, width:] = extra[place].astype(BF16)
        return carry

    lax.fori_loop(0, seq_len // chunk, tokens_block, 0)
    scatter = Scatter(blocks, *scatter_parts)
    scatter.start()
    gates_own[...] = gates[at_own, :]
    owners = grads.shape[0]
    share = width // owners
    count = chunk // share

    def weight_tile(index, carry):
        columns = pl.ds(pl.multiple_of(index * chunk, chunk), chunk)
        turned = normed[:, columns]
        for local in range(experts):
            value = dot(turned, grad_acts[local], ((0,), (0,))).astype(BF16)
            grads[pl.ds(index * count, count), local, :, :in_span] = value.reshape(
                count, share, in_span
            )
            value = dot(grad_results[local, :, columns], acts[local], ((0,), (0,))).astype(BF16)
            grads[pl.ds(index * count, count), local, :, in_span:] = value.reshape(
                count, share, hidden
            )
        return carry

    tiles = width // chunk
    lax.fori_loop(0, tiles // 4, weight_tile, 0)
    scatter.middle()
    lax.fori_loop(tiles // 4, tiles // 2, weight_tile, 0)
    scatter.near_blocks()
    lax.fori_loop(tiles // 2, tiles, weight_tile, 0)
    scatter.end(back)


def wide_call(kernel, name, number, inputs, in_specs, outs, out_specs, scratch):
    return pl.pallas_call(
        kernel,
        name=name,
        out_shape=outs,
        in_specs=in_specs,
        out_specs=out_specs,
        scratch_shapes=scratch,
        cost_estimate=pl.CostEstimate(
            flops=2 * 10**10, bytes_accessed=2 * 10**7, transcendentals=0
        ),
        compiler_params=pltpu.CompilerParams(
            collective_id=number, has_side_effects=True, vmem_limit_bytes=60 * 2**20
        ),
    )(*inputs)


def shards(
    tokens,
    segments,
    top_idx,
    cotangent,
    norm1_gain,
    qkv_weight,
    out_weight,
    norm2_gain,
    router_weight,
    expert_in,
    expert_out,
):
    n_sp = lax.axis_size("sp")
    n_fsdp = lax.axis_size("fsdp")
    sp_index = lax.axis_index("sp")
    rows, width = tokens.shape
    seq_len = rows * n_sp
    weight_rows = qkv_weight.shape[0]
    hidden = expert_out.shape[2]
    q_span, k_span = HQ * HEAD_SIZE, KEY_VALUE_HEADS * HEAD_SIZE
    group = q_span // n_sp
    head = k_span // n_sp
    pack_width = 2 * group + 128
    any_shape = jax.ShapeDtypeStruct
    cosine, sine = rope_tables(seq_len)
    seg_row = segments
    n_experts = expert_in.shape[0]
    in_span = expert_in.shape[2]
    slab = any_shape((seq_len, group), BF16)
    (
        _, _, qkv_own, small_own, gains, normed_one, context, query, key2, value2, sums,
        out_own, normed_own, middle_own, gates_own, mixed, back, grads,
    ) = wide_call(
        forward_kernel,
        "forward",
        1,
        (
            tokens, cotangent, top_idx, qkv_weight, norm1_gain[None, :], norm2_gain[None, :],
            router_weight, out_weight, expert_in, expert_out, cosine, sine, seg_row,
        ),
        [HBM] + [VMEM] * 6 + [HBM] * 3 + [VMEM] * 3,
        (
            any_shape((SP * weight_rows, pack_width), BF16),
            any_shape((SP * weight_rows, width), BF16),
            any_shape((width, 2 * group), BF16),
            any_shape((width, 128), BF16),
            any_shape((8, width), F32),
            any_shape((seq_len, width), BF16),
            slab, slab, slab, slab,
            any_shape((seq_len // BLOCK, 2 * BLOCK, 128), F32),
            any_shape((group, width), BF16),
            any_shape((rows, width), BF16),
            any_shape((rows, width), F32),
            any_shape((rows, 128), F32),
            any_shape((seq_len, width), BF16),
            any_shape((rows, width + 128), F32),
            any_shape((n_fsdp, n_experts, width // n_fsdp, in_span + hidden), BF16),
        ),
        (HBM, HBM) + (VMEM,) * 16,
        [
            pltpu.VMEM((SP, weight_rows, pack_width), BF16),
            pltpu.VMEM((rows, width + 128), BF16),
            pltpu.VMEM((SP, rows, width), BF16),
            pltpu.VMEM((SP, rows, width + 128), BF16),
            pltpu.VMEM((n_fsdp, SP * weight_rows, pack_width), BF16),
            pltpu.VMEM((n_fsdp, 2, SP * weight_rows // 2, width), BF16),
            pltpu.VMEM((n_experts, 4, 4, width // n_fsdp, in_span + hidden), BF16),
            pltpu.VMEM((seq_len, width), BF16),
            pltpu.VMEM((seq_len, 2 * group), F32),
            pltpu.VMEM((seq_len, width), BF16),
            pltpu.VMEM((n_experts, seq_len, hidden), BF16),
            pltpu.VMEM((n_experts, seq_len, in_span), BF16),
            pltpu.VMEM((n_experts, seq_len, width), BF16),
            pltpu.VMEM((SP, rows, width + 128), BF16),
            pltpu.VMEM((2, rows, width), F32),
            pltpu.VMEM((seq_len, 128), F32),
            pltpu.VMEM((seq_len, 1), F32),
        ]
        + scatter_scratch(rows, width + 128)
        + [DMA((8,))] * 6
        + [DMA((n_fsdp,))] * 2
        + [DMA((8,))] * 2
        + [DMA((n_fsdp,))] * 4
        + [DMA((8,))] * 2
        + [DMA((12,))]
        + [DMA((4,))] * 8,
    )
    share = width // n_fsdp
    shares = group // n_fsdp
    half_grads = (4, share // 2, in_span + hidden)
    half_share = (share // 2, in_span + hidden)
    block_out, input_grad, bundle, out_sum, expert_grads = wide_call(
        back_kernel,
        "backward",
        4,
        (
            back, gates_own, normed_own, middle_own, tokens, cotangent, gains, small_own, out_own,
            context, query, key2, value2, sums, cosine, sine, seg_row, qkv_own,
            normed_one, grads.reshape(4, 4, n_experts, share, in_span + hidden),
            mixed.reshape(SP, rows, width),
        ),
        [VMEM] * 21,
        (
            any_shape((rows, width), F32),
            any_shape((rows, width), F32),
            any_shape((SP, weight_rows, pack_width), F32),
            any_shape((shares, width), F32),
            any_shape((n_experts, share, in_span + hidden), F32),
        ),
        (VMEM,) * 5,
        [
            pltpu.VMEM((rows, width), F32),
            pltpu.VMEM((rows, width), F32),
            pltpu.VMEM((rows, width), F32),
            pltpu.VMEM((rows, width), BF16),
            pltpu.VMEM((SP, rows, width), BF16),
            pltpu.VMEM((seq_len, group), BF16),
            pltpu.VMEM((seq_len, 2 * group), BF16),
            pltpu.VMEM((seq_len, group), F32),
            pltpu.VMEM((seq_len, group), F32),
            pltpu.VMEM((SP, rows, width), BF16),
            pltpu.VMEM((width, 128), F32),
            pltpu.VMEM((4, 4, share, pack_width), BF16),
            pltpu.VMEM((n_fsdp, shares, width), BF16),
            pltpu.VMEM((n_fsdp, shares, width), BF16),
            pltpu.VMEM((SP, weight_rows, pack_width), F32),
            pltpu.VMEM((2,) + half_grads, BF16),
            pltpu.VMEM((2,) + half_grads, BF16),
            pltpu.VMEM((2, 4, share // 4, pack_width), BF16),
            pltpu.VMEM((2, 4, share // 4, pack_width), BF16),
            pltpu.VMEM((seq_len, 1), F32),
        ]
        + scatter_scratch(rows, width) * 2
        + quad_scratch(half_grads) * 2
        + quad_scratch(half_share) * 2
        + quad_scratch((4, share // 4, pack_width)) * 2
        + quad_scratch((share // 4, pack_width)) * 2
        + [DMA((8,))] * 2
        + [DMA((n_fsdp,))] * 2
        + [DMA((8,))] * 2
        + [DMA((4,))],
    )
    moves = []
    for f in range(n_fsdp):
        for s in range(n_sp):
            moves.append((f * n_sp + s, (s * group + f * shares) // weight_rows))
    if shares == weight_rows:
        out_grad = lax.ppermute(out_sum, ("fsdp", "sp"), moves)
    else:
        whole = lax.all_gather(out_sum, ("fsdp", "sp"), axis=0, tiled=False)
        whole = whole.reshape(n_fsdp, n_sp, shares, width).transpose(1, 0, 2, 3)
        device = lax.axis_index("fsdp") * n_sp + sp_index
        out_grad = lax.dynamic_slice_in_dim(
            whole.reshape(width, width), device * weight_rows, weight_rows, 0
        )

    qkv_grad = jnp.concatenate(
        [
            bundle[:, :, :group].transpose(1, 0, 2).reshape(weight_rows, q_span),
            bundle[:, :, group : group + head].transpose(1, 0, 2).reshape(weight_rows, k_span),
            bundle[:, :, group + head : 2 * group].transpose(1, 0, 2).reshape(weight_rows, k_span),
        ],
        1,
    )
    smalls = jnp.sum(bundle[:, :, 2 * group :], 0)
    gain_two_grad = smalls[:, 1]
    router_grad = smalls[:, 2 : 2 + E]
    gain_one_grad = jnp.sum(qkv_grad * qkv_weight.astype(F32), 1) / norm1_gain.astype(F32)
    return (
        block_out,
        input_grad,
        gain_one_grad,
        qkv_grad,
        out_grad,
        gain_two_grad,
        router_grad,
        expert_grads[:, :, :in_span],
        expert_grads[:, :, in_span:],
    )


def solution(mesh):
    both = P(("fsdp", "sp"), None)
    flat = P(("fsdp", "sp"))
    expert = P("sp", "fsdp", None)
    return jax.shard_map(
        shards,
        mesh=mesh,
        in_specs=(both, P("fsdp", None), both, both, flat, both, both, flat, both, expert, expert),
        out_specs=(both, both, flat, both, both, flat, both, expert, expert),
        check_vma=False,
    )
```
